128 devices in a mesh: wide: 16 (over y, z), narrow: 8 (over x, core).
Axes of the slice: x: 4, y: 4, z: 4, core: 2. Of those that a mesh axis runs over, the one named last changes fastest.
Arguments:
- hidden_in: bfloat16 [1024, 7168], P(None, ('wide', 'narrow'))
- attn_gain: bfloat16 [7168], P(('wide', 'narrow')), may hold values from 0.099609375 to 1.8984375
- w_qkv: bfloat16 [7168, 8, 1152], P('wide', 'narrow'), may hold values from -0.0625 to 0.0625
- cache_kv: bfloat16 [2, 4096, 8, 2, 128], P(None, 'wide', 'narrow'), as said below
- lengths: int32 [2], replicated, may hold values from 1 to 4096, as said below
- offsets: int32 [2], replicated, may hold values from 0 to 4095
- w_out: bfloat16 [7168, 7168], P('narrow', 'wide'), may hold values from -0.0625 to 0.0625
- mlp_gain: bfloat16 [7168], P(('wide', 'narrow')), may hold values from 0.099609375 to 1.8984375
- w_gate_up: bfloat16 [7168, 2, 20480], P('wide', None, 'narrow'), may hold values from -0.0625 to 0.0625
- w_down: bfloat16 [20480, 7168], P('narrow', 'wide'), may hold values from -0.0390625 to 0.0390625
Outputs:
- hidden_out: bfloat16 [1024, 7168], P(None, ('wide', 'narrow'))
- softmax_sums: float32 [1024, 56], P('wide', 'narrow')
- new_cache: bfloat16 [1024, 8, 2, 128], P('wide', 'narrow')
The draws below stay inside these ranges and needn't reach their ends.
Inputs may be any that keep to these rules, and one draw needn't show every extreme that they name: `lengths`: at least one request has all 4096 cached positions in use. `cache_kv`: positions at or beyond a request's length are never read.
All inputs are finite; a program needn't handle non-finite values.
Results may differ from the reference program's by a relative error of at most 0.01.
Values may be sent and summed in bfloat16 or wider, within the bound.
A program may use at most 192 MiB of HBM per device.

```python
import math
import jax
import jax.numpy as jnp
from jax import lax

D = 7168
FF = 20480
HQ = 56
KVH = 8
HDIM = 128
R = 2
SPAN = 512
LMAX = 4096
GROUP = 7


def draw_hidden_in(key, part):
    noise_key, row_key, col_key = jax.random.split(key, 3)
    shape_rows = (R * SPAN, 1)
    along = jnp.arange(D, dtype=jnp.float32) / (D - 1.0)
    entries = jax.random.normal(noise_key, (R * SPAN, D), jnp.float32)
    row_scale = jnp.exp(jax.random.uniform(row_key, shape_rows, jnp.float32, math.log(0.3), math.log(3.0)))
    rough = jnp.exp(jax.random.uniform(col_key, (1, D), jnp.float32, math.log(0.6), math.log(1.6)))
    ramp = jnp.exp((along - 0.5) * 0.5 * math.log(6.0))[None, :]
    return (entries * row_scale * rough * ramp).astype(jnp.bfloat16)


def draw_cache_kv(key, part):
    entries = jax.random.normal(key, (R, LMAX, KVH, 2, HDIM), jnp.float32)
    return entries.astype(jnp.bfloat16)


def draw_lengths(key, part):
    length_key, pick_key = jax.random.split(key)
    drawn = jax.random.randint(length_key, (R,), 1, LMAX // 4 + 1)
    longest = jax.random.randint(pick_key, (), 0, R)
    return jnp.where(jnp.arange(R) == longest, LMAX, drawn).astype(jnp.int32)


def steps_of(key, shape, cuts, smallest, largest):
    factor_of = 1.0
    for dim, shards_of in cuts:
        heights = jax.random.uniform(jax.random.fold_in(jax.random.fold_in(key, 6), dim), (shards_of,), jnp.float32, smallest / len(cuts), largest / len(cuts))
        factor_of = factor_of * jnp.repeat(jnp.exp(heights), shape[dim] // shards_of).reshape((-1,) + (1,) * (len(shape) - 1 - dim))
    return factor_of


def bell_draw(stream_key, dims, deviation, bound, pieces=(), kind=jnp.bfloat16):
    values = jax.random.normal(stream_key, dims, jnp.float32) * deviation
    if len(pieces) > 0:
        values = steps_of(stream_key, dims, pieces, -0.22, 0.18) * values
    return jnp.clip(values, min=-bound, max=bound).astype(kind)


def setup_inputs(seed: int = 0) -> dict:
    splits = jax.random.split(jax.random.key(seed), 11)
    return {
        "hidden_in": draw_hidden_in(jax.random.fold_in(splits[10], 71), 0),
        "attn_gain": jnp.clip(1.0 + 0.18 * jax.random.normal(splits[1], (D,), jnp.float32), 0.099609375, 1.8984375).astype(jnp.bfloat16),
        "w_qkv": bell_draw(splits[2], (D, KVH, (GROUP + 2) * HDIM), D ** -0.5, 0.0625, ((0, 16), (1, 8))),
        "cache_kv": draw_cache_kv(jax.random.fold_in(splits[10], 71), 0),
        "lengths": draw_lengths(jax.random.fold_in(splits[10], 71), 0),
        "offsets": jax.random.randint(splits[5], (R,), 0, LMAX).astype(jnp.int32),
        "w_out": bell_draw(splits[6], (HQ * HDIM, D), (HQ * HDIM) ** -0.5, 0.0625, ((0, 8), (1, 16))),
        "mlp_gain": jnp.clip(1.0 + 0.18 * jax.random.normal(splits[7], (D,), jnp.float32), 0.099609375, 1.8984375).astype(jnp.bfloat16),
        "w_gate_up": bell_draw(splits[8], (D, 2, FF), D ** -0.5, 0.0625, ((0, 16), (2, 8))),
        "w_down": bell_draw(splits[9], (FF, D), FF ** -0.5, 0.0390625, ((0, 8), (1, 16))),
    }


epsilon = 1e-05
rope_base = 5000000.0
floor_score = -1e+30

def rms_norm(values, gain_row):
    widened = values.astype(jnp.float32)
    inv_scale = lax.rsqrt(lax.optimization_barrier(jnp.mean(widened * widened, axis=1, keepdims=True)) + epsilon)
    return (widened * inv_scale * gain_row.astype(jnp.float32)[None, :]).astype(jnp.bfloat16)

def token_angles(lengths, offsets, first_token, row_count, dim_size):
    token_ids = first_token + jnp.arange(row_count, dtype=jnp.int32)
    request_ids = token_ids % R
    start_pos = offsets + lengths
    matches = request_ids[:, None] == jnp.arange(start_pos.shape[0], dtype=jnp.int32)[None, :]
    chosen = lax.optimization_barrier(jnp.sum(jnp.where(matches, start_pos[None, :], 0), axis=1))
    position = (chosen + token_ids // R).astype(jnp.float32)
    inverse = rope_base ** (-(jnp.arange(dim_size // 2, dtype=jnp.float32) * 2.0) / dim_size)
    return position[:, None] * inverse[None, :]

def rotate(values, angles):
    half_dim = values.shape[-1] // 2
    first_half = values[..., :half_dim]
    second_half = values[..., half_dim:]
    cosine = jnp.cos(angles)[:, None, :]
    sine_part = jnp.sin(angles)[:, None, :]
    return jnp.concatenate([first_half * cosine - second_half * sine_part, second_half * cosine + first_half * sine_part], axis=-1)

def reference(hidden_in, attn_gain, w_qkv, cache_kv, lengths, offsets, w_out, mlp_gain, w_gate_up, w_down):
    all_tokens = hidden_in.shape[0]
    score_scale = HDIM ** (-0.5)
    normed = rms_norm(hidden_in, attn_gain)
    projected = jnp.dot(normed, w_qkv.reshape(D, -1), preferred_element_type=jnp.float32)
    projected = projected.reshape(all_tokens, KVH, GROUP + 2, HDIM)
    angles = token_angles(lengths, offsets, 0, all_tokens, HDIM)
    queries = rotate(projected[:, :, :GROUP].reshape(all_tokens, KVH * GROUP, HDIM), angles)
    queries = queries.astype(jnp.bfloat16).reshape(all_tokens, KVH, GROUP, HDIM)
    new_keys = rotate(projected[:, :, GROUP], angles).astype(jnp.bfloat16)
    new_values = projected[:, :, GROUP + 1].astype(jnp.bfloat16)
    new_cache = jnp.stack([new_keys, new_values], axis=2)
    outputs = []
    sums_all = []
    for request in range(R):
        furthest = lengths[request]

        def one_head(items):
            query_block, key_new, value_new, key_old, value_old = items
            key_all = jnp.concatenate([key_old, key_new], axis=0)
            value_all = jnp.concatenate([value_old, value_new], axis=0)
            scores = jnp.dot(query_block.reshape(SPAN * GROUP, HDIM), key_all.T, preferred_element_type=jnp.float32)
            scores = scores.reshape(SPAN, GROUP, LMAX + SPAN) * score_scale
            position = jnp.arange(LMAX + SPAN, dtype=jnp.int32)
            row_ids = jnp.arange(SPAN, dtype=jnp.int32)
            allowed = jnp.where(position[None, :] < LMAX, position[None, :] < furthest, position[None, :] - LMAX <= row_ids[:, None])
            scores = jnp.where(allowed[:, None, :], scores, floor_score)
            peak = lax.optimization_barrier(jnp.max(scores, axis=2, keepdims=True))
            weights = jnp.where(allowed[:, None, :], jnp.exp(scores - peak), 0.0)
            weight_sum = lax.optimization_barrier(jnp.sum(weights, axis=2))
            gathered = jnp.dot(weights.astype(jnp.bfloat16).reshape(SPAN * GROUP, LMAX + SPAN), value_all, preferred_element_type=jnp.float32)
            gathered = gathered.reshape(SPAN, GROUP, HDIM)
            attended_head = (gathered / weight_sum[..., None]).astype(jnp.bfloat16)
            return (attended_head, peak[..., 0] + jnp.log(weight_sum))
        items = (queries[request::R].transpose(1, 0, 2, 3), new_keys[request::R].transpose(1, 0, 2), new_values[request::R].transpose(1, 0, 2), cache_kv[request, :, :, 0].transpose(1, 0, 2), cache_kv[request, :, :, 1].transpose(1, 0, 2))
        heads_out, head_sums = lax.map(one_head, items)
        outputs.append(heads_out.transpose(1, 0, 2, 3).reshape(SPAN, HQ * HDIM))
        sums_all.append(head_sums.transpose(1, 0, 2).reshape(SPAN, HQ))
    attended = jnp.stack(outputs, axis=1).reshape(all_tokens, HQ * HDIM)
    softmax_sums = jnp.stack(sums_all, axis=1).reshape(all_tokens, HQ)
    residual = (hidden_in.astype(jnp.float32) + jnp.dot(attended, w_out, preferred_element_type=jnp.float32)).astype(jnp.bfloat16)
    normed_mlp = rms_norm(residual, mlp_gain)
    both = jnp.dot(normed_mlp, w_gate_up.reshape(D, 2 * FF), preferred_element_type=jnp.float32).reshape(all_tokens, 2, FF)
    hidden = (jax.nn.silu(both[:, 0]) * both[:, 1]).astype(jnp.bfloat16)
    hidden_out = (residual.astype(jnp.float32) + jnp.dot(hidden, w_down, preferred_element_type=jnp.float32)).astype(jnp.bfloat16)
    return (hidden_out, softmax_sums, new_cache)
```

```python
import functools

import jax
import jax.numpy as jnp
from jax import lax
from jax.experimental import pallas as pl
from jax.experimental.pallas import tpu as pltpu
from jax.sharding import PartitionSpec as P

D = 7168
HDIM = 128
R = 2
GROUP = 7
SIDE = 4

epsilon = 1e-05
rope_base = 5000000.0
floor_score = -1e30

MESH = pl.DeviceIdType.MESH
BF = jnp.bfloat16
F32 = jnp.float32
ANY = pl.BlockSpec(memory_space=pl.ANY)
VM = pl.BlockSpec(memory_space=pltpu.VMEM)
SM = pl.BlockSpec(memory_space=pltpu.SMEM)
VMEM_LIMIT = 60 * 1024 * 1024


def wide_place():
    w = lax.axis_index("wide")
    return lax.div(w, SIDE), lax.rem(w, SIDE)


def turn(pos, by):
    return lax.rem(pos + by, SIDE)


def ring_devices(axis, by):
    if axis == "x":
        n = lax.axis_index("narrow")
        return {"narrow": turn(lax.div(n, 2), by) * 2 + lax.rem(n, 2)}
    y, z = wide_place()
    if axis == "y":
        return {"wide": turn(y, by) * SIDE + z}
    return {"wide": y * SIDE + turn(z, by)}


def partner_device():
    n = lax.axis_index("narrow")
    return {"narrow": lax.div(n, 2) * 2 + 1 - lax.rem(n, 2)}


def greet(devices):
    barrier = pltpu.get_barrier_semaphore()
    for device in devices:
        pl.semaphore_signal(barrier, inc=1, device_id=device, device_id_type=MESH)
    pl.semaphore_wait(barrier, len(devices))


class Copies:
    def __init__(self, send_sem, recv_sem):
        self.send_sem, self.recv_sem, self.used, self.made = send_sem, recv_sem, 0, []

    def slot(self):
        self.used += 1
        return self.used - 1

    def start(self, slot, src, dst, device):
        copy = pltpu.make_async_remote_copy(
            src_ref=src,
            dst_ref=dst,
            send_sem=self.send_sem.at[slot],
            recv_sem=self.recv_sem.at[slot],
            device_id=device,
            device_id_type=MESH,
        )
        copy.start()
        self.made.append(copy)

    def arrived(self, slot, dst):
        pltpu.make_async_copy(dst, dst, self.recv_sem.at[slot]).wait()

    def sent(self):
        for copy in self.made:
            copy.wait_send()


def interleave(*parts):
    live = list(parts)
    while live:
        for part in list(live):
            try:
                next(part)
            except StopIteration:
                live.remove(part)


def gather_wide_steps(x_ref, out_ref, local_sem, copies):
    y, z = wide_place()
    depth = x_ref.shape[1] // 2
    lower, upper = pl.ds(0, depth), pl.ds(depth, depth)

    def place(half, first, second):
        if half == 0:
            return out_ref.at[first, second, 0]
        return out_ref.at[second, first, 1]

    names = (("y", "z"), ("z", "y"))
    spots = ((y, z), (z, y))
    own = pltpu.make_async_copy(x_ref, out_ref.at[y, z], local_sem)
    own.start()
    hop1 = [[copies.slot() for _ in range(4)] for _ in range(2)]
    hop2 = [[[copies.slot() for _ in range(4)] for _ in range(4)] for _ in range(2)]

    def send2(half, block, src):
        first = turn(spots[half][0], block)
        target = place(half, first, spots[half][1])
        for way, by in ((0, 1), (1, 3)):
            copies.start(hop2[half][block][way], src, target, ring_devices(names[half][1], by))

    def relay2(half, block):
        first = turn(spots[half][0], block)
        for way, by, part in ((0, 1, lower), (1, 3, upper)):
            came = place(half, first, turn(spots[half][1], 4 - by))
            copies.arrived(hop2[half][block][way], came)
            copies.start(
                hop2[half][block][2 + way], came.at[part], came.at[part], ring_devices(names[half][1], by)
            )

    for half in range(2):
        target = place(half, *spots[half])
        for way, by in ((0, 1), (1, 3)):
            copies.start(hop1[half][way], x_ref.at[half], target, ring_devices(names[half][0], by))
        send2(half, 0, x_ref.at[half])
    yield
    for half in range(2):
        for way, by, part in ((0, 1, lower), (1, 3, upper)):
            came = place(half, turn(spots[half][0], 4 - by), spots[half][1])
            copies.arrived(hop1[half][way], came)
            copies.start(hop1[half][2 + way], came.at[part], came.at[part], ring_devices(names[half][0], by))
            send2(half, 4 - by, came)
        yield
    for half in range(2):
        relay2(half, 0)
        yield
    for half in range(2):
        far = place(half, turn(spots[half][0], 2), spots[half][1])
        copies.arrived(hop1[half][2], far.at[lower])
        copies.arrived(hop1[half][3], far.at[upper])
        send2(half, 2, far)
        yield
    for block in (3, 1, 2):
        for half in range(2):
            relay2(half, block)
            yield
    for half in range(2):
        for block in (0, 3, 1, 2):
            far = place(half, turn(spots[half][0], block), turn(spots[half][1], 2))
            copies.arrived(hop2[half][block][2], far.at[lower])
            copies.arrived(hop2[half][block][3], far.at[upper])
    own.wait()


WIDE_COPIES = 40


def wide_neighbours():
    return [ring_devices(axis, by) for axis in ("y", "z") for by in (1, 3)]


def gather_wide_kernel(x_ref, out_ref, local_sem, send_sem, recv_sem):
    copies = Copies(send_sem, recv_sem)
    greet(wide_neighbours())
    interleave(gather_wide_steps(x_ref, out_ref, local_sem, copies))
    copies.sent()


def gather_wide(x, collective_id):
    return pl.pallas_call(
        gather_wide_kernel,
        out_shape=jax.ShapeDtypeStruct((SIDE, SIDE) + x.shape, x.dtype),
        in_specs=[VM],
        out_specs=ANY,
        scratch_shapes=[
            pltpu.SemaphoreType.DMA,
            pltpu.SemaphoreType.DMA((WIDE_COPIES,)),
            pltpu.SemaphoreType.DMA((WIDE_COPIES,)),
        ],
        compiler_params=pltpu.CompilerParams(collective_id=collective_id, has_side_effects=True),
        name=f"gather_wide_{collective_id}",
    )(x)


def gather_narrow_steps(x_ref, out_ref, local_sem, copies):
    n = lax.axis_index("narrow")
    x, core = lax.div(n, 2), lax.rem(n, 2)
    depth = x_ref.shape[0] // 2
    lower, upper = pl.ds(0, depth), pl.ds(depth, depth)
    own = pltpu.make_async_copy(x_ref, out_ref.at[n], local_sem)
    own.start()
    slots = [copies.slot() for _ in range(8)]
    for way, by in ((0, 1), (1, 3)):
        copies.start(slots[way], x_ref, out_ref.at[n], ring_devices("x", by))
    copies.start(slots[4], x_ref, out_ref.at[n], partner_device())
    yield
    for way, by, part in ((0, 1, lower), (1, 3, upper)):
        came = out_ref.at[turn(x, 4 - by) * 2 + core]
        copies.arrived(slots[way], came)
        copies.start(slots[2 + way], came.at[part], came.at[part], ring_devices("x", by))
        copies.start(slots[5 + way], came, came, partner_device())
    yield
    far = out_ref.at[turn(x, 2) * 2 + core]
    copies.arrived(slots[2], far.at[lower])
    copies.arrived(slots[3], far.at[upper])
    copies.start(slots[7], far, far, partner_device())
    yield
    for slot, by in ((4, 0), (5, 3), (6, 1), (7, 2)):
        copies.arrived(slots[slot], out_ref.at[turn(x, by) * 2 + 1 - core])
    own.wait()


NARROW_COPIES = 8


def narrow_neighbours():
    return [ring_devices("x", 1), ring_devices("x", 3), partner_device()]


def gather_narrow_kernel(x_ref, out_ref, local_sem, send_sem, recv_sem):
    copies = Copies(send_sem, recv_sem)
    greet(narrow_neighbours())
    interleave(gather_narrow_steps(x_ref, out_ref, local_sem, copies))
    copies.sent()


def gather_narrow(x, collective_id):
    return pl.pallas_call(
        gather_narrow_kernel,
        out_shape=jax.ShapeDtypeStruct((8,) + x.shape, x.dtype),
        in_specs=[VM],
        out_specs=VM,
        scratch_shapes=[
            pltpu.SemaphoreType.DMA,
            pltpu.SemaphoreType.DMA((NARROW_COPIES,)),
            pltpu.SemaphoreType.DMA((NARROW_COPIES,)),
        ],
        compiler_params=pltpu.CompilerParams(collective_id=collective_id, has_side_effects=True),
        name=f"gather_narrow_{collective_id}",
    )(x)


def gather_both_kernel(x_ref, cache_ref, xo_ref, cacheo_ref, local_sem, send_n, recv_n, send_w, recv_w):
    near, far = Copies(send_n, recv_n), Copies(send_w, recv_w)
    greet(narrow_neighbours() + wide_neighbours())
    interleave(
        gather_narrow_steps(x_ref, xo_ref, local_sem.at[0], near),
        gather_wide_steps(cache_ref, cacheo_ref, local_sem.at[1], far),
    )
    near.sent()
    far.sent()


def gather_both(x, cache, collective_id):
    return pl.pallas_call(
        gather_both_kernel,
        out_shape=(
            jax.ShapeDtypeStruct((8,) + x.shape, x.dtype),
            jax.ShapeDtypeStruct((SIDE, SIDE) + cache.shape, cache.dtype),
        ),
        in_specs=[VM, VM],
        out_specs=(VM, ANY),
        scratch_shapes=[
            pltpu.SemaphoreType.DMA((2,)),
            pltpu.SemaphoreType.DMA((NARROW_COPIES,)),
            pltpu.SemaphoreType.DMA((NARROW_COPIES,)),
            pltpu.SemaphoreType.DMA((WIDE_COPIES,)),
            pltpu.SemaphoreType.DMA((WIDE_COPIES,)),
        ],
        compiler_params=pltpu.CompilerParams(collective_id=collective_id, has_side_effects=True),
        name="gather_both",
    )(x, cache)


def sum_narrow_kernel(p_ref, out_ref, mate, total, relay, direct, joined, send_sem, recv_sem):
    copies = Copies(send_sem, recv_sem)
    n = lax.axis_index("narrow")
    x, core = lax.div(n, 2), lax.rem(n, 2)
    width = p_ref.shape[3] // 2
    lower, upper = pl.ds(0, width), pl.ds(width, width)
    right, left = ring_devices("x", 1), ring_devices("x", 3)
    greet(narrow_neighbours())
    order = (2, 1, 3, 0)
    mates = {by: copies.slot() for by in order}
    slots = [copies.slot() for _ in range(6)]
    for by in order:
        copies.start(mates[by], p_ref.at[turn(x, by), 1 - core], mate.at[by], partner_device())

    def pair(by):
        copies.arrived(mates[by], mate.at[by])
        return p_ref[turn(x, by), core].astype(F32) + mate[by].astype(F32)

    total[2] = pair(2).astype(BF)
    copies.start(slots[0], total.at[2, :, lower], relay.at[0], right)
    copies.start(slots[1], total.at[2, :, upper], relay.at[1], left)
    total[1] = pair(1).astype(BF)
    copies.start(slots[2], total.at[1, :, upper], direct.at[0], right)
    total[3] = pair(3).astype(BF)
    copies.start(slots[3], total.at[3, :, lower], direct.at[1], left)
    copies.arrived(slots[0], relay.at[0])
    total[1, :, lower] = (total[1, :, lower].astype(F32) + relay[0].astype(F32)).astype(BF)
    copies.start(slots[4], total.at[1, :, lower], joined.at[0], right)
    copies.arrived(slots[1], relay.at[1])
    total[3, :, upper] = (total[3, :, upper].astype(F32) + relay[1].astype(F32)).astype(BF)
    copies.start(slots[5], total.at[3, :, upper], joined.at[1], left)
    out_ref[...] = pair(0)
    copies.arrived(slots[2], direct.at[0])
    out_ref[:, upper] += direct[0].astype(F32)
    copies.arrived(slots[3], direct.at[1])
    out_ref[:, lower] += direct[1].astype(F32)
    copies.arrived(slots[4], joined.at[0])
    out_ref[:, lower] += joined[0].astype(F32)
    copies.arrived(slots[5], joined.at[1])
    out_ref[:, upper] += joined[1].astype(F32)
    copies.sent()


def sum_narrow(p, collective_id):
    rows, cols = p.shape[2:]
    piece = pltpu.VMEM((2, rows, cols // 2), BF)
    return pl.pallas_call(
        sum_narrow_kernel,
        out_shape=jax.ShapeDtypeStruct((rows, cols), F32),
        in_specs=[VM],
        out_specs=VM,
        scratch_shapes=[
            pltpu.VMEM((4, rows, cols), BF),
            pltpu.VMEM((4, rows, cols), BF),
            piece,
            piece,
            piece,
            pltpu.SemaphoreType.DMA((10,)),
            pltpu.SemaphoreType.DMA((10,)),
        ],
        compiler_params=pltpu.CompilerParams(
            collective_id=collective_id, has_side_effects=True, vmem_limit_bytes=VMEM_LIMIT
        ),
        name=f"sum_narrow_{collective_id}",
    )(p)


def matmul_sum_kernel(
    x_ref, w_ref, sq_ref, out_ref, sqo_ref, part, mid, got1, got2, sq1, sqm, sq2,
    send1, recv1, send2, recv2, sq_send, sq_recv,
):
    pieces, width = part.shape[0], part.shape[-1]
    rows = x_ref.shape[3]
    y, z = wide_place()
    names = (("y", "z"), ("z", "y"))
    spots = ((y, z), (z, y))
    greet([ring_devices(axis, by) for axis in ("y", "z") for by in (1, 2, 3)])
    squares = Copies(sq_send, sq_recv)
    for by in (1, 2, 3):
        squares.start(by - 1, sq_ref.at[turn(y, by)], sq1.at[by - 1], ring_devices("y", by))

    def product(half, chunk, piece):
        block = x_ref[chunk, :, 0] if half == 0 else x_ref[:, chunk, 1]
        block = block.reshape(SIDE * rows, block.shape[-1])
        columns = pl.ds(pl.multiple_of(piece * width, 128), width)
        got = jnp.dot(block, w_ref[:, columns], preferred_element_type=F32)
        return got.reshape(SIDE, rows, width)

    def copy1(piece, half, kind, way, src):
        return pltpu.make_async_remote_copy(
            src_ref=src,
            dst_ref=got1.at[piece, half, kind, way],
            send_sem=send1.at[piece, half, kind, way],
            recv_sem=recv1.at[piece, half, kind, way],
            device_id=ring_devices(names[half][0], 1 if way == 0 else 3),
            device_id_type=MESH,
        )

    def copy2(piece, half, kind, way, src):
        return pltpu.make_async_remote_copy(
            src_ref=src,
            dst_ref=got2.at[piece, half, kind, way],
            send_sem=send2.at[piece, half, kind, way],
            recv_sem=recv2.at[piece, half, kind, way],
            device_id=ring_devices(names[half][1], 1 if way == 0 else 3),
            device_id_type=MESH,
        )

    def await1(piece, half, kind, way):
        ref = got1.at[piece, half, kind, way]
        pltpu.make_async_copy(ref, ref, recv1.at[piece, half, kind, way]).wait()
        return got1[piece, half, kind, way].astype(F32)

    def await2(piece, half, kind, way):
        ref = got2.at[piece, half, kind, way]
        pltpu.make_async_copy(ref, ref, recv2.at[piece, half, kind, way]).wait()
        return got2[piece, half, kind, way].astype(F32)

    lower, upper = pl.ds(0, 2), pl.ds(2, 2)
    low, high = pl.ds(0, rows // 2), pl.ds(rows // 2, rows // 2)

    def first(piece):
        for half in range(2):
            far = turn(spots[half][0], 2)
            part[piece, half, far] = product(half, far, piece).astype(BF)
            copy1(piece, half, 0, 0, part.at[piece, half, far, lower]).start()
            copy1(piece, half, 0, 1, part.at[piece, half, far, upper]).start()
        for half in range(2):
            right, left = turn(spots[half][0], 1), turn(spots[half][0], 3)
            part[piece, half, right] = product(half, right, piece).astype(BF)
            copy1(piece, half, 1, 0, part.at[piece, half, right, upper]).start()
            part[piece, half, left] = product(half, left, piece).astype(BF)
            copy1(piece, half, 1, 1, part.at[piece, half, left, lower]).start()

    def second(piece):
        for half in range(2):
            right, left = turn(spots[half][0], 1), turn(spots[half][0], 3)
            got = await1(piece, half, 0, 0)
            part[piece, half, right, lower] = (part[piece, half, right, lower].astype(F32) + got).astype(BF)
            copy1(piece, half, 2, 0, part.at[piece, half, right, lower]).start()
            got = await1(piece, half, 0, 1)
            part[piece, half, left, upper] = (part[piece, half, left, upper].astype(F32) + got).astype(BF)
            copy1(piece, half, 2, 1, part.at[piece, half, left, upper]).start()

    def third(piece):
        for half in range(2):
            own = product(half, spots[half][0], piece)
            mid[piece, half, lower] = (
                own[:2] + await1(piece, half, 1, 1) + await1(piece, half, 2, 0)
            ).astype(BF)
            mid[piece, half, upper] = (
                own[2:] + await1(piece, half, 1, 0) + await1(piece, half, 2, 1)
            ).astype(BF)
            far, right, left = (turn(spots[half][1], by) for by in (2, 1, 3))
            copy2(piece, half, 0, 0, mid.at[piece, half, far, low]).start()
            copy2(piece, half, 0, 1, mid.at[piece, half, far, high]).start()
            copy2(piece, half, 1, 0, mid.at[piece, half, right, high]).start()
            copy2(piece, half, 1, 1, mid.at[piece, half, left, low]).start()

    def fourth(piece):
        for half in range(2):
            right, left = turn(spots[half][1], 1), turn(spots[half][1], 3)
            got = await2(piece, half, 0, 0)
            mid[piece, half, right, low] = (mid[piece, half, right, low].astype(F32) + got).astype(BF)
            copy2(piece, half, 2, 0, mid.at[piece, half, right, low]).start()
            got = await2(piece, half, 0, 1)
            mid[piece, half, left, high] = (mid[piece, half, left, high].astype(F32) + got).astype(BF)
            copy2(piece, half, 2, 1, mid.at[piece, half, left, high]).start()

    def fifth(piece):
        columns = pl.ds(pl.multiple_of(piece * width, 128), width)
        for half in range(2):
            own = spots[half][1]
            out_ref[half, low, columns] = (
                mid[piece, half, own, low].astype(F32) + await2(piece, half, 1, 1) + await2(piece, half, 2, 0)
            )
            out_ref[half, high, columns] = (
                mid[piece, half, own, high].astype(F32) + await2(piece, half, 1, 0) + await2(piece, half, 2, 1)
            )

    stages = (first, second, third, fourth, fifth)

    def step(t, carry):
        for lag, stage in enumerate(stages):
            piece = t - lag

            @pl.when((piece >= 0) & (piece < pieces))
            def _():
                stage(jnp.clip(piece, 0, pieces - 1))

        return carry

    lax.fori_loop(0, pieces + len(stages) - 1, step, 0)

    for by in (1, 2, 3):
        squares.arrived(by - 1, sq1.at[by - 1])
    sqm[...] = sq_ref[y] + sq1[0] + sq1[1] + sq1[2]
    for by in (1, 2, 3):
        squares.start(2 + by, sqm.at[turn(z, by)], sq2.at[by - 1], ring_devices("z", by))
    for by in (1, 2, 3):
        squares.arrived(2 + by, sq2.at[by - 1])
    sqo_ref[...] = sqm[z] + sq2[0] + sq2[1] + sq2[2]
    squares.sent()

    def drain(piece, carry):
        for half in range(2):
            for kind in range(3):
                for way in range(2):
                    copy1(piece, half, kind, way, part.at[piece, half, 0, lower]).wait_send()
                    copy2(piece, half, kind, way, mid.at[piece, half, 0, low]).wait_send()
        return carry

    lax.fori_loop(0, pieces, drain, 0)


def matmul_sum(x, w, sq, pieces, collective_id):
    tokens, depth = x.shape
    cols = w.shape[1]
    width = cols // pieces
    rows = tokens // (2 * SIDE * SIDE)
    blocks = jnp.pad(sq.reshape(SIDE, SIDE, 1, 2 * rows), ((0, 0), (0, 0), (0, 0), (0, 128 - 2 * rows)))
    blocks = jnp.broadcast_to(blocks, (SIDE, SIDE, 8, 128))
    out, sq_out = pl.pallas_call(
        matmul_sum_kernel,
        out_shape=(
            jax.ShapeDtypeStruct((2, rows, cols), F32),
            jax.ShapeDtypeStruct((8, 128), F32),
        ),
        in_specs=[VM, VM, VM],
        out_specs=(VM, VM),
        scratch_shapes=[
            pltpu.VMEM((pieces, 2, SIDE, SIDE, rows, width), BF),
            pltpu.VMEM((pieces, 2, SIDE, rows, width), BF),
            pltpu.VMEM((pieces, 2, 3, 2, 2, rows, width), BF),
            pltpu.VMEM((pieces, 2, 3, 2, rows // 2, width), BF),
            pltpu.VMEM((3, SIDE, 8, 128), F32),
            pltpu.VMEM((SIDE, 8, 128), F32),
            pltpu.VMEM((3, 8, 128), F32),
            pltpu.SemaphoreType.DMA((pieces, 2, 3, 2)),
            pltpu.SemaphoreType.DMA((pieces, 2, 3, 2)),
            pltpu.SemaphoreType.DMA((pieces, 2, 3, 2)),
            pltpu.SemaphoreType.DMA((pieces, 2, 3, 2)),
            pltpu.SemaphoreType.DMA((6,)),
            pltpu.SemaphoreType.DMA((6,)),
        ],
        compiler_params=pltpu.CompilerParams(
            collective_id=collective_id, has_side_effects=True, vmem_limit_bytes=VMEM_LIMIT
        ),
        name=f"matmul_sum_{collective_id}",
    )(x.reshape(SIDE, SIDE, 2, rows, depth), w, blocks)
    return out.reshape(2 * rows, cols), sq_out[0, : 2 * rows]


def attend_kernel(lengths_ref, spot_ref, q_ref, cache_ref, span_ref, out_ref, sums_ref):
    scale = HDIM ** (-0.5)
    rows = q_ref.shape[1]
    per = span_ref.shape[2]
    block = cache_ref.shape[2] * 2

    for request in range(R):
        q = q_ref[request]

        def absorb(running, keys, values, allowed):
            peak, weight_sum, gathered = running
            scores = lax.dot_general(q, keys, (((1,), (1,)), ((), ())), preferred_element_type=F32) * scale
            scores = jnp.where(allowed(scores.shape), scores, floor_score)
            new_peak = jnp.maximum(peak, jnp.max(scores, axis=1, keepdims=True))
            weights = jnp.exp(scores - new_peak)
            factor = jnp.exp(peak - new_peak)
            weight_sum = weight_sum * factor + jnp.sum(weights, axis=1, keepdims=True)
            gathered = gathered * factor + jnp.dot(weights.astype(BF), values, preferred_element_type=F32)
            return new_peak, weight_sum, gathered

        span = span_ref[:, request].reshape(SIDE * SIDE * per, 2 * HDIM)

        def own_keys(shape):
            key = lax.broadcasted_iota(jnp.int32, shape, 1)
            row = lax.broadcasted_iota(jnp.int32, shape, 0)
            return key <= spot_ref[0] * per + lax.rem(row, per)

        running = absorb(
            (
                jnp.full((rows, 1), floor_score, F32),
                jnp.zeros((rows, 1), F32),
                jnp.zeros((rows, HDIM), F32),
            ),
            span[:, :HDIM],
            span[:, HDIM:],
            own_keys,
        )
        length = lengths_ref[request]

        def cached(index, running):
            pair = cache_ref[pl.ds(index * 2, 2), request].reshape(block, 2 * HDIM)

            def in_use(shape):
                return index * block + lax.broadcasted_iota(jnp.int32, shape, 1) < length

            keep = index * block + lax.broadcasted_iota(jnp.int32, (block, HDIM), 0) < length
            values = jnp.where(keep, pair[:, HDIM:], jnp.zeros((), BF))
            return absorb(running, pair[:, :HDIM], values, in_use)

        peak, weight_sum, gathered = lax.fori_loop(0, lax.div(length + block - 1, block), cached, running)
        out_ref[request] = (gathered / weight_sum).astype(BF)
        sums_ref[request] = jnp.broadcast_to(peak + jnp.log(weight_sum), (rows, HDIM))


def attend(lengths, spot, queries, cache, span):
    return pl.pallas_call(
        attend_kernel,
        out_shape=(
            jax.ShapeDtypeStruct(queries.shape, BF),
            jax.ShapeDtypeStruct(queries.shape, F32),
        ),
        in_specs=[SM, SM, VM, VM, VM],
        out_specs=(VM, VM),
        compiler_params=pltpu.CompilerParams(vmem_limit_bytes=VMEM_LIMIT),
        name="attend",
    )(lengths, spot, queries, cache, span)


def token_angles(lengths, offsets, first_token, row_count, dim_size):
    token_ids = first_token + jnp.arange(row_count, dtype=jnp.int32)
    request_ids = token_ids % R
    start_pos = offsets + lengths
    matches = request_ids[:, None] == jnp.arange(start_pos.shape[0], dtype=jnp.int32)[None, :]
    chosen = jnp.sum(jnp.where(matches, start_pos[None, :], 0), axis=1)
    position = (chosen + token_ids // R).astype(jnp.float32)
    inverse = rope_base ** (-(jnp.arange(dim_size // 2, dtype=jnp.float32) * 2.0) / dim_size)
    return position[:, None] * inverse[None, :]


def rotate(values, angles):
    half_dim = values.shape[-1] // 2
    first_half = values[..., :half_dim]
    second_half = values[..., half_dim:]
    cosine = jnp.cos(angles)[:, None, :]
    sine_part = jnp.sin(angles)[:, None, :]
    return jnp.concatenate(
        [
            first_half * cosine - second_half * sine_part,
            second_half * cosine + first_half * sine_part,
        ],
        axis=-1,
    )


def to_send(flipped, gain):
    widened = flipped.astype(F32)
    squares = jnp.sum(widened * widened, axis=0, keepdims=True)
    high = lax.reduce_precision(squares, 8, 7)
    rest = squares - high
    middle = lax.reduce_precision(rest, 8, 7)
    low = rest - middle
    scaled = widened * gain.astype(F32)[:, None]
    pad = jnp.zeros((5, flipped.shape[1]), F32)
    return jnp.concatenate([scaled, high, middle, low, pad], axis=0).astype(BF)


def unpack(gathered, rows):
    scaled = gathered[:, :rows].reshape(8 * rows, -1).T
    squares = jnp.sum(gathered[:, rows : rows + 3].astype(F32), axis=(0, 1))
    return scaled, squares


def rescale(sums, squares):
    inv_scale = lax.rsqrt(squares / D + epsilon)[:, None]
    return jnp.where(inv_scale > 0, sums * inv_scale, 0.0)


def local(
    hidden_in, attn_gain, w_qkv, cache_kv, lengths, offsets, w_out, mlp_gain, w_gate_up, w_down
):
    wide_index = lax.axis_index("wide")
    all_tokens, features = hidden_in.shape
    per_device = all_tokens // lax.axis_size("wide")
    first_token = wide_index * per_device
    flipped = hidden_in.T
    positions = cache_kv.shape[1]
    cache = cache_kv.reshape(R, positions, 2 * HDIM)
    gathered, cache_all = gather_both(to_send(flipped, attn_gain), cache, 1)
    scaled, squares = unpack(gathered, features)
    projected, squares = matmul_sum(scaled, w_qkv.reshape(w_qkv.shape[0], -1), squares, 3, 2)
    projected = rescale(projected, squares).reshape(per_device, GROUP + 2, HDIM)
    angles = token_angles(lengths, offsets, first_token, per_device, HDIM)
    rotated = rotate(projected[:, : GROUP + 1], angles).astype(BF)
    new_keys, new_values = rotated[:, GROUP], projected[:, GROUP + 1].astype(BF)
    new_cache = jnp.stack([new_keys, new_values], axis=1)[:, None]
    per_request = per_device // R
    span = jnp.concatenate([new_keys, new_values], axis=1).reshape(per_request, R, 2 * HDIM)
    span_all = gather_wide(span.transpose(1, 0, 2), 3)
    queries = rotated[:, :GROUP].reshape(per_request, R, GROUP, HDIM).transpose(1, 2, 0, 3)
    attended, sums = attend(
        lengths,
        wide_index.reshape(1),
        queries.reshape(R, GROUP * per_request, HDIM),
        cache_all.reshape(SIDE * SIDE, R, positions, 2 * HDIM),
        span_all.reshape(SIDE * SIDE, R, per_request, 2 * HDIM),
    )
    attended = attended.reshape(R, GROUP, per_request, HDIM).transpose(2, 0, 1, 3).reshape(2, -1, GROUP * HDIM)
    softmax_sums = sums[:, :, 0].reshape(R, GROUP, per_request).transpose(2, 0, 1).reshape(per_device, GROUP)
    attended_all = gather_wide(attended, 4).reshape(all_tokens, -1)
    out_terms = lax.dot_general(
        w_out, attended_all, (((0,), (1,)), ((), ())), preferred_element_type=F32
    ).astype(BF)
    summed = sum_narrow(out_terms.reshape(4, 2, features, all_tokens), 5)
    residual = (flipped.astype(F32) + summed).astype(BF)
    scaled, squares = unpack(gather_narrow(to_send(residual, mlp_gain), 6), features)
    units = w_gate_up.shape[2]
    both, squares = matmul_sum(scaled, w_gate_up.reshape(w_gate_up.shape[0], -1), squares, 4, 7)
    both = rescale(both, squares)
    hidden = (jax.nn.silu(both[:, :units]) * both[:, units:]).astype(BF)
    hidden_all = gather_wide(hidden.reshape(2, -1, units), 8).reshape(all_tokens, units)
    down_terms = lax.dot_general(
        w_down, hidden_all, (((0,), (1,)), ((), ())), preferred_element_type=F32
    ).astype(BF)
    summed = sum_narrow(down_terms.reshape(4, 2, features, all_tokens), 9)
    hidden_out = (residual.astype(F32) + summed).astype(BF).T
    return (hidden_out, softmax_sums, new_cache)


def solution(mesh):
    return jax.shard_map(
        local,
        mesh=mesh,
        in_specs=(
            P(None, ("wide", "narrow")),
            P(("wide", "narrow")),
            P("wide", "narrow", None),
            P(None, "wide", "narrow", None, None),
            P(),
            P(),
            P("narrow", "wide"),
            P(("wide", "narrow")),
            P("wide", None, "narrow"),
            P("narrow", "wide"),
        ),
        out_specs=(
            P(None, ("wide", "narrow")),
            P("wide", "narrow"),
            P("wide", "narrow", None, None),
        ),
        check_vma=False,
    )
```

```python
import functools

import jax
import jax.numpy as jnp
from jax import lax
from jax.experimental import pallas as pl
from jax.experimental.pallas import tpu as pltpu
from jax.sharding import PartitionSpec as P

D = 7168
HDIM = 128
R = 2
GROUP = 7
SIDE = 4

epsilon = 1e-05
rope_base = 5000000.0
floor_score = -1e30

MESH = pl.DeviceIdType.MESH
BF = jnp.bfloat16
F32 = jnp.float32
VM = pl.BlockSpec(memory_space=pltpu.VMEM)
SM = pl.BlockSpec(memory_space=pltpu.SMEM)
VMEM_LIMIT = 60 * 1024 * 1024


def wide_place():
    w = lax.axis_index("wide")
    return lax.div(w, SIDE), lax.rem(w, SIDE)


def turn(pos, by):
    return lax.rem(pos + by, SIDE)


def ring_devices(axis, by):
    if axis == "x":
        n = lax.axis_index("narrow")
        return {"narrow": turn(lax.div(n, 2), by) * 2 + lax.rem(n, 2)}
    y, z = wide_place()
    if axis == "y":
        return {"wide": turn(y, by) * SIDE + z}
    return {"wide": y * SIDE + turn(z, by)}


def partner_device():
    n = lax.axis_index("narrow")
    return {"narrow": lax.div(n, 2) * 2 + 1 - lax.rem(n, 2)}


def greet(devices):
    barrier = pltpu.get_barrier_semaphore()
    for device in devices:
        pl.semaphore_signal(barrier, inc=1, device_id=device, device_id_type=MESH)
    pl.semaphore_wait(barrier, len(devices))


class Copies:
    def __init__(self, send_sem, recv_sem):
        self.send_sem, self.recv_sem, self.used, self.made = send_sem, recv_sem, 0, []

    def slot(self):
        self.used += 1
        return self.used - 1

    def start(self, slot, src, dst, device):
        copy = pltpu.make_async_remote_copy(
            src_ref=src,
            dst_ref=dst,
            send_sem=self.send_sem.at[slot],
            recv_sem=self.recv_sem.at[slot],
            device_id=device,
            device_id_type=MESH,
        )
        copy.start()
        self.made.append(copy)

    def arrived(self, slot, dst):
        pltpu.make_async_copy(dst, dst, self.recv_sem.at[slot]).wait()

    def sent(self):
        for copy in self.made:
            copy.wait_send()


def interleave(*parts):
    live = list(parts)
    while live:
        for part in list(live):
            try:
                next(part)
            except StopIteration:
                live.remove(part)


def gather_wide_steps(x_ref, out_ref, local_sem, copies):
    y, z = wide_place()
    depth = x_ref.shape[1] // 2
    lower, upper = pl.ds(0, depth), pl.ds(depth, depth)

    def place(half, first, second):
        if half == 0:
            return out_ref.at[first, second, 0]
        return out_ref.at[second, first, 1]

    names = (("y", "z"), ("z", "y"))
    spots = ((y, z), (z, y))
    own = pltpu.make_async_copy(x_ref, out_ref.at[y, z], local_sem)
    own.start()
    hop1 = [[copies.slot() for _ in range(4)] for _ in range(2)]
    hop2 = [[[copies.slot() for _ in range(4)] for _ in range(4)] for _ in range(2)]

    def send2(half, block, src):
        first = turn(spots[half][0], block)
        target = place(half, first, spots[half][1])
        for way, by in ((0, 1), (1, 3)):
            copies.start(hop2[half][block][way], src, target, ring_devices(names[half][1], by))

    def relay2(half, block):
        first = turn(spots[half][0], block)
        for way, by, part in ((0, 1, lower), (1, 3, upper)):
            came = place(half, first, turn(spots[half][1], 4 - by))
            copies.arrived(hop2[half][block][way], came)
            copies.start(
                hop2[half][block][2 + way], came.at[part], came.at[part], ring_devices(names[half][1], by)
            )

    for half in range(2):
        target = place(half, *spots[half])
        for way, by in ((0, 1), (1, 3)):
            copies.start(hop1[half][way], x_ref.at[half], target, ring_devices(names[half][0], by))
        send2(half, 0, x_ref.at[half])
    yield
    for half in range(2):
        for way, by, part in ((0, 1, lower), (1, 3, upper)):
            came = place(half, turn(spots[half][0], 4 - by), spots[half][1])
            copies.arrived(hop1[half][way], came)
            copies.start(hop1[half][2 + way], came.at[part], came.at[part], ring_devices(names[half][0], by))
            send2(half, 4 - by, came)
        yield
    for half in range(2):
        relay2(half, 0)
        yield
    for half in range(2):
        far = place(half, turn(spots[half][0], 2), spots[half][1])
        copies.arrived(hop1[half][2], far.at[lower])
        copies.arrived(hop1[half][3], far.at[upper])
        send2(half, 2, far)
        yield
    for block in (3, 1, 2):
        for half in range(2):
            relay2(half, block)
            yield
    for half in range(2):
        for block in (0, 3, 1, 2):
            far = place(half, turn(spots[half][0], block), turn(spots[half][1], 2))
            copies.arrived(hop2[half][block][2], far.at[lower])
            copies.arrived(hop2[half][block][3], far.at[upper])
    own.wait()


WIDE_COPIES = 40


def gather_direct_steps(x_ref, out_ref, local_sem, copies):
    y, z = wide_place()
    names = (("y", "z"), ("z", "y"))
    spots = ((y, z), (z, y))

    def place(half, first, second):
        if half == 0:
            return out_ref.at[first, second, 0]
        return out_ref.at[second, first, 1]

    own = pltpu.make_async_copy(x_ref, out_ref.at[y, z], local_sem)
    own.start()
    hop1 = [[copies.slot() for _ in range(3)] for _ in range(2)]
    hop2 = [[[copies.slot() for _ in range(3)] for _ in range(4)] for _ in range(2)]

    def send2(half, block, src):
        target = place(half, turn(spots[half][0], block), spots[half][1])
        for by in (2, 1, 3):
            copies.start(hop2[half][block][by - 1], src, target, ring_devices(names[half][1], by))

    for half in range(2):
        target = place(half, *spots[half])
        for by in (2, 1, 3):
            copies.start(hop1[half][by - 1], x_ref.at[half], target, ring_devices(names[half][0], by))
    for half in range(2):
        send2(half, 0, x_ref.at[half])
    yield
    for by in (1, 3, 2):
        for half in range(2):
            came = place(half, turn(spots[half][0], 4 - by), spots[half][1])
            copies.arrived(hop1[half][by - 1], came)
            send2(half, 4 - by, came)
        yield
    for block in range(4):
        for half in range(2):
            for by in (1, 3, 2):
                came = place(half, turn(spots[half][0], block), turn(spots[half][1], 4 - by))
                copies.arrived(hop2[half][block][by - 1], came)
    own.wait()


DIRECT_COPIES = 30


def wide_lines():
    return [ring_devices(axis, by) for axis in ("y", "z") for by in (1, 2, 3)]


def wide_neighbours():
    return [ring_devices(axis, by) for axis in ("y", "z") for by in (1, 3)]


def gather_wide_kernel(x_ref, out_ref, local_sem, send_sem, recv_sem):
    copies = Copies(send_sem, recv_sem)
    greet(wide_neighbours())
    interleave(gather_wide_steps(x_ref, out_ref, local_sem, copies))
    copies.sent()


def gather_wide(x, collective_id):
    return pl.pallas_call(
        gather_wide_kernel,
        out_shape=jax.ShapeDtypeStruct((SIDE, SIDE) + x.shape, x.dtype),
        in_specs=[VM],
        out_specs=VM,
        scratch_shapes=[
            pltpu.SemaphoreType.DMA,
            pltpu.SemaphoreType.DMA((WIDE_COPIES,)),
            pltpu.SemaphoreType.DMA((WIDE_COPIES,)),
        ],
        compiler_params=pltpu.CompilerParams(
            collective_id=collective_id, has_side_effects=True, vmem_limit_bytes=VMEM_LIMIT
        ),
        name=f"gather_wide_{collective_id}",
    )(x)


def gather_narrow_steps(x_ref, out_ref, local_sem, copies):
    n = lax.axis_index("narrow")
    x, core = lax.div(n, 2), lax.rem(n, 2)
    depth = x_ref.shape[0] // 2
    lower, upper = pl.ds(0, depth), pl.ds(depth, depth)
    own = pltpu.make_async_copy(x_ref, out_ref.at[n], local_sem)
    own.start()
    slots = [copies.slot() for _ in range(8)]
    for way, by in ((0, 1), (1, 3)):
        copies.start(slots[way], x_ref, out_ref.at[n], ring_devices("x", by))
    copies.start(slots[4], x_ref, out_ref.at[n], partner_device())
    yield
    for way, by, part in ((0, 1, lower), (1, 3, upper)):
        came = out_ref.at[turn(x, 4 - by) * 2 + core]
        copies.arrived(slots[way], came)
        copies.start(slots[2 + way], came.at[part], came.at[part], ring_devices("x", by))
        copies.start(slots[5 + way], came, came, partner_device())
    yield
    far = out_ref.at[turn(x, 2) * 2 + core]
    copies.arrived(slots[2], far.at[lower])
    copies.arrived(slots[3], far.at[upper])
    copies.start(slots[7], far, far, partner_device())
    yield
    for slot, by in ((4, 0), (5, 3), (6, 1), (7, 2)):
        copies.arrived(slots[slot], out_ref.at[turn(x, by) * 2 + 1 - core])
    own.wait()


NARROW_COPIES = 8


def narrow_neighbours():
    return [ring_devices("x", 1), ring_devices("x", 3), partner_device()]


def gather_narrow_kernel(x_ref, out_ref, local_sem, send_sem, recv_sem):
    copies = Copies(send_sem, recv_sem)
    greet(narrow_neighbours())
    interleave(gather_narrow_steps(x_ref, out_ref, local_sem, copies))
    copies.sent()


def gather_narrow(x, collective_id):
    return pl.pallas_call(
        gather_narrow_kernel,
        out_shape=jax.ShapeDtypeStruct((8,) + x.shape, x.dtype),
        in_specs=[VM],
        out_specs=VM,
        scratch_shapes=[
            pltpu.SemaphoreType.DMA,
            pltpu.SemaphoreType.DMA((NARROW_COPIES,)),
            pltpu.SemaphoreType.DMA((NARROW_COPIES,)),
        ],
        compiler_params=pltpu.CompilerParams(
            collective_id=collective_id, has_side_effects=True, vmem_limit_bytes=VMEM_LIMIT
        ),
        name=f"gather_narrow_{collective_id}",
    )(x)


def gather_both_kernel(x_ref, cache_ref, xo_ref, cacheo_ref, local_sem, send_n, recv_n, send_w, recv_w):
    near, far = Copies(send_n, recv_n), Copies(send_w, recv_w)
    greet(narrow_neighbours() + wide_neighbours())
    interleave(
        gather_narrow_steps(x_ref, xo_ref, local_sem.at[0], near),
        gather_wide_steps(cache_ref, cacheo_ref, local_sem.at[1], far),
    )
    near.sent()
    far.sent()


def gather_both(x, cache, collective_id):
    return pl.pallas_call(
        gather_both_kernel,
        out_shape=(
            jax.ShapeDtypeStruct((8,) + x.shape, x.dtype),
            jax.ShapeDtypeStruct((SIDE, SIDE) + cache.shape, cache.dtype),
        ),
        in_specs=[VM, VM],
        out_specs=(VM, VM),
        scratch_shapes=[
            pltpu.SemaphoreType.DMA((2,)),
            pltpu.SemaphoreType.DMA((NARROW_COPIES,)),
            pltpu.SemaphoreType.DMA((NARROW_COPIES,)),
            pltpu.SemaphoreType.DMA((WIDE_COPIES,)),
            pltpu.SemaphoreType.DMA((WIDE_COPIES,)),
        ],
        compiler_params=pltpu.CompilerParams(
            collective_id=collective_id, has_side_effects=True, vmem_limit_bytes=VMEM_LIMIT
        ),
        name="gather_both",
    )(x, cache)


def sum_narrow_kernel(p_ref, out_ref, mate, total, relay, direct, joined, send_sem, recv_sem):
    copies = Copies(send_sem, recv_sem)
    n = lax.axis_index("narrow")
    x, core = lax.div(n, 2), lax.rem(n, 2)
    width = p_ref.shape[3] // 2
    lower, upper = pl.ds(0, width), pl.ds(width, width)
    right, left = ring_devices("x", 1), ring_devices("x", 3)
    greet(narrow_neighbours())
    order = (2, 1, 3, 0)
    mates = {by: copies.slot() for by in order}
    slots = [copies.slot() for _ in range(6)]
    for by in order:
        copies.start(mates[by], p_ref.at[turn(x, by), 1 - core], mate.at[by], partner_device())

    def pair(by):
        copies.arrived(mates[by], mate.at[by])
        return p_ref[turn(x, by), core].astype(F32) + mate[by].astype(F32)

    total[2] = pair(2).astype(BF)
    copies.start(slots[0], total.at[2, :, lower], relay.at[0], right)
    copies.start(slots[1], total.at[2, :, upper], relay.at[1], left)
    total[1] = pair(1).astype(BF)
    copies.start(slots[2], total.at[1, :, upper], direct.at[0], right)
    total[3] = pair(3).astype(BF)
    copies.start(slots[3], total.at[3, :, lower], direct.at[1], left)
    copies.arrived(slots[0], relay.at[0])
    total[1, :, lower] = (total[1, :, lower].astype(F32) + relay[0].astype(F32)).astype(BF)
    copies.start(slots[4], total.at[1, :, lower], joined.at[0], right)
    copies.arrived(slots[1], relay.at[1])
    total[3, :, upper] = (total[3, :, upper].astype(F32) + relay[1].astype(F32)).astype(BF)
    copies.start(slots[5], total.at[3, :, upper], joined.at[1], left)
    out_ref[...] = pair(0)
    copies.arrived(slots[2], direct.at[0])
    out_ref[:, upper] += direct[0].astype(F32)
    copies.arrived(slots[3], direct.at[1])
    out_ref[:, lower] += direct[1].astype(F32)
    copies.arrived(slots[4], joined.at[0])
    out_ref[:, lower] += joined[0].astype(F32)
    copies.arrived(slots[5], joined.at[1])
    out_ref[:, upper] += joined[1].astype(F32)
    copies.sent()


def sum_narrow(p, collective_id):
    rows, cols = p.shape[2:]
    piece = pltpu.VMEM((2, rows, cols // 2), BF)
    return pl.pallas_call(
        sum_narrow_kernel,
        out_shape=jax.ShapeDtypeStruct((rows, cols), F32),
        in_specs=[VM],
        out_specs=VM,
        scratch_shapes=[
            pltpu.VMEM((4, rows, cols), BF),
            pltpu.VMEM((4, rows, cols), BF),
            piece,
            piece,
            piece,
            pltpu.SemaphoreType.DMA((10,)),
            pltpu.SemaphoreType.DMA((10,)),
        ],
        compiler_params=pltpu.CompilerParams(
            collective_id=collective_id, has_side_effects=True, vmem_limit_bytes=VMEM_LIMIT
        ),
        name=f"sum_narrow_{collective_id}",
    )(p)


def matmul_sum_kernel(
    x_ref, w_ref, sq_ref, out_ref, sqo_ref, part, mid, got1, got2, sq1, sqm, sq2,
    send1, recv1, send2, recv2, sq_send, sq_recv,
):
    pieces, width = part.shape[0], part.shape[-1]
    rows = x_ref.shape[3]
    y, z = wide_place()
    names = (("y", "z"), ("z", "y"))
    spots = ((y, z), (z, y))
    greet([ring_devices(axis, by) for axis in ("y", "z") for by in (1, 2, 3)])
    squares = Copies(sq_send, sq_recv)
    for by in (1, 2, 3):
        squares.start(by - 1, sq_ref.at[turn(y, by)], sq1.at[by - 1], ring_devices("y", by))

    def product(half, chunk, piece):
        block = x_ref[chunk, :, 0] if half == 0 else x_ref[:, chunk, 1]
        block = block.reshape(SIDE * rows, block.shape[-1])
        columns = pl.ds(pl.multiple_of(piece * width, 128), width)
        got = jnp.dot(block, w_ref[:, columns], preferred_element_type=F32)
        return got.reshape(SIDE, rows, width)

    def copy1(piece, half, kind, way, src):
        return pltpu.make_async_remote_copy(
            src_ref=src,
            dst_ref=got1.at[piece, half, kind, way],
            send_sem=send1.at[piece, half, kind, way],
            recv_sem=recv1.at[piece, half, kind, way],
            device_id=ring_devices(names[half][0], 1 if way == 0 else 3),
            device_id_type=MESH,
        )

    def copy2(piece, half, kind, way, src):
        return pltpu.make_async_remote_copy(
            src_ref=src,
            dst_ref=got2.at[piece, half, kind, way],
            send_sem=send2.at[piece, half, kind, way],
            recv_sem=recv2.at[piece, half, kind, way],
            device_id=ring_devices(names[half][1], 1 if way == 0 else 3),
            device_id_type=MESH,
        )

    def await1(piece, half, kind, way):
        ref = got1.at[piece, half, kind, way]
        pltpu.make_async_copy(ref, ref, recv1.at[piece, half, kind, way]).wait()
        return got1[piece, half, kind, way].astype(F32)

    def await2(piece, half, kind, way):
        ref = got2.at[piece, half, kind, way]
        pltpu.make_async_copy(ref, ref, recv2.at[piece, half, kind, way]).wait()
        return got2[piece, half, kind, way].astype(F32)

    lower, upper = pl.ds(0, 2), pl.ds(2, 2)
    low, high = pl.ds(0, rows // 2), pl.ds(rows // 2, rows // 2)

    def first(piece):
        for half in range(2):
            far = turn(spots[half][0], 2)
            part[piece, half, far] = product(half, far, piece).astype(BF)
            copy1(piece, half, 0, 0, part.at[piece, half, far, lower]).start()
            copy1(piece, half, 0, 1, part.at[piece, half, far, upper]).start()
        for half in range(2):
            right, left = turn(spots[half][0], 1), turn(spots[half][0], 3)
            part[piece, half, right] = product(half, right, piece).astype(BF)
            copy1(piece, half, 1, 0, part.at[piece, half, right, upper]).start()
            part[piece, half, left] = product(half, left, piece).astype(BF)
            copy1(piece, half, 1, 1, part.at[piece, half, left, lower]).start()

    def second(piece):
        for half in range(2):
            right, left = turn(spots[half][0], 1), turn(spots[half][0], 3)
            got = await1(piece, half, 0, 0)
            part[piece, half, right, lower] = (part[piece, half, right, lower].astype(F32) + got).astype(BF)
            copy1(piece, half, 2, 0, part.at[piece, half, right, lower]).start()
            got = await1(piece, half, 0, 1)
            part[piece, half, left, upper] = (part[piece, half, left, upper].astype(F32) + got).astype(BF)
            copy1(piece, half, 2, 1, part.at[piece, half, left, upper]).start()

    def third(piece):
        for half in range(2):
            own = product(half, spots[half][0], piece)
            mid[piece, half, lower] = (
                own[:2] + await1(piece, half, 1, 1) + await1(piece, half, 2, 0)
            ).astype(BF)
            mid[piece, half, upper] = (
                own[2:] + await1(piece, half, 1, 0) + await1(piece, half, 2, 1)
            ).astype(BF)
            far, right, left = (turn(spots[half][1], by) for by in (2, 1, 3))
            copy2(piece, half, 0, 0, mid.at[piece, half, far, low]).start()
            copy2(piece, half, 0, 1, mid.at[piece, half, far, high]).start()
            copy2(piece, half, 1, 0, mid.at[piece, half, right, high]).start()
            copy2(piece, half, 1, 1, mid.at[piece, half, left, low]).start()

    def fourth(piece):
        for half in range(2):
            right, left = turn(spots[half][1], 1), turn(spots[half][1], 3)
            got = await2(piece, half, 0, 0)
            mid[piece, half, right, low] = (mid[piece, half, right, low].astype(F32) + got).astype(BF)
            copy2(piece, half, 2, 0, mid.at[piece, half, right, low]).start()
            got = await2(piece, half, 0, 1)
            mid[piece, half, left, high] = (mid[piece, half, left, high].astype(F32) + got).astype(BF)
            copy2(piece, half, 2, 1, mid.at[piece, half, left, high]).start()

    def fifth(piece):
        columns = pl.ds(pl.multiple_of(piece * width, 128), width)
        for half in range(2):
            own = spots[half][1]
            out_ref[half, low, columns] = (
                mid[piece, half, own, low].astype(F32) + await2(piece, half, 1, 1) + await2(piece, half, 2, 0)
            )
            out_ref[half, high, columns] = (
                mid[piece, half, own, high].astype(F32) + await2(piece, half, 1, 0) + await2(piece, half, 2, 1)
            )

    stages = (first, second, third, fourth, fifth)

    def step(t, carry):
        for lag, stage in enumerate(stages):
            piece = t - lag

            @pl.when((piece >= 0) & (piece < pieces))
            def _():
                stage(jnp.clip(piece, 0, pieces - 1))

        return carry

    lax.fori_loop(0, pieces + len(stages) - 1, step, 0)

    for by in (1, 2, 3):
        squares.arrived(by - 1, sq1.at[by - 1])
    sqm[...] = sq_ref[y] + sq1[0] + sq1[1] + sq1[2]
    for by in (1, 2, 3):
        squares.start(2 + by, sqm.at[turn(z, by)], sq2.at[by - 1], ring_devices("z", by))
    for by in (1, 2, 3):
        squares.arrived(2 + by, sq2.at[by - 1])
    sqo_ref[...] = sqm[z] + sq2[0] + sq2[1] + sq2[2]
    squares.sent()

    def drain(piece, carry):
        for half in range(2):
            for kind in range(3):
                for way in range(2):
                    copy1(piece, half, kind, way, part.at[piece, half, 0, lower]).wait_send()
                    copy2(piece, half, kind, way, mid.at[piece, half, 0, low]).wait_send()
        return carry

    lax.fori_loop(0, pieces, drain, 0)


def matmul_sum(x, w, sq, pieces, collective_id):
    tokens, depth = x.shape
    cols = w.shape[1]
    width = cols // pieces
    rows = tokens // (2 * SIDE * SIDE)
    blocks = jnp.pad(sq.reshape(SIDE, SIDE, 1, 2 * rows), ((0, 0), (0, 0), (0, 0), (0, 128 - 2 * rows)))
    blocks = jnp.broadcast_to(blocks, (SIDE, SIDE, 8, 128))
    out, sq_out = pl.pallas_call(
        matmul_sum_kernel,
        out_shape=(
            jax.ShapeDtypeStruct((2, rows, cols), F32),
            jax.ShapeDtypeStruct((8, 128), F32),
        ),
        in_specs=[VM, VM, VM],
        out_specs=(VM, VM),
        scratch_shapes=[
            pltpu.VMEM((pieces, 2, SIDE, SIDE, rows, width), BF),
            pltpu.VMEM((pieces, 2, SIDE, rows, width), BF),
            pltpu.VMEM((pieces, 2, 3, 2, 2, rows, width), BF),
            pltpu.VMEM((pieces, 2, 3, 2, rows // 2, width), BF),
            pltpu.VMEM((3, SIDE, 8, 128), F32),
            pltpu.VMEM((SIDE, 8, 128), F32),
            pltpu.VMEM((3, 8, 128), F32),
            pltpu.SemaphoreType.DMA((pieces, 2, 3, 2)),
            pltpu.SemaphoreType.DMA((pieces, 2, 3, 2)),
            pltpu.SemaphoreType.DMA((pieces, 2, 3, 2)),
            pltpu.SemaphoreType.DMA((pieces, 2, 3, 2)),
            pltpu.SemaphoreType.DMA((6,)),
            pltpu.SemaphoreType.DMA((6,)),
        ],
        compiler_params=pltpu.CompilerParams(
            collective_id=collective_id, has_side_effects=True, vmem_limit_bytes=VMEM_LIMIT
        ),
        name=f"matmul_sum_{collective_id}",
    )(x.reshape(SIDE, SIDE, 2, rows, depth), w, blocks)
    return out.reshape(2 * rows, cols), sq_out[0, : 2 * rows]


CHUNK = 2


def attend_kernel(
    lengths_ref, q_ref, cache_ref, own_ref, out_ref, sums_ref, span_ref, local_sem, send_sem, recv_sem
):
    scale = HDIM ** (-0.5)
    rows = q_ref.shape[1]
    per = own_ref.shape[1]
    block = cache_ref.shape[2] * CHUNK
    spot = lax.axis_index("wide")
    copies = Copies(send_sem, recv_sem)
    greet(wide_lines())
    gather = gather_direct_steps(own_ref, span_ref, local_sem, copies)
    next(gather)
    queries = [q_ref[request] for request in range(R)]

    def absorb(running, q, keys, values, allowed):
        peak, weight_sum, gathered = running
        scores = lax.dot_general(q, keys, (((1,), (1,)), ((), ())), preferred_element_type=F32) * scale
        scores = jnp.where(allowed(scores.shape), scores, floor_score)
        new_peak = jnp.maximum(peak, jnp.max(scores, axis=1, keepdims=True))
        weights = jnp.exp(scores - new_peak)
        factor = jnp.exp(peak - new_peak)
        weight_sum = weight_sum * factor + jnp.sum(weights, axis=1, keepdims=True)
        gathered = gathered * factor + jnp.dot(weights.astype(BF), values, preferred_element_type=F32)
        return new_peak, weight_sum, gathered

    def own_keys(shape):
        key = lax.broadcasted_iota(jnp.int32, shape, 1)
        row = lax.broadcasted_iota(jnp.int32, shape, 0)
        return key <= spot * per + lax.rem(row, per)

    running = [
        (
            jnp.full((rows, 1), floor_score, F32),
            jnp.zeros((rows, 1), F32),
            jnp.zeros((rows, HDIM), F32),
        )
        for _ in range(R)
    ]
    for index in range(cache_ref.shape[0] // CHUNK):
        for request in range(R):
            pair = cache_ref[pl.ds(index * CHUNK, CHUNK), request].reshape(block, 2 * HDIM)
            running[request] = absorb(
                running[request],
                queries[request],
                pair[:, :HDIM],
                pair[:, HDIM:],
                lambda shape: index * block + lax.broadcasted_iota(jnp.int32, shape, 1) < lengths_ref[request],
            )
        if index >= 2:
            next(gather, None)
    interleave(gather)
    for request in range(R):
        span = span_ref[:, :, request].reshape(SIDE * SIDE * per, 2 * HDIM)
        peak, weight_sum, gathered = absorb(
            running[request], queries[request], span[:, :HDIM], span[:, HDIM:], own_keys
        )
        out_ref[request] = (gathered / weight_sum).astype(BF)
        sums_ref[request] = jnp.broadcast_to(peak + jnp.log(weight_sum), (rows, HDIM))
    copies.sent()


def attend(lengths, queries, cache, own, collective_id):
    return pl.pallas_call(
        attend_kernel,
        out_shape=(
            jax.ShapeDtypeStruct(queries.shape, BF),
            jax.ShapeDtypeStruct(queries.shape, F32),
        ),
        in_specs=[SM, VM, VM, VM],
        out_specs=(VM, VM),
        scratch_shapes=[
            pltpu.VMEM((SIDE, SIDE) + own.shape, BF),
            pltpu.SemaphoreType.DMA,
            pltpu.SemaphoreType.DMA((DIRECT_COPIES,)),
            pltpu.SemaphoreType.DMA((DIRECT_COPIES,)),
        ],
        compiler_params=pltpu.CompilerParams(
            collective_id=collective_id, has_side_effects=True, vmem_limit_bytes=VMEM_LIMIT
        ),
        name="attend",
    )(lengths, queries, cache, own)


def token_angles(lengths, offsets, first_token, row_count, dim_size):
    token_ids = first_token + jnp.arange(row_count, dtype=jnp.int32)
    request_ids = token_ids % R
    start_pos = offsets + lengths
    matches = request_ids[:, None] == jnp.arange(start_pos.shape[0], dtype=jnp.int32)[None, :]
    chosen = jnp.sum(jnp.where(matches, start_pos[None, :], 0), axis=1)
    position = (chosen + token_ids // R).astype(jnp.float32)
    inverse = rope_base ** (-(jnp.arange(dim_size // 2, dtype=jnp.float32) * 2.0) / dim_size)
    return position[:, None] * inverse[None, :]


def rotate(values, angles):
    half_dim = values.shape[-1] // 2
    first_half = values[..., :half_dim]
    second_half = values[..., half_dim:]
    cosine = jnp.cos(angles)[:, None, :]
    sine_part = jnp.sin(angles)[:, None, :]
    return jnp.concatenate(
        [
            first_half * cosine - second_half * sine_part,
            second_half * cosine + first_half * sine_part,
        ],
        axis=-1,
    )


def to_send(flipped, gain):
    widened = flipped.astype(F32)
    squares = jnp.sum(widened * widened, axis=0, keepdims=True)
    high = lax.reduce_precision(squares, 8, 7)
    rest = squares - high
    middle = lax.reduce_precision(rest, 8, 7)
    low = rest - middle
    scaled = widened * gain.astype(F32)[:, None]
    pad = jnp.zeros((5, flipped.shape[1]), F32)
    return jnp.concatenate([scaled, high, middle, low, pad], axis=0).astype(BF)


def unpack(gathered, rows):
    scaled = gathered[:, :rows].reshape(8 * rows, -1).T
    squares = jnp.sum(gathered[:, rows : rows + 3].astype(F32), axis=(0, 1))
    return scaled, squares


def rescale(sums, squares):
    inv_scale = lax.rsqrt(squares / D + epsilon)[:, None]
    return jnp.where(inv_scale > 0, sums * inv_scale, 0.0)


def local(
    hidden_in, attn_gain, w_qkv, cache_kv, lengths, offsets, w_out, mlp_gain, w_gate_up, w_down
):
    all_tokens, features = hidden_in.shape
    per_device = all_tokens // lax.axis_size("wide")
    first_token = lax.axis_index("wide") * per_device
    flipped = hidden_in.T
    positions = cache_kv.shape[1]
    cache = cache_kv.reshape(R, positions, 2 * HDIM)
    gathered, cache_all = gather_both(to_send(flipped, attn_gain), cache, 1)
    scaled, squares = unpack(gathered, features)
    projected, squares = matmul_sum(scaled, w_qkv.reshape(w_qkv.shape[0], -1), squares, 3, 2)
    projected = rescale(projected, squares).reshape(per_device, GROUP + 2, HDIM)
    angles = token_angles(lengths, offsets, first_token, per_device, HDIM)
    rotated = rotate(projected[:, : GROUP + 1], angles).astype(BF)
    new_keys, new_values = rotated[:, GROUP], projected[:, GROUP + 1].astype(BF)
    new_cache = jnp.stack([new_keys, new_values], axis=1)[:, None]
    per_request = per_device // R
    span = jnp.concatenate([new_keys, new_values], axis=1).reshape(per_request, R, 2 * HDIM)
    queries = rotated[:, :GROUP].reshape(per_request, R, GROUP, HDIM).transpose(1, 2, 0, 3)
    attended, sums = attend(
        lengths,
        queries.reshape(R, GROUP * per_request, HDIM),
        cache_all.reshape(SIDE * SIDE, R, positions, 2 * HDIM),
        span.transpose(1, 0, 2),
        3,
    )
    attended = attended.reshape(R, GROUP, per_request, HDIM).transpose(2, 0, 1, 3).reshape(2, -1, GROUP * HDIM)
    softmax_sums = sums[:, :, 0].reshape(R, GROUP, per_request).transpose(2, 0, 1).reshape(per_device, GROUP)
    attended_all = gather_wide(attended, 4).reshape(all_tokens, -1)
    out_terms = lax.dot_general(
        w_out, attended_all, (((0,), (1,)), ((), ())), preferred_element_type=F32
    ).astype(BF)
    summed = sum_narrow(out_terms.reshape(4, 2, features, all_tokens), 5)
    residual = (flipped.astype(F32) + summed).astype(BF)
    scaled, squares = unpack(gather_narrow(to_send(residual, mlp_gain), 6), features)
    units = w_gate_up.shape[2]
    both, squares = matmul_sum(scaled, w_gate_up.reshape(w_gate_up.shape[0], -1), squares, 4, 7)
    both = rescale(both, squares)
    hidden = (jax.nn.silu(both[:, :units]) * both[:, units:]).astype(BF)
    hidden_all = gather_wide(hidden.reshape(2, -1, units), 8).reshape(all_tokens, units)
    down_terms = lax.dot_general(
        w_down, hidden_all, (((0,), (1,)), ((), ())), preferred_element_type=F32
    ).astype(BF)
    summed = sum_narrow(down_terms.reshape(4, 2, features, all_tokens), 9)
    hidden_out = (residual.astype(F32) + summed).astype(BF).T
    return (hidden_out, softmax_sums, new_cache)


def solution(mesh):
    return jax.shard_map(
        local,
        mesh=mesh,
        in_specs=(
            P(None, ("wide", "narrow")),
            P(("wide", "narrow")),
            P("wide", "narrow", None),
            P(None, "wide", "narrow", None, None),
            P(),
            P(),
            P("narrow", "wide"),
            P(("wide", "narrow")),
            P("wide", None, "narrow"),
            P("narrow", "wide"),
        ),
        out_specs=(
            P(None, ("wide", "narrow")),
            P("wide", "narrow"),
            P("wide", "narrow", None, None),
        ),
        check_vma=False,
    )
```

```python
import functools

import jax
import jax.numpy as jnp
from jax import lax
from jax.experimental import pallas as pl
from jax.experimental.pallas import tpu as pltpu
from jax.sharding import PartitionSpec as P

D = 7168
HDIM = 128
R = 2
GROUP = 7
SIDE = 4

epsilon = 1e-05
rope_base = 5000000.0
floor_score = -1e30

MESH = pl.DeviceIdType.MESH
BF = jnp.bfloat16
F32 = jnp.float32
VM = pl.BlockSpec(memory_space=pltpu.VMEM)
SM = pl.BlockSpec(memory_space=pltpu.SMEM)
VMEM_LIMIT = 60 * 1024 * 1024


def wide_place():
    w = lax.axis_index("wide")
    return lax.div(w, SIDE), lax.rem(w, SIDE)


def turn(pos, by):
    return lax.rem(pos + by, SIDE)


def ring_devices(axis, by):
    if axis == "x":
        n = lax.axis_index("narrow")
        return {"narrow": turn(lax.div(n, 2), by) * 2 + lax.rem(n, 2)}
    y, z = wide_place()
    if axis == "y":
        return {"wide": turn(y, by) * SIDE + z}
    return {"wide": y * SIDE + turn(z, by)}


def partner_device():
    n = lax.axis_index("narrow")
    return {"narrow": lax.div(n, 2) * 2 + 1 - lax.rem(n, 2)}


def greet(devices):
    barrier = pltpu.get_barrier_semaphore()
    for device in devices:
        pl.semaphore_signal(barrier, inc=1, device_id=device, device_id_type=MESH)
    pl.semaphore_wait(barrier, len(devices))


class Copies:
    def __init__(self, send_sem, recv_sem):
        self.send_sem, self.recv_sem, self.used, self.made = send_sem, recv_sem, 0, []

    def slot(self):
        self.used += 1
        return self.used - 1

    def start(self, slot, src, dst, device):
        copy = pltpu.make_async_remote_copy(
            src_ref=src,
            dst_ref=dst,
            send_sem=self.send_sem.at[slot],
            recv_sem=self.recv_sem.at[slot],
            device_id=device,
            device_id_type=MESH,
        )
        copy.start()
        self.made.append(copy)

    def arrived(self, slot, dst):
        pltpu.make_async_copy(dst, dst, self.recv_sem.at[slot]).wait()

    def sent(self):
        for copy in self.made:
            copy.wait_send()


def interleave(*parts):
    live = list(parts)
    while live:
        for part in list(live):
            try:
                next(part)
            except StopIteration:
                live.remove(part)


def gather_wide_steps(x_ref, out_ref, local_sem, copies):
    y, z = wide_place()
    depth = x_ref.shape[1] // 2
    lower, upper = pl.ds(0, depth), pl.ds(depth, depth)

    def place(half, first, second):
        if half == 0:
            return out_ref.at[first, second, 0]
        return out_ref.at[second, first, 1]

    names = (("y", "z"), ("z", "y"))
    spots = ((y, z), (z, y))
    own = pltpu.make_async_copy(x_ref, out_ref.at[y, z], local_sem)
    own.start()
    hop1 = [[copies.slot() for _ in range(4)] for _ in range(2)]
    hop2 = [[[copies.slot() for _ in range(4)] for _ in range(4)] for _ in range(2)]

    def send2(half, block, src):
        first = turn(spots[half][0], block)
        target = place(half, first, spots[half][1])
        for way, by in ((0, 1), (1, 3)):
            copies.start(hop2[half][block][way], src, target, ring_devices(names[half][1], by))

    def relay2(half, block):
        first = turn(spots[half][0], block)
        for way, by, part in ((0, 1, lower), (1, 3, upper)):
            came = place(half, first, turn(spots[half][1], 4 - by))
            copies.arrived(hop2[half][block][way], came)
            copies.start(
                hop2[half][block][2 + way], came.at[part], came.at[part], ring_devices(names[half][1], by)
            )

    for half in range(2):
        target = place(half, *spots[half])
        for way, by in ((0, 1), (1, 3)):
            copies.start(hop1[half][way], x_ref.at[half], target, ring_devices(names[half][0], by))
        send2(half, 0, x_ref.at[half])
    yield
    for half in range(2):
        for way, by, part in ((0, 1, lower), (1, 3, upper)):
            came = place(half, turn(spots[half][0], 4 - by), spots[half][1])
            copies.arrived(hop1[half][way], came)
            copies.start(hop1[half][2 + way], came.at[part], came.at[part], ring_devices(names[half][0], by))
            send2(half, 4 - by, came)
        yield
    for half in range(2):
        relay2(half, 0)
        yield
    for half in range(2):
        far = place(half, turn(spots[half][0], 2), spots[half][1])
        copies.arrived(hop1[half][2], far.at[lower])
        copies.arrived(hop1[half][3], far.at[upper])
        send2(half, 2, far)
        yield
    for block in (3, 1, 2):
        for half in range(2):
            relay2(half, block)
            yield
    for half in range(2):
        for block in (0, 3, 1, 2):
            far = place(half, turn(spots[half][0], block), turn(spots[half][1], 2))
            copies.arrived(hop2[half][block][2], far.at[lower])
            copies.arrived(hop2[half][block][3], far.at[upper])
    own.wait()


WIDE_COPIES = 40


def gather_direct_steps(x_ref, out_ref, local_sem, copies):
    y, z = wide_place()
    names = (("y", "z"), ("z", "y"))
    spots = ((y, z), (z, y))

    def place(half, first, second):
        if half == 0:
            return out_ref.at[first, second, 0]
        return out_ref.at[second, first, 1]

    own = pltpu.make_async_copy(x_ref, out_ref.at[y, z], local_sem)
    own.start()
    hop1 = [[copies.slot() for _ in range(3)] for _ in range(2)]
    hop2 = [[[copies.slot() for _ in range(3)] for _ in range(4)] for _ in range(2)]

    def send2(half, block, src):
        target = place(half, turn(spots[half][0], block), spots[half][1])
        for by in (2, 1, 3):
            copies.start(hop2[half][block][by - 1], src, target, ring_devices(names[half][1], by))

    for half in range(2):
        target = place(half, *spots[half])
        for by in (2, 1, 3):
            copies.start(hop1[half][by - 1], x_ref.at[half], target, ring_devices(names[half][0], by))
    for half in range(2):
        send2(half, 0, x_ref.at[half])
    yield
    for by in (1, 3, 2):
        for half in range(2):
            came = place(half, turn(spots[half][0], 4 - by), spots[half][1])
            copies.arrived(hop1[half][by - 1], came)
            send2(half, 4 - by, came)
        yield
    for block in range(4):
        for half in range(2):
            for by in (1, 3, 2):
                came = place(half, turn(spots[half][0], block), turn(spots[half][1], 4 - by))
                copies.arrived(hop2[half][block][by - 1], came)
    own.wait()


DIRECT_COPIES = 30


def wide_lines():
    return [ring_devices(axis, by) for axis in ("y", "z") for by in (1, 2, 3)]


def wide_neighbours():
    return [ring_devices(axis, by) for axis in ("y", "z") for by in (1, 3)]


def gather_wide_kernel(x_ref, out_ref, local_sem, send_sem, recv_sem):
    copies = Copies(send_sem, recv_sem)
    greet(wide_neighbours())
    interleave(gather_wide_steps(x_ref, out_ref, local_sem, copies))
    copies.sent()


def gather_wide(x, collective_id):
    return pl.pallas_call(
        gather_wide_kernel,
        out_shape=jax.ShapeDtypeStruct((SIDE, SIDE) + x.shape, x.dtype),
        in_specs=[VM],
        out_specs=VM,
        scratch_shapes=[
            pltpu.SemaphoreType.DMA,
            pltpu.SemaphoreType.DMA((WIDE_COPIES,)),
            pltpu.SemaphoreType.DMA((WIDE_COPIES,)),
        ],
        compiler_params=pltpu.CompilerParams(
            collective_id=collective_id, has_side_effects=True, vmem_limit_bytes=VMEM_LIMIT
        ),
        name=f"gather_wide_{collective_id}",
    )(x)


def gather_narrow_steps(x_ref, out_ref, local_sem, copies):
    n = lax.axis_index("narrow")
    x, core = lax.div(n, 2), lax.rem(n, 2)
    depth = x_ref.shape[0] // 2
    lower, upper = pl.ds(0, depth), pl.ds(depth, depth)
    own = pltpu.make_async_copy(x_ref, out_ref.at[n], local_sem)
    own.start()
    slots = [copies.slot() for _ in range(8)]
    for way, by in ((0, 1), (1, 3)):
        copies.start(slots[way], x_ref, out_ref.at[n], ring_devices("x", by))
    copies.start(slots[4], x_ref, out_ref.at[n], partner_device())
    yield
    for way, by, part in ((0, 1, lower), (1, 3, upper)):
        came = out_ref.at[turn(x, 4 - by) * 2 + core]
        copies.arrived(slots[way], came)
        copies.start(slots[2 + way], came.at[part], came.at[part], ring_devices("x", by))
        copies.start(slots[5 + way], came, came, partner_device())
    yield
    far = out_ref.at[turn(x, 2) * 2 + core]
    copies.arrived(slots[2], far.at[lower])
    copies.arrived(slots[3], far.at[upper])
    copies.start(slots[7], far, far, partner_device())
    yield
    for slot, by in ((4, 0), (5, 3), (6, 1), (7, 2)):
        copies.arrived(slots[slot], out_ref.at[turn(x, by) * 2 + 1 - core])
    own.wait()


NARROW_COPIES = 8


def narrow_neighbours():
    return [ring_devices("x", 1), ring_devices("x", 3), partner_device()]


def gather_narrow_kernel(x_ref, out_ref, local_sem, send_sem, recv_sem):
    copies = Copies(send_sem, recv_sem)
    greet(narrow_neighbours())
    interleave(gather_narrow_steps(x_ref, out_ref, local_sem, copies))
    copies.sent()


def gather_narrow(x, collective_id):
    return pl.pallas_call(
        gather_narrow_kernel,
        out_shape=jax.ShapeDtypeStruct((8,) + x.shape, x.dtype),
        in_specs=[VM],
        out_specs=VM,
        scratch_shapes=[
            pltpu.SemaphoreType.DMA,
            pltpu.SemaphoreType.DMA((NARROW_COPIES,)),
            pltpu.SemaphoreType.DMA((NARROW_COPIES,)),
        ],
        compiler_params=pltpu.CompilerParams(
            collective_id=collective_id, has_side_effects=True, vmem_limit_bytes=VMEM_LIMIT
        ),
        name=f"gather_narrow_{collective_id}",
    )(x)


def gather_both_kernel(x_ref, cache_ref, xo_ref, cacheo_ref, local_sem, send_n, recv_n, send_w, recv_w):
    near, far = Copies(send_n, recv_n), Copies(send_w, recv_w)
    greet(narrow_neighbours() + wide_neighbours())
    interleave(
        gather_narrow_steps(x_ref, xo_ref, local_sem.at[0], near),
        gather_wide_steps(cache_ref, cacheo_ref, local_sem.at[1], far),
    )
    near.sent()
    far.sent()


def gather_both(x, cache, collective_id):
    return pl.pallas_call(
        gather_both_kernel,
        out_shape=(
            jax.ShapeDtypeStruct((8,) + x.shape, x.dtype),
            jax.ShapeDtypeStruct((SIDE, SIDE) + cache.shape, cache.dtype),
        ),
        in_specs=[VM, VM],
        out_specs=(VM, VM),
        scratch_shapes=[
            pltpu.SemaphoreType.DMA((2,)),
            pltpu.SemaphoreType.DMA((NARROW_COPIES,)),
            pltpu.SemaphoreType.DMA((NARROW_COPIES,)),
            pltpu.SemaphoreType.DMA((WIDE_COPIES,)),
            pltpu.SemaphoreType.DMA((WIDE_COPIES,)),
        ],
        compiler_params=pltpu.CompilerParams(
            collective_id=collective_id, has_side_effects=True, vmem_limit_bytes=VMEM_LIMIT
        ),
        name="gather_both",
    )(x, cache)


def sum_narrow_kernel(p_ref, out_ref, mate, total, relay, direct, joined, send_sem, recv_sem):
    copies = Copies(send_sem, recv_sem)
    n = lax.axis_index("narrow")
    x, core = lax.div(n, 2), lax.rem(n, 2)
    width = p_ref.shape[3] // 2
    lower, upper = pl.ds(0, width), pl.ds(width, width)
    right, left = ring_devices("x", 1), ring_devices("x", 3)
    greet(narrow_neighbours())
    order = (2, 1, 3, 0)
    mates = {by: copies.slot() for by in order}
    slots = [copies.slot() for _ in range(6)]
    for by in order:
        copies.start(mates[by], p_ref.at[turn(x, by), 1 - core], mate.at[by], partner_device())

    def pair(by):
        copies.arrived(mates[by], mate.at[by])
        return p_ref[turn(x, by), core].astype(F32) + mate[by].astype(F32)

    total[2] = pair(2).astype(BF)
    copies.start(slots[0], total.at[2, :, lower], relay.at[0], right)
    copies.start(slots[1], total.at[2, :, upper], relay.at[1], left)
    total[1] = pair(1).astype(BF)
    copies.start(slots[2], total.at[1, :, upper], direct.at[0], right)
    total[3] = pair(3).astype(BF)
    copies.start(slots[3], total.at[3, :, lower], direct.at[1], left)
    copies.arrived(slots[0], relay.at[0])
    total[1, :, lower] = (total[1, :, lower].astype(F32) + relay[0].astype(F32)).astype(BF)
    copies.start(slots[4], total.at[1, :, lower], joined.at[0], right)
    copies.arrived(slots[1], relay.at[1])
    total[3, :, upper] = (total[3, :, upper].astype(F32) + relay[1].astype(F32)).astype(BF)
    copies.start(slots[5], total.at[3, :, upper], joined.at[1], left)
    out_ref[...] = pair(0)
    copies.arrived(slots[2], direct.at[0])
    out_ref[:, upper] += direct[0].astype(F32)
    copies.arrived(slots[3], direct.at[1])
    out_ref[:, lower] += direct[1].astype(F32)
    copies.arrived(slots[4], joined.at[0])
    out_ref[:, lower] += joined[0].astype(F32)
    copies.arrived(slots[5], joined.at[1])
    out_ref[:, upper] += joined[1].astype(F32)
    copies.sent()


def sum_narrow(p, collective_id):
    rows, cols = p.shape[2:]
    piece = pltpu.VMEM((2, rows, cols // 2), BF)
    return pl.pallas_call(
        sum_narrow_kernel,
        out_shape=jax.ShapeDtypeStruct((rows, cols), F32),
        in_specs=[VM],
        out_specs=VM,
        scratch_shapes=[
            pltpu.VMEM((4, rows, cols), BF),
            pltpu.VMEM((4, rows, cols), BF),
            piece,
            piece,
            piece,
            pltpu.SemaphoreType.DMA((10,)),
            pltpu.SemaphoreType.DMA((10,)),
        ],
        compiler_params=pltpu.CompilerParams(
            collective_id=collective_id, has_side_effects=True, vmem_limit_bytes=VMEM_LIMIT
        ),
        name=f"sum_narrow_{collective_id}",
    )(p)


def matmul_sum_kernel(
    x_ref, w_ref, sq_ref, out_ref, sqo_ref, part, mid, got1, got2, sq1, sqm, sq2,
    send1, recv1, send2, recv2, sq_send, sq_recv,
):
    pieces, width = part.shape[0], part.shape[-1]
    rows = x_ref.shape[3]
    y, z = wide_place()
    names = (("y", "z"), ("z", "y"))
    spots = ((y, z), (z, y))
    greet([ring_devices(axis, by) for axis in ("y", "z") for by in (1, 2, 3)])
    squares = Copies(sq_send, sq_recv)
    for by in (1, 2, 3):
        squares.start(by - 1, sq_ref.at[turn(y, by)], sq1.at[by - 1], ring_devices("y", by))

    def product(half, chunk, piece):
        block = x_ref[chunk, :, 0] if half == 0 else x_ref[:, chunk, 1]
        block = block.reshape(SIDE * rows, block.shape[-1])
        columns = pl.ds(pl.multiple_of(piece * width, 128), width)
        got = jnp.dot(block, w_ref[:, columns], preferred_element_type=F32)
        return got.reshape(SIDE, rows, width)

    def copy1(piece, half, kind, way, src):
        return pltpu.make_async_remote_copy(
            src_ref=src,
            dst_ref=got1.at[piece, half, kind, way],
            send_sem=send1.at[piece, half, kind, way],
            recv_sem=recv1.at[piece, half, kind, way],
            device_id=ring_devices(names[half][0], 1 if way == 0 else 3),
            device_id_type=MESH,
        )

    def copy2(piece, half, kind, way, src):
        return pltpu.make_async_remote_copy(
            src_ref=src,
            dst_ref=got2.at[piece, half, kind, way],
            send_sem=send2.at[piece, half, kind, way],
            recv_sem=recv2.at[piece, half, kind, way],
            device_id=ring_devices(names[half][1], 1 if way == 0 else 3),
            device_id_type=MESH,
        )

    def await1(piece, half, kind, way):
        ref = got1.at[piece, half, kind, way]
        pltpu.make_async_copy(ref, ref, recv1.at[piece, half, kind, way]).wait()
        return got1[piece, half, kind, way].astype(F32)

    def await2(piece, half, kind, way):
        ref = got2.at[piece, half, kind, way]
        pltpu.make_async_copy(ref, ref, recv2.at[piece, half, kind, way]).wait()
        return got2[piece, half, kind, way].astype(F32)

    lower, upper = pl.ds(0, 2), pl.ds(2, 2)
    low, high = pl.ds(0, rows // 2), pl.ds(rows // 2, rows // 2)

    def first(piece):
        for half in range(2):
            far = turn(spots[half][0], 2)
            part[piece, half, far] = product(half, far, piece).astype(BF)
            copy1(piece, half, 0, 0, part.at[piece, half, far, lower]).start()
            copy1(piece, half, 0, 1, part.at[piece, half, far, upper]).start()
        for half in range(2):
            right, left = turn(spots[half][0], 1), turn(spots[half][0], 3)
            part[piece, half, right] = product(half, right, piece).astype(BF)
            copy1(piece, half, 1, 0, part.at[piece, half, right, upper]).start()
            part[piece, half, left] = product(half, left, piece).astype(BF)
            copy1(piece, half, 1, 1, part.at[piece, half, left, lower]).start()

    def second(piece):
        for half in range(2):
            right, left = turn(spots[half][0], 1), turn(spots[half][0], 3)
            got = await1(piece, half, 0, 0)
            part[piece, half, right, lower] = (part[piece, half, right, lower].astype(F32) + got).astype(BF)
            copy1(piece, half, 2, 0, part.at[piece, half, right, lower]).start()
            got = await1(piece, half, 0, 1)
            part[piece, half, left, upper] = (part[piece, half, left, upper].astype(F32) + got).astype(BF)
            copy1(piece, half, 2, 1, part.at[piece, half, left, upper]).start()

    def third(piece):
        for half in range(2):
            own = product(half, spots[half][0], piece)
            mid[piece, half, lower] = (
                own[:2] + await1(piece, half, 1, 1) + await1(piece, half, 2, 0)
            ).astype(BF)
            mid[piece, half, upper] = (
                own[2:] + await1(piece, half, 1, 0) + await1(piece, half, 2, 1)
            ).astype(BF)
            far, right, left = (turn(spots[half][1], by) for by in (2, 1, 3))
            copy2(piece, half, 0, 0, mid.at[piece, half, far, low]).start()
            copy2(piece, half, 0, 1, mid.at[piece, half, far, high]).start()
            copy2(piece, half, 1, 0, mid.at[piece, half, right, high]).start()
            copy2(piece, half, 1, 1, mid.at[piece, half, left, low]).start()

    def fourth(piece):
        for half in range(2):
            right, left = turn(spots[half][1], 1), turn(spots[half][1], 3)
            got = await2(piece, half, 0, 0)
            mid[piece, half, right, low] = (mid[piece, half, right, low].astype(F32) + got).astype(BF)
            copy2(piece, half, 2, 0, mid.at[piece, half, right, low]).start()
            got = await2(piece, half, 0, 1)
            mid[piece, half, left, high] = (mid[piece, half, left, high].astype(F32) + got).astype(BF)
            copy2(piece, half, 2, 1, mid.at[piece, half, left, high]).start()

    def fifth(piece):
        columns = pl.ds(pl.multiple_of(piece * width, 128), width)
        for half in range(2):
            own = spots[half][1]
            out_ref[half, low, columns] = (
                mid[piece, half, own, low].astype(F32) + await2(piece, half, 1, 1) + await2(piece, half, 2, 0)
            )
            out_ref[half, high, columns] = (
                mid[piece, half, own, high].astype(F32) + await2(piece, half, 1, 0) + await2(piece, half, 2, 1)
            )

    stages = (first, second, third, fourth, fifth)

    def step(t, carry):
        for lag, stage in enumerate(stages):
            piece = t - lag

            @pl.when((piece >= 0) & (piece < pieces))
            def _():
                stage(jnp.clip(piece, 0, pieces - 1))

        return carry

    lax.fori_loop(0, pieces + len(stages) - 1, step, 0)

    for by in (1, 2, 3):
        squares.arrived(by - 1, sq1.at[by - 1])
    sqm[...] = sq_ref[y] + sq1[0] + sq1[1] + sq1[2]
    for by in (1, 2, 3):
        squares.start(2 + by, sqm.at[turn(z, by)], sq2.at[by - 1], ring_devices("z", by))
    for by in (1, 2, 3):
        squares.arrived(2 + by, sq2.at[by - 1])
    sqo_ref[...] = sqm[z] + sq2[0] + sq2[1] + sq2[2]
    squares.sent()

    def drain(piece, carry):
        for half in range(2):
            for kind in range(3):
                for way in range(2):
                    copy1(piece, half, kind, way, part.at[piece, half, 0, lower]).wait_send()
                    copy2(piece, half, kind, way, mid.at[piece, half, 0, low]).wait_send()
        return carry

    lax.fori_loop(0, pieces, drain, 0)


def matmul_sum(x, w, sq, pieces, collective_id):
    tokens, depth = x.shape
    cols = w.shape[1]
    width = cols // pieces
    rows = tokens // (2 * SIDE * SIDE)
    blocks = jnp.pad(sq.reshape(SIDE, SIDE, 1, 2 * rows), ((0, 0), (0, 0), (0, 0), (0, 128 - 2 * rows)))
    blocks = jnp.broadcast_to(blocks, (SIDE, SIDE, 8, 128))
    out, sq_out = pl.pallas_call(
        matmul_sum_kernel,
        out_shape=(
            jax.ShapeDtypeStruct((2, rows, cols), F32),
            jax.ShapeDtypeStruct((8, 128), F32),
        ),
        in_specs=[VM, VM, VM],
        out_specs=(VM, VM),
        scratch_shapes=[
            pltpu.VMEM((pieces, 2, SIDE, SIDE, rows, width), BF),
            pltpu.VMEM((pieces, 2, SIDE, rows, width), BF),
            pltpu.VMEM((pieces, 2, 3, 2, 2, rows, width), BF),
            pltpu.VMEM((pieces, 2, 3, 2, rows // 2, width), BF),
            pltpu.VMEM((3, SIDE, 8, 128), F32),
            pltpu.VMEM((SIDE, 8, 128), F32),
            pltpu.VMEM((3, 8, 128), F32),
            pltpu.SemaphoreType.DMA((pieces, 2, 3, 2)),
            pltpu.SemaphoreType.DMA((pieces, 2, 3, 2)),
            pltpu.SemaphoreType.DMA((pieces, 2, 3, 2)),
            pltpu.SemaphoreType.DMA((pieces, 2, 3, 2)),
            pltpu.SemaphoreType.DMA((6,)),
            pltpu.SemaphoreType.DMA((6,)),
        ],
        compiler_params=pltpu.CompilerParams(
            collective_id=collective_id, has_side_effects=True, vmem_limit_bytes=VMEM_LIMIT
        ),
        name=f"matmul_sum_{collective_id}",
    )(x.reshape(SIDE, SIDE, 2, rows, depth), w, blocks)
    return out.reshape(2 * rows, cols), sq_out[0, : 2 * rows]


def gate_up_kernel(
    x_ref, w_ref, sq_ref, out_ref, part, mid, hid, got1, got2, sq1, sqm, sq2, inv,
    send1, recv1, send2, recv2, send3, recv3, send4, recv4, own_sem, sq_send, sq_recv,
):
    pieces, width = part.shape[0], part.shape[-1]
    units = out_ref.shape[-1]
    wide = width // 2
    rows = x_ref.shape[3]
    y, z = wide_place()
    names = (("y", "z"), ("z", "y"))
    spots = ((y, z), (z, y))
    greet(wide_lines())
    squares = Copies(sq_send, sq_recv)
    for by in (1, 2, 3):
        squares.start(by - 1, sq_ref.at[turn(y, by)], sq1.at[by - 1], ring_devices("y", by))

    lower, upper = pl.ds(0, 2), pl.ds(2, 2)
    low, high = pl.ds(0, rows // 2), pl.ds(rows // 2, rows // 2)

    def product(half, chunk, piece):
        block = x_ref[chunk, :, 0] if half == 0 else x_ref[:, chunk, 1]
        block = block.reshape(SIDE * rows, block.shape[-1])
        at = pl.multiple_of(piece * wide, 128)
        gate = jnp.dot(block, w_ref[:, pl.ds(at, wide)], preferred_element_type=F32)
        up = jnp.dot(block, w_ref[:, pl.ds(pl.multiple_of(units + at, 128), wide)], preferred_element_type=F32)
        return jnp.concatenate([gate, up], axis=1).reshape(SIDE, rows, width)

    def remote(src, dst, send, recv, axis, way):
        return pltpu.make_async_remote_copy(
            src_ref=src,
            dst_ref=dst,
            send_sem=send,
            recv_sem=recv,
            device_id=ring_devices(axis, 1 if way == 0 else 3),
            device_id_type=MESH,
        )

    def copy1(piece, half, kind, way, src):
        spot = (piece, half, kind, way)
        return remote(src, got1.at[spot], send1.at[spot], recv1.at[spot], names[half][0], way)

    def copy2(piece, half, kind, way, src):
        spot = (piece, half, kind, way)
        return remote(src, got2.at[spot], send2.at[spot], recv2.at[spot], names[half][1], way)

    def landed(ref, sem):
        pltpu.make_async_copy(ref, ref, sem).wait()

    def await1(piece, half, kind, way):
        landed(got1.at[piece, half, kind, way], recv1.at[piece, half, kind, way])
        return got1[piece, half, kind, way].astype(F32)

    def await2(piece, half, kind, way):
        landed(got2.at[piece, half, kind, way], recv2.at[piece, half, kind, way])
        return got2[piece, half, kind, way].astype(F32)

    def place(piece, half, first, second, part_rows):
        columns = pl.ds(pl.multiple_of(piece * wide, 128), wide)
        if half == 0:
            return out_ref.at[first, second, 0, part_rows, columns]
        return out_ref.at[second, first, 1, part_rows, columns]

    whole = pl.ds(0, rows)

    def copy3(piece, half, kind, way, src, dst):
        return remote(src, dst, send3.at[piece, half, kind, way], recv3.at[piece, half, kind, way], names[half][0], way)

    def copy4(piece, half, block, kind, way, src, dst):
        spot = (piece, half, block, kind, way)
        return remote(src, dst, send4.at[spot], recv4.at[spot], names[half][1], way)

    def send4_whole(piece, half, block, src):
        dst = place(piece, half, turn(spots[half][0], block), spots[half][1], whole)
        for way in range(2):
            copy4(piece, half, block, 0, way, src, dst).start()

    def relay4(piece, half, block):
        first = turn(spots[half][0], block)
        for way, by, part_rows in ((0, 3, low), (1, 1, high)):
            second = turn(spots[half][1], by)
            landed(place(piece, half, first, second, whole), recv4.at[piece, half, block, 0, way])
            came = place(piece, half, first, second, part_rows)
            copy4(piece, half, block, 1, way, came, came).start()

    def stage1(piece):
        for half in range(2):
            far = turn(spots[half][0], 2)
            part[piece, half, far] = product(half, far, piece).astype(BF)
            copy1(piece, half, 0, 0, part.at[piece, half, far, lower]).start()
            copy1(piece, half, 0, 1, part.at[piece, half, far, upper]).start()
        for half in range(2):
            right, left = turn(spots[half][0], 1), turn(spots[half][0], 3)
            part[piece, half, right] = product(half, right, piece).astype(BF)
            copy1(piece, half, 1, 0, part.at[piece, half, right, upper]).start()
            part[piece, half, left] = product(half, left, piece).astype(BF)
            copy1(piece, half, 1, 1, part.at[piece, half, left, lower]).start()

    def stage2(piece):
        for half in range(2):
            right, left = turn(spots[half][0], 1), turn(spots[half][0], 3)
            got = await1(piece, half, 0, 0)
            part[piece, half, right, lower] = (part[piece, half, right, lower].astype(F32) + got).astype(BF)
            copy1(piece, half, 2, 0, part.at[piece, half, right, lower]).start()
            got = await1(piece, half, 0, 1)
            part[piece, half, left, upper] = (part[piece, half, left, upper].astype(F32) + got).astype(BF)
            copy1(piece, half, 2, 1, part.at[piece, half, left, upper]).start()

    def stage3(piece):
        for half in range(2):
            own = product(half, spots[half][0], piece)
            mid[piece, half, lower] = (
                own[:2] + await1(piece, half, 1, 1) + await1(piece, half, 2, 0)
            ).astype(BF)
            mid[piece, half, upper] = (
                own[2:] + await1(piece, half, 1, 0) + await1(piece, half, 2, 1)
            ).astype(BF)
            far, right, left = (turn(spots[half][1], by) for by in (2, 1, 3))
            copy2(piece, half, 0, 0, mid.at[piece, half, far, low]).start()
            copy2(piece, half, 0, 1, mid.at[piece, half, far, high]).start()
            copy2(piece, half, 1, 0, mid.at[piece, half, right, high]).start()
            copy2(piece, half, 1, 1, mid.at[piece, half, left, low]).start()

    def stage4(piece):
        for half in range(2):
            right, left = turn(spots[half][1], 1), turn(spots[half][1], 3)
            got = await2(piece, half, 0, 0)
            mid[piece, half, right, low] = (mid[piece, half, right, low].astype(F32) + got).astype(BF)
            copy2(piece, half, 2, 0, mid.at[piece, half, right, low]).start()
            got = await2(piece, half, 0, 1)
            mid[piece, half, left, high] = (mid[piece, half, left, high].astype(F32) + got).astype(BF)
            copy2(piece, half, 2, 1, mid.at[piece, half, left, high]).start()

    def activate(sums, factor):
        sums = jnp.where(factor > 0, sums * factor, 0.0)
        gate, up = sums[:, :wide], sums[:, wide:]
        return (gate / (1.0 + jnp.exp(-gate)) * up).astype(BF)

    def stage5(piece):
        for half in range(2):
            own = spots[half][1]
            hid[piece, half, low] = activate(
                mid[piece, half, own, low].astype(F32) + await2(piece, half, 1, 1) + await2(piece, half, 2, 0),
                inv[half, low][:, :1],
            )
            hid[piece, half, high] = activate(
                mid[piece, half, own, high].astype(F32) + await2(piece, half, 1, 0) + await2(piece, half, 2, 1),
                inv[half, high][:, :1],
            )
            mine = hid.at[piece, half]
            dst = place(piece, half, *spots[half], whole)
            pltpu.make_async_copy(mine, dst, own_sem.at[piece, half]).start()
            for way in range(2):
                copy3(piece, half, 0, way, mine, dst).start()
            send4_whole(piece, half, 0, mine)

    def stage6(piece):
        for half in range(2):
            for way, by, part_rows in ((0, 3, low), (1, 1, high)):
                first = turn(spots[half][0], by)
                landed(place(piece, half, first, spots[half][1], whole), recv3.at[piece, half, 0, way])
                came = place(piece, half, first, spots[half][1], part_rows)
                copy3(piece, half, 1, way, came, came).start()
                send4_whole(piece, half, by, place(piece, half, first, spots[half][1], whole))
        for half in range(2):
            relay4(piece, half, 0)

    def stage7(piece):
        for half in range(2):
            far = turn(spots[half][0], 2)
            landed(place(piece, half, far, spots[half][1], low), recv3.at[piece, half, 1, 0])
            landed(place(piece, half, far, spots[half][1], high), recv3.at[piece, half, 1, 1])
            send4_whole(piece, half, 2, place(piece, half, far, spots[half][1], whole))
        for half in range(2):
            relay4(piece, half, 3)
            relay4(piece, half, 1)

    def stage8(piece):
        for half in range(2):
            relay4(piece, half, 2)

    def stage9(piece):
        for half in range(2):
            for block in range(4):
                first, second = turn(spots[half][0], block), turn(spots[half][1], 2)
                landed(place(piece, half, first, second, low), recv4.at[piece, half, block, 1, 0])
                landed(place(piece, half, first, second, high), recv4.at[piece, half, block, 1, 1])
            mine = place(piece, half, *spots[half], whole)
            landed(mine, own_sem.at[piece, half])
            for way in range(2):
                for kind in range(3):
                    copy1(piece, half, kind, way, part.at[piece, half, 0, lower]).wait_send()
                    copy2(piece, half, kind, way, mid.at[piece, half, 0, low]).wait_send()
                for kind, part_rows in ((0, whole), (1, low)):
                    ref = place(piece, half, *spots[half], part_rows)
                    copy3(piece, half, kind, way, ref, ref).wait_send()
                    for block in range(4):
                        copy4(piece, half, block, kind, way, ref, ref).wait_send()

    stages = (stage1, stage2, stage3, stage4, stage5, stage6, stage7, stage8, stage9)

    def step(t, carry):
        for lag, stage in enumerate(stages):
            piece = t - lag

            @pl.when((piece >= 0) & (piece < pieces))
            def _():
                stage(jnp.clip(piece, 0, pieces - 1))

        return carry

    lax.fori_loop(0, 3, step, 0)

    for by in (1, 2, 3):
        squares.arrived(by - 1, sq1.at[by - 1])
    sqm[...] = sq_ref[y] + sq1[0] + sq1[1] + sq1[2]
    for by in (1, 2, 3):
        squares.start(2 + by, sqm.at[turn(z, by)], sq2.at[by - 1], ring_devices("z", by))
    lax.fori_loop(3, 4, step, 0)
    for by in (1, 2, 3):
        squares.arrived(2 + by, sq2.at[by - 1])
    total = (sqm[z] + sq2[0] + sq2[1] + sq2[2])[:1]
    factor = lax.rsqrt(total / D + epsilon)
    token = lax.broadcasted_iota(jnp.int32, (2 * rows, 128), 0)
    lane = lax.broadcasted_iota(jnp.int32, (2 * rows, 128), 1)
    column = jnp.sum(jnp.where(token == lane, factor, 0.0), axis=1, keepdims=True)
    inv[...] = jnp.broadcast_to(column, (2 * rows, 128)).reshape(2, rows, 128)
    lax.fori_loop(4, pieces + len(stages) - 1, step, 0)
    squares.sent()


def token_blocks(sq, rows):
    blocks = jnp.pad(sq.reshape(SIDE, SIDE, 1, 2 * rows), ((0, 0), (0, 0), (0, 0), (0, 128 - 2 * rows)))
    return jnp.broadcast_to(blocks, (SIDE, SIDE, 8, 128))


def gate_up(x, w, sq, pieces, collective_id):
    tokens, depth = x.shape
    units = w.shape[1] // 2
    width = 2 * units // pieces
    rows = tokens // (2 * SIDE * SIDE)
    dma = pltpu.SemaphoreType.DMA
    return pl.pallas_call(
        gate_up_kernel,
        out_shape=jax.ShapeDtypeStruct((SIDE, SIDE, 2, rows, units), BF),
        in_specs=[VM, VM, VM],
        out_specs=VM,
        scratch_shapes=[
            pltpu.VMEM((pieces, 2, SIDE, SIDE, rows, width), BF),
            pltpu.VMEM((pieces, 2, SIDE, rows, width), BF),
            pltpu.VMEM((pieces, 2, rows, width // 2), BF),
            pltpu.VMEM((pieces, 2, 3, 2, 2, rows, width), BF),
            pltpu.VMEM((pieces, 2, 3, 2, rows // 2, width), BF),
            pltpu.VMEM((3, SIDE, 8, 128), F32),
            pltpu.VMEM((SIDE, 8, 128), F32),
            pltpu.VMEM((3, 8, 128), F32),
            pltpu.VMEM((2, rows, 128), F32),
            dma((pieces, 2, 3, 2)),
            dma((pieces, 2, 3, 2)),
            dma((pieces, 2, 3, 2)),
            dma((pieces, 2, 3, 2)),
            dma((pieces, 2, 2, 2)),
            dma((pieces, 2, 2, 2)),
            dma((pieces, 2, 4, 2, 2)),
            dma((pieces, 2, 4, 2, 2)),
            dma((pieces, 2)),
            dma((6,)),
            dma((6,)),
        ],
        compiler_params=pltpu.CompilerParams(
            collective_id=collective_id, has_side_effects=True, vmem_limit_bytes=VMEM_LIMIT
        ),
        name="gate_up",
    )(x.reshape(SIDE, SIDE, 2, rows, depth), w, token_blocks(sq, rows))


CHUNK = 2


def attend_kernel(
    lengths_ref, q_ref, cache_ref, own_ref, out_ref, sums_ref, span_ref, local_sem, send_sem, recv_sem
):
    scale = HDIM ** (-0.5)
    rows = q_ref.shape[1]
    per = own_ref.shape[1]
    block = cache_ref.shape[2] * CHUNK
    spot = lax.axis_index("wide")
    copies = Copies(send_sem, recv_sem)
    greet(wide_lines())
    gather = gather_direct_steps(own_ref, span_ref, local_sem, copies)
    next(gather)
    queries = [q_ref[request] for request in range(R)]

    def absorb(running, q, keys, values, allowed):
        peak, weight_sum, gathered = running
        scores = lax.dot_general(q, keys, (((1,), (1,)), ((), ())), preferred_element_type=F32) * scale
        scores = jnp.where(allowed(scores.shape), scores, floor_score)
        new_peak = jnp.maximum(peak, jnp.max(scores, axis=1, keepdims=True))
        weights = jnp.exp(scores - new_peak)
        factor = jnp.exp(peak - new_peak)
        weight_sum = weight_sum * factor + jnp.sum(weights, axis=1, keepdims=True)
        gathered = gathered * factor + jnp.dot(weights.astype(BF), values, preferred_element_type=F32)
        return new_peak, weight_sum, gathered

    def own_keys(shape):
        key = lax.broadcasted_iota(jnp.int32, shape, 1)
        row = lax.broadcasted_iota(jnp.int32, shape, 0)
        return key <= spot * per + lax.rem(row, per)

    running = [
        (
            jnp.full((rows, 1), floor_score, F32),
            jnp.zeros((rows, 1), F32),
            jnp.zeros((rows, HDIM), F32),
        )
        for _ in range(R)
    ]
    for index in range(cache_ref.shape[0] // CHUNK):
        for request in range(R):
            pair = cache_ref[pl.ds(index * CHUNK, CHUNK), request].reshape(block, 2 * HDIM)
            running[request] = absorb(
                running[request],
                queries[request],
                pair[:, :HDIM],
                pair[:, HDIM:],
                lambda shape: index * block + lax.broadcasted_iota(jnp.int32, shape, 1) < lengths_ref[request],
            )
        if index >= 2:
            next(gather, None)
    interleave(gather)
    for request in range(R):
        span = span_ref[:, :, request].reshape(SIDE * SIDE * per, 2 * HDIM)
        peak, weight_sum, gathered = absorb(
            running[request], queries[request], span[:, :HDIM], span[:, HDIM:], own_keys
        )
        out_ref[request] = (gathered / weight_sum).astype(BF)
        sums_ref[request] = jnp.broadcast_to(peak + jnp.log(weight_sum), (rows, HDIM))
    copies.sent()


def attend(lengths, queries, cache, own, collective_id):
    return pl.pallas_call(
        attend_kernel,
        out_shape=(
            jax.ShapeDtypeStruct(queries.shape, BF),
            jax.ShapeDtypeStruct(queries.shape, F32),
        ),
        in_specs=[SM, VM, VM, VM],
        out_specs=(VM, VM),
        scratch_shapes=[
            pltpu.VMEM((SIDE, SIDE) + own.shape, BF),
            pltpu.SemaphoreType.DMA,
            pltpu.SemaphoreType.DMA((DIRECT_COPIES,)),
            pltpu.SemaphoreType.DMA((DIRECT_COPIES,)),
        ],
        compiler_params=pltpu.CompilerParams(
            collective_id=collective_id, has_side_effects=True, vmem_limit_bytes=VMEM_LIMIT
        ),
        name="attend",
    )(lengths, queries, cache, own)


def token_angles(lengths, offsets, first_token, row_count, dim_size):
    token_ids = first_token + jnp.arange(row_count, dtype=jnp.int32)
    request_ids = token_ids % R
    start_pos = offsets + lengths
    matches = request_ids[:, None] == jnp.arange(start_pos.shape[0], dtype=jnp.int32)[None, :]
    chosen = jnp.sum(jnp.where(matches, start_pos[None, :], 0), axis=1)
    position = (chosen + token_ids // R).astype(jnp.float32)
    inverse = rope_base ** (-(jnp.arange(dim_size // 2, dtype=jnp.float32) * 2.0) / dim_size)
    return position[:, None] * inverse[None, :]


def rotate(values, angles):
    half_dim = values.shape[-1] // 2
    first_half = values[..., :half_dim]
    second_half = values[..., half_dim:]
    cosine = jnp.cos(angles)[:, None, :]
    sine_part = jnp.sin(angles)[:, None, :]
    return jnp.concatenate(
        [
            first_half * cosine - second_half * sine_part,
            second_half * cosine + first_half * sine_part,
        ],
        axis=-1,
    )


def to_send(flipped, gain):
    widened = flipped.astype(F32)
    squares = jnp.sum(widened * widened, axis=0, keepdims=True)
    high = lax.reduce_precision(squares, 8, 7)
    rest = squares - high
    middle = lax.reduce_precision(rest, 8, 7)
    low = rest - middle
    scaled = widened * gain.astype(F32)[:, None]
    pad = jnp.zeros((5, flipped.shape[1]), F32)
    return jnp.concatenate([scaled, high, middle, low, pad], axis=0).astype(BF)


def unpack(gathered, rows):
    scaled = gathered[:, :rows].reshape(8 * rows, -1).T
    squares = jnp.sum(gathered[:, rows : rows + 3].astype(F32), axis=(0, 1))
    return scaled, squares


def rescale(sums, squares):
    inv_scale = lax.rsqrt(squares / D + epsilon)[:, None]
    return jnp.where(inv_scale > 0, sums * inv_scale, 0.0)


def local(
    hidden_in, attn_gain, w_qkv, cache_kv, lengths, offsets, w_out, mlp_gain, w_gate_up, w_down
):
    all_tokens, features = hidden_in.shape
    per_device = all_tokens // lax.axis_size("wide")
    first_token = lax.axis_index("wide") * per_device
    flipped = hidden_in.T
    positions = cache_kv.shape[1]
    cache = cache_kv.reshape(R, positions, 2 * HDIM)
    gathered, cache_all = gather_both(to_send(flipped, attn_gain), cache, 1)
    scaled, squares = unpack(gathered, features)
    projected, squares = matmul_sum(scaled, w_qkv.reshape(w_qkv.shape[0], -1), squares, 3, 2)
    projected = rescale(projected, squares).reshape(per_device, GROUP + 2, HDIM)
    angles = token_angles(lengths, offsets, first_token, per_device, HDIM)
    rotated = rotate(projected[:, : GROUP + 1], angles).astype(BF)
    new_keys, new_values = rotated[:, GROUP], projected[:, GROUP + 1].astype(BF)
    new_cache = jnp.stack([new_keys, new_values], axis=1)[:, None]
    per_request = per_device // R
    span = jnp.concatenate([new_keys, new_values], axis=1).reshape(per_request, R, 2 * HDIM)
    queries = rotated[:, :GROUP].reshape(per_request, R, GROUP, HDIM).transpose(1, 2, 0, 3)
    attended, sums = attend(
        lengths,
        queries.reshape(R, GROUP * per_request, HDIM),
        cache_all.reshape(SIDE * SIDE, R, positions, 2 * HDIM),
        span.transpose(1, 0, 2),
        3,
    )
    attended = attended.reshape(R, GROUP, per_request, HDIM).transpose(2, 0, 1, 3).reshape(2, -1, GROUP * HDIM)
    softmax_sums = sums[:, :, 0].reshape(R, GROUP, per_request).transpose(2, 0, 1).reshape(per_device, GROUP)
    attended_all = gather_wide(attended, 4).reshape(all_tokens, -1)
    out_terms = lax.dot_general(
        w_out, attended_all, (((0,), (1,)), ((), ())), preferred_element_type=F32
    ).astype(BF)
    summed = sum_narrow(out_terms.reshape(4, 2, features, all_tokens), 5)
    residual = (flipped.astype(F32) + summed).astype(BF)
    scaled, squares = unpack(gather_narrow(to_send(residual, mlp_gain), 6), features)
    units = w_gate_up.shape[2]
    hidden_all = gate_up(scaled, w_gate_up.reshape(w_gate_up.shape[0], -1), squares, 4, 7).reshape(all_tokens, units)
    down_terms = lax.dot_general(
        w_down, hidden_all, (((0,), (1,)), ((), ())), preferred_element_type=F32
    ).astype(BF)
    summed = sum_narrow(down_terms.reshape(4, 2, features, all_tokens), 9)
    hidden_out = (residual.astype(F32) + summed).astype(BF).T
    return (hidden_out, softmax_sums, new_cache)


def solution(mesh):
    return jax.shard_map(
        local,
        mesh=mesh,
        in_specs=(
            P(None, ("wide", "narrow")),
            P(("wide", "narrow")),
            P("wide", "narrow", None),
            P(None, "wide", "narrow", None, None),
            P(),
            P(),
            P("narrow", "wide"),
            P(("wide", "narrow")),
            P("wide", None, "narrow"),
            P("narrow", "wide"),
        ),
        out_specs=(
            P(None, ("wide", "narrow")),
            P("wide", "narrow"),
            P("wide", "narrow", None, None),
        ),
        check_vma=False,
    )
```

```python
import functools

import jax
import jax.numpy as jnp
from jax import lax
from jax.experimental import pallas as pl
from jax.experimental.pallas import tpu as pltpu
from jax.sharding import PartitionSpec as P

D = 7168
HDIM = 128
R = 2
GROUP = 7
SIDE = 4

epsilon = 1e-05
rope_base = 5000000.0
floor_score = -1e30

MESH = pl.DeviceIdType.MESH
BF = jnp.bfloat16
F32 = jnp.float32
VM = pl.BlockSpec(memory_space=pltpu.VMEM)
SM = pl.BlockSpec(memory_space=pltpu.SMEM)
VMEM_LIMIT = 60 * 1024 * 1024


def wide_place():
    w = lax.axis_index("wide")
    return lax.div(w, SIDE), lax.rem(w, SIDE)


def turn(pos, by):
    return lax.rem(pos + by, SIDE)


def ring_devices(axis, by):
    if axis == "x":
        n = lax.axis_index("narrow")
        return {"narrow": turn(lax.div(n, 2), by) * 2 + lax.rem(n, 2)}
    y, z = wide_place()
    if axis == "y":
        return {"wide": turn(y, by) * SIDE + z}
    return {"wide": y * SIDE + turn(z, by)}


def partner_device():
    n = lax.axis_index("narrow")
    return {"narrow": lax.div(n, 2) * 2 + 1 - lax.rem(n, 2)}


def greet(devices):
    barrier = pltpu.get_barrier_semaphore()
    for device in devices:
        pl.semaphore_signal(barrier, inc=1, device_id=device, device_id_type=MESH)
    pl.semaphore_wait(barrier, len(devices))


class Copies:
    def __init__(self, send_sem, recv_sem):
        self.send_sem, self.recv_sem, self.used, self.made = send_sem, recv_sem, 0, []

    def slot(self):
        self.used += 1
        return self.used - 1

    def start(self, slot, src, dst, device):
        copy = pltpu.make_async_remote_copy(
            src_ref=src,
            dst_ref=dst,
            send_sem=self.send_sem.at[slot],
            recv_sem=self.recv_sem.at[slot],
            device_id=device,
            device_id_type=MESH,
        )
        copy.start()
        self.made.append(copy)

    def arrived(self, slot, dst):
        pltpu.make_async_copy(dst, dst, self.recv_sem.at[slot]).wait()

    def sent(self):
        for copy in self.made:
            copy.wait_send()


def interleave(*parts):
    live = list(parts)
    while live:
        for part in list(live):
            try:
                next(part)
            except StopIteration:
                live.remove(part)


def gather_wide_steps(x_ref, out_ref, local_sem, copies):
    y, z = wide_place()
    depth = x_ref.shape[1] // 2
    lower, upper = pl.ds(0, depth), pl.ds(depth, depth)

    def place(half, first, second):
        if half == 0:
            return out_ref.at[first, second, 0]
        return out_ref.at[second, first, 1]

    names = (("y", "z"), ("z", "y"))
    spots = ((y, z), (z, y))
    own = pltpu.make_async_copy(x_ref, out_ref.at[y, z], local_sem)
    own.start()
    hop1 = [[copies.slot() for _ in range(4)] for _ in range(2)]
    hop2 = [[[copies.slot() for _ in range(4)] for _ in range(4)] for _ in range(2)]

    def send2(half, block, src):
        first = turn(spots[half][0], block)
        target = place(half, first, spots[half][1])
        for way, by in ((0, 1), (1, 3)):
            copies.start(hop2[half][block][way], src, target, ring_devices(names[half][1], by))

    def relay2(half, block):
        first = turn(spots[half][0], block)
        for way, by, part in ((0, 1, lower), (1, 3, upper)):
            came = place(half, first, turn(spots[half][1], 4 - by))
            copies.arrived(hop2[half][block][way], came)
            copies.start(
                hop2[half][block][2 + way], came.at[part], came.at[part], ring_devices(names[half][1], by)
            )

    for half in range(2):
        target = place(half, *spots[half])
        for way, by in ((0, 1), (1, 3)):
            copies.start(hop1[half][way], x_ref.at[half], target, ring_devices(names[half][0], by))
        send2(half, 0, x_ref.at[half])
    yield
    for half in range(2):
        for way, by, part in ((0, 1, lower), (1, 3, upper)):
            came = place(half, turn(spots[half][0], 4 - by), spots[half][1])
            copies.arrived(hop1[half][way], came)
            copies.start(hop1[half][2 + way], came.at[part], came.at[part], ring_devices(names[half][0], by))
            send2(half, 4 - by, came)
        yield
    for half in range(2):
        relay2(half, 0)
        yield
    for half in range(2):
        far = place(half, turn(spots[half][0], 2), spots[half][1])
        copies.arrived(hop1[half][2], far.at[lower])
        copies.arrived(hop1[half][3], far.at[upper])
        send2(half, 2, far)
        yield
    for block in (3, 1, 2):
        for half in range(2):
            relay2(half, block)
            yield
    for half in range(2):
        for block in (0, 3, 1, 2):
            far = place(half, turn(spots[half][0], block), turn(spots[half][1], 2))
            copies.arrived(hop2[half][block][2], far.at[lower])
            copies.arrived(hop2[half][block][3], far.at[upper])
    own.wait()


WIDE_COPIES = 40


def gather_direct_steps(x_ref, out_ref, local_sem, copies):
    y, z = wide_place()
    names = (("y", "z"), ("z", "y"))
    spots = ((y, z), (z, y))

    def place(half, first, second):
        if half == 0:
            return out_ref.at[first, second, 0]
        return out_ref.at[second, first, 1]

    own = pltpu.make_async_copy(x_ref, out_ref.at[y, z], local_sem)
    own.start()
    hop1 = [[copies.slot() for _ in range(3)] for _ in range(2)]
    hop2 = [[[copies.slot() for _ in range(3)] for _ in range(4)] for _ in range(2)]

    def send2(half, block, src):
        target = place(half, turn(spots[half][0], block), spots[half][1])
        for by in (2, 1, 3):
            copies.start(hop2[half][block][by - 1], src, target, ring_devices(names[half][1], by))

    for half in range(2):
        target = place(half, *spots[half])
        for by in (2, 1, 3):
            copies.start(hop1[half][by - 1], x_ref.at[half], target, ring_devices(names[half][0], by))
    for half in range(2):
        send2(half, 0, x_ref.at[half])
    yield
    for by in (1, 3, 2):
        for half in range(2):
            came = place(half, turn(spots[half][0], 4 - by), spots[half][1])
            copies.arrived(hop1[half][by - 1], came)
            send2(half, 4 - by, came)
        yield
    for block in range(4):
        for half in range(2):
            for by in (1, 3, 2):
                came = place(half, turn(spots[half][0], block), turn(spots[half][1], 4 - by))
                copies.arrived(hop2[half][block][by - 1], came)
    own.wait()


DIRECT_COPIES = 30


def wide_lines():
    return [ring_devices(axis, by) for axis in ("y", "z") for by in (1, 2, 3)]


def wide_neighbours():
    return [ring_devices(axis, by) for axis in ("y", "z") for by in (1, 3)]


def gather_narrow_steps(x_ref, out_ref, local_sem, copies):
    n = lax.axis_index("narrow")
    x, core = lax.div(n, 2), lax.rem(n, 2)
    depth = x_ref.shape[0] // 2
    lower, upper = pl.ds(0, depth), pl.ds(depth, depth)
    own = pltpu.make_async_copy(x_ref, out_ref.at[n], local_sem)
    own.start()
    slots = [copies.slot() for _ in range(8)]
    for way, by in ((0, 1), (1, 3)):
        copies.start(slots[way], x_ref, out_ref.at[n], ring_devices("x", by))
    copies.start(slots[4], x_ref, out_ref.at[n], partner_device())
    yield
    for way, by, part in ((0, 1, lower), (1, 3, upper)):
        came = out_ref.at[turn(x, 4 - by) * 2 + core]
        copies.arrived(slots[way], came)
        copies.start(slots[2 + way], came.at[part], came.at[part], ring_devices("x", by))
        copies.start(slots[5 + way], came, came, partner_device())
    yield
    far = out_ref.at[turn(x, 2) * 2 + core]
    copies.arrived(slots[2], far.at[lower])
    copies.arrived(slots[3], far.at[upper])
    copies.start(slots[7], far, far, partner_device())
    yield
    for slot, by in ((4, 0), (5, 3), (6, 1), (7, 2)):
        copies.arrived(slots[slot], out_ref.at[turn(x, by) * 2 + 1 - core])
    own.wait()


NARROW_COPIES = 8


def narrow_neighbours():
    return [ring_devices("x", 1), ring_devices("x", 3), partner_device()]


def gather_both_kernel(x_ref, cache_ref, xo_ref, cacheo_ref, local_sem, send_n, recv_n, send_w, recv_w):
    near, far = Copies(send_n, recv_n), Copies(send_w, recv_w)
    greet(narrow_neighbours() + wide_neighbours())
    interleave(
        gather_narrow_steps(x_ref, xo_ref, local_sem.at[0], near),
        gather_wide_steps(cache_ref, cacheo_ref, local_sem.at[1], far),
    )
    near.sent()
    far.sent()


def gather_both(x, cache, collective_id):
    return pl.pallas_call(
        gather_both_kernel,
        out_shape=(
            jax.ShapeDtypeStruct((8,) + x.shape, x.dtype),
            jax.ShapeDtypeStruct((SIDE, SIDE) + cache.shape, cache.dtype),
        ),
        in_specs=[VM, VM],
        out_specs=(VM, VM),
        scratch_shapes=[
            pltpu.SemaphoreType.DMA((2,)),
            pltpu.SemaphoreType.DMA((NARROW_COPIES,)),
            pltpu.SemaphoreType.DMA((NARROW_COPIES,)),
            pltpu.SemaphoreType.DMA((WIDE_COPIES,)),
            pltpu.SemaphoreType.DMA((WIDE_COPIES,)),
        ],
        compiler_params=pltpu.CompilerParams(
            collective_id=collective_id, has_side_effects=True, vmem_limit_bytes=VMEM_LIMIT
        ),
        name="gather_both",
    )(x, cache)


SUM_COPIES = 10


def sum_narrow_body(p_ref, acc, mate, total, relay, direct, joined, copies):
    n = lax.axis_index("narrow")
    x, core = lax.div(n, 2), lax.rem(n, 2)
    width = p_ref.shape[3] // 2
    lower, upper = pl.ds(0, width), pl.ds(width, width)
    right, left = ring_devices("x", 1), ring_devices("x", 3)
    order = (2, 1, 3, 0)
    mates = {by: copies.slot() for by in order}
    slots = [copies.slot() for _ in range(6)]
    for by in order:
        copies.start(mates[by], p_ref.at[turn(x, by), 1 - core], mate.at[by], partner_device())

    def pair(by):
        copies.arrived(mates[by], mate.at[by])
        return p_ref[turn(x, by), core].astype(F32) + mate[by].astype(F32)

    total[2] = pair(2).astype(BF)
    copies.start(slots[0], total.at[2, :, lower], relay.at[0], right)
    copies.start(slots[1], total.at[2, :, upper], relay.at[1], left)
    total[1] = pair(1).astype(BF)
    copies.start(slots[2], total.at[1, :, upper], direct.at[0], right)
    total[3] = pair(3).astype(BF)
    copies.start(slots[3], total.at[3, :, lower], direct.at[1], left)
    copies.arrived(slots[0], relay.at[0])
    total[1, :, lower] = (total[1, :, lower].astype(F32) + relay[0].astype(F32)).astype(BF)
    copies.start(slots[4], total.at[1, :, lower], joined.at[0], right)
    copies.arrived(slots[1], relay.at[1])
    total[3, :, upper] = (total[3, :, upper].astype(F32) + relay[1].astype(F32)).astype(BF)
    copies.start(slots[5], total.at[3, :, upper], joined.at[1], left)
    acc[...] = pair(0)
    copies.arrived(slots[2], direct.at[0])
    acc[:, upper] += direct[0].astype(F32)
    copies.arrived(slots[3], direct.at[1])
    acc[:, lower] += direct[1].astype(F32)
    copies.arrived(slots[4], joined.at[0])
    acc[:, lower] += joined[0].astype(F32)
    copies.arrived(slots[5], joined.at[1])
    acc[:, upper] += joined[1].astype(F32)


def sum_scratch(rows, cols):
    piece = pltpu.VMEM((2, rows, cols // 2), BF)
    dma = pltpu.SemaphoreType.DMA
    return [
        pltpu.VMEM((4, 2, rows, cols), BF),
        pltpu.VMEM((rows, cols), F32),
        pltpu.VMEM((4, rows, cols), BF),
        pltpu.VMEM((4, rows, cols), BF),
        piece,
        piece,
        piece,
        dma((SUM_COPIES,)),
        dma((SUM_COPIES,)),
    ]


def split_terms(terms):
    return terms.astype(BF).reshape(4, 2, terms.shape[0] // 8, terms.shape[1])


def out_proj_kernel(
    own_ref, w_ref, x_ref, gain_ref, res_ref, out_ref, all_ref, block, terms, acc, mate, total, relay, direct, joined,
    sum_send, sum_recv, local_sem, wide_send, wide_recv, near_send, near_recv,
):
    rows = x_ref.shape[0]
    wide, sums, near = Copies(wide_send, wide_recv), Copies(sum_send, sum_recv), Copies(near_send, near_recv)
    greet(wide_neighbours() + narrow_neighbours())
    interleave(gather_wide_steps(own_ref, all_ref, local_sem.at[0], wide))
    depth = w_ref.shape[1]
    tokens = x_ref.shape[1] // SIDE
    for group in range(SIDE):
        values = all_ref[group].reshape(tokens, depth)
        got = lax.dot_general(w_ref[...], values, (((1,), (1,)), ((), ())), preferred_element_type=F32)
        terms[:, :, :, pl.ds(group * tokens, tokens)] = split_terms(got)
    sum_narrow_body(terms, acc, mate, total, relay, direct, joined, sums)
    residual = (x_ref[...].astype(F32) + acc[...]).astype(BF)
    res_ref[...] = residual
    widened = residual.astype(F32)
    squares = jnp.sum(widened * widened, axis=0, keepdims=True)
    high = squares.astype(BF).astype(F32)
    rest = squares - high
    middle = rest.astype(BF).astype(F32)
    low = rest - middle
    line = lax.broadcasted_iota(jnp.int32, (8, widened.shape[1]), 0)
    tail = jnp.where(line == 0, high, jnp.where(line == 1, middle, jnp.where(line == 2, low, 0.0)))
    block[...] = jnp.concatenate([widened * gain_ref[:, :1], tail], axis=0).astype(BF)
    interleave(gather_narrow_steps(block, out_ref, local_sem.at[1], near))
    wide.sent()
    sums.sent()
    near.sent()


def out_proj(own, w, x, gain, collective_id):
    rows, tokens = x.shape
    dma = pltpu.SemaphoreType.DMA
    return pl.pallas_call(
        out_proj_kernel,
        out_shape=(
            jax.ShapeDtypeStruct((rows, tokens), BF),
            jax.ShapeDtypeStruct((8, rows + 8, tokens), BF),
        ),
        in_specs=[VM] * 4,
        out_specs=(VM, VM),
        scratch_shapes=[
            pltpu.VMEM((SIDE, SIDE) + own.shape, BF),
            pltpu.VMEM((rows + 8, tokens), BF),
        ]
        + sum_scratch(rows, tokens)
        + [
            dma((2,)),
            dma((WIDE_COPIES,)),
            dma((WIDE_COPIES,)),
            dma((NARROW_COPIES,)),
            dma((NARROW_COPIES,)),
        ],
        compiler_params=pltpu.CompilerParams(
            collective_id=collective_id, has_side_effects=True, vmem_limit_bytes=VMEM_LIMIT
        ),
        name="out_proj",
    )(own, w, x, jnp.broadcast_to(gain.astype(F32)[:, None], (rows, 128)))


def matmul_sum_kernel(
    x_ref, w_ref, sq_ref, out_ref, sqo_ref, part, mid, got1, got2, sq1, sqm, sq2,
    send1, recv1, send2, recv2, sq_send, sq_recv,
):
    pieces, width = part.shape[0], part.shape[-1]
    rows = x_ref.shape[3]
    y, z = wide_place()
    names = (("y", "z"), ("z", "y"))
    spots = ((y, z), (z, y))
    greet([ring_devices(axis, by) for axis in ("y", "z") for by in (1, 2, 3)])
    squares = Copies(sq_send, sq_recv)
    for by in (1, 2, 3):
        squares.start(by - 1, sq_ref.at[turn(y, by)], sq1.at[by - 1], ring_devices("y", by))

    def product(half, chunk, piece):
        block = x_ref[chunk, :, 0] if half == 0 else x_ref[:, chunk, 1]
        block = block.reshape(SIDE * rows, block.shape[-1])
        columns = pl.ds(pl.multiple_of(piece * width, 128), width)
        got = jnp.dot(block, w_ref[:, columns], preferred_element_type=F32)
        return got.reshape(SIDE, rows, width)

    def copy1(piece, half, kind, way, src):
        return pltpu.make_async_remote_copy(
            src_ref=src,
            dst_ref=got1.at[piece, half, kind, way],
            send_sem=send1.at[piece, half, kind, way],
            recv_sem=recv1.at[piece, half, kind, way],
            device_id=ring_devices(names[half][0], 1 if way == 0 else 3),
            device_id_type=MESH,
        )

    def copy2(piece, half, kind, way, src):
        return pltpu.make_async_remote_copy(
            src_ref=src,
            dst_ref=got2.at[piece, half, kind, way],
            send_sem=send2.at[piece, half, kind, way],
            recv_sem=recv2.at[piece, half, kind, way],
            device_id=ring_devices(names[half][1], 1 if way == 0 else 3),
            device_id_type=MESH,
        )

    def await1(piece, half, kind, way):
        ref = got1.at[piece, half, kind, way]
        pltpu.make_async_copy(ref, ref, recv1.at[piece, half, kind, way]).wait()
        return got1[piece, half, kind, way].astype(F32)

    def await2(piece, half, kind, way):
        ref = got2.at[piece, half, kind, way]
        pltpu.make_async_copy(ref, ref, recv2.at[piece, half, kind, way]).wait()
        return got2[piece, half, kind, way].astype(F32)

    lower, upper = pl.ds(0, 2), pl.ds(2, 2)
    low, high = pl.ds(0, rows // 2), pl.ds(rows // 2, rows // 2)

    def first(piece):
        for half in range(2):
            far = turn(spots[half][0], 2)
            part[piece, half, far] = product(half, far, piece).astype(BF)
            copy1(piece, half, 0, 0, part.at[piece, half, far, lower]).start()
            copy1(piece, half, 0, 1, part.at[piece, half, far, upper]).start()
        for half in range(2):
            right, left = turn(spots[half][0], 1), turn(spots[half][0], 3)
            part[piece, half, right] = product(half, right, piece).astype(BF)
            copy1(piece, half, 1, 0, part.at[piece, half, right, upper]).start()
            part[piece, half, left] = product(half, left, piece).astype(BF)
            copy1(piece, half, 1, 1, part.at[piece, half, left, lower]).start()

    def second(piece):
        for half in range(2):
            right, left = turn(spots[half][0], 1), turn(spots[half][0], 3)
            got = await1(piece, half, 0, 0)
            part[piece, half, right, lower] = (part[piece, half, right, lower].astype(F32) + got).astype(BF)
            copy1(piece, half, 2, 0, part.at[piece, half, right, lower]).start()
            got = await1(piece, half, 0, 1)
            part[piece, half, left, upper] = (part[piece, half, left, upper].astype(F32) + got).astype(BF)
            copy1(piece, half, 2, 1, part.at[piece, half, left, upper]).start()

    def third(piece):
        for half in range(2):
            own = product(half, spots[half][0], piece)
            mid[piece, half, lower] = (
                own[:2] + await1(piece, half, 1, 1) + await1(piece, half, 2, 0)
            ).astype(BF)
            mid[piece, half, upper] = (
                own[2:] + await1(piece, half, 1, 0) + await1(piece, half, 2, 1)
            ).astype(BF)
            far, right, left = (turn(spots[half][1], by) for by in (2, 1, 3))
            copy2(piece, half, 0, 0, mid.at[piece, half, far, low]).start()
            copy2(piece, half, 0, 1, mid.at[piece, half, far, high]).start()
            copy2(piece, half, 1, 0, mid.at[piece, half, right, high]).start()
            copy2(piece, half, 1, 1, mid.at[piece, half, left, low]).start()

    def fourth(piece):
        for half in range(2):
            right, left = turn(spots[half][1], 1), turn(spots[half][1], 3)
            got = await2(piece, half, 0, 0)
            mid[piece, half, right, low] = (mid[piece, half, right, low].astype(F32) + got).astype(BF)
            copy2(piece, half, 2, 0, mid.at[piece, half, right, low]).start()
            got = await2(piece, half, 0, 1)
            mid[piece, half, left, high] = (mid[piece, half, left, high].astype(F32) + got).astype(BF)
            copy2(piece, half, 2, 1, mid.at[piece, half, left, high]).start()

    def fifth(piece):
        columns = pl.ds(pl.multiple_of(piece * width, 128), width)
        for half in range(2):
            own = spots[half][1]
            out_ref[half, low, columns] = (
                mid[piece, half, own, low].astype(F32) + await2(piece, half, 1, 1) + await2(piece, half, 2, 0)
            )
            out_ref[half, high, columns] = (
                mid[piece, half, own, high].astype(F32) + await2(piece, half, 1, 0) + await2(piece, half, 2, 1)
            )

    stages = (first, second, third, fourth, fifth)

    def step(t, carry):
        for lag, stage in enumerate(stages):
            piece = t - lag

            @pl.when((piece >= 0) & (piece < pieces))
            def _():
                stage(jnp.clip(piece, 0, pieces - 1))

        return carry

    lax.fori_loop(0, pieces + len(stages) - 1, step, 0)

    for by in (1, 2, 3):
        squares.arrived(by - 1, sq1.at[by - 1])
    sqm[...] = sq_ref[y] + sq1[0] + sq1[1] + sq1[2]
    for by in (1, 2, 3):
        squares.start(2 + by, sqm.at[turn(z, by)], sq2.at[by - 1], ring_devices("z", by))
    for by in (1, 2, 3):
        squares.arrived(2 + by, sq2.at[by - 1])
    sqo_ref[...] = sqm[z] + sq2[0] + sq2[1] + sq2[2]
    squares.sent()

    def drain(piece, carry):
        for half in range(2):
            for kind in range(3):
                for way in range(2):
                    copy1(piece, half, kind, way, part.at[piece, half, 0, lower]).wait_send()
                    copy2(piece, half, kind, way, mid.at[piece, half, 0, low]).wait_send()
        return carry

    lax.fori_loop(0, pieces, drain, 0)


def matmul_sum(x, w, sq, pieces, collective_id):
    tokens, depth = x.shape
    cols = w.shape[1]
    width = cols // pieces
    rows = tokens // (2 * SIDE * SIDE)
    blocks = jnp.pad(sq.reshape(SIDE, SIDE, 1, 2 * rows), ((0, 0), (0, 0), (0, 0), (0, 128 - 2 * rows)))
    blocks = jnp.broadcast_to(blocks, (SIDE, SIDE, 8, 128))
    out, sq_out = pl.pallas_call(
        matmul_sum_kernel,
        out_shape=(
            jax.ShapeDtypeStruct((2, rows, cols), F32),
            jax.ShapeDtypeStruct((8, 128), F32),
        ),
        in_specs=[VM, VM, VM],
        out_specs=(VM, VM),
        scratch_shapes=[
            pltpu.VMEM((pieces, 2, SIDE, SIDE, rows, width), BF),
            pltpu.VMEM((pieces, 2, SIDE, rows, width), BF),
            pltpu.VMEM((pieces, 2, 3, 2, 2, rows, width), BF),
            pltpu.VMEM((pieces, 2, 3, 2, rows // 2, width), BF),
            pltpu.VMEM((3, SIDE, 8, 128), F32),
            pltpu.VMEM((SIDE, 8, 128), F32),
            pltpu.VMEM((3, 8, 128), F32),
            pltpu.SemaphoreType.DMA((pieces, 2, 3, 2)),
            pltpu.SemaphoreType.DMA((pieces, 2, 3, 2)),
            pltpu.SemaphoreType.DMA((pieces, 2, 3, 2)),
            pltpu.SemaphoreType.DMA((pieces, 2, 3, 2)),
            pltpu.SemaphoreType.DMA((6,)),
            pltpu.SemaphoreType.DMA((6,)),
        ],
        compiler_params=pltpu.CompilerParams(
            collective_id=collective_id, has_side_effects=True, vmem_limit_bytes=VMEM_LIMIT
        ),
        name=f"matmul_sum_{collective_id}",
    )(x.reshape(SIDE, SIDE, 2, rows, depth), w, blocks)
    return out.reshape(2 * rows, cols), sq_out[0, : 2 * rows]


def gate_up_kernel(
    x_ref, w_ref, sq_ref, down_ref, res_ref, final_ref, out_ref, part, mid, hid, got1, got2, sq1, sqm, sq2, inv,
    send1, recv1, send2, recv2, send3, recv3, send4, recv4, own_sem, sq_send, sq_recv,
    grown, terms, acc, mate, total, relay, direct, joined, sum_send, sum_recv,
):
    pieces, width = part.shape[0], part.shape[-1]
    units = out_ref.shape[-1]
    wide = width // 2
    rows = x_ref.shape[3]
    y, z = wide_place()
    names = (("y", "z"), ("z", "y"))
    spots = ((y, z), (z, y))
    greet(wide_lines() + narrow_neighbours())
    squares = Copies(sq_send, sq_recv)
    for by in (1, 2, 3):
        squares.start(by - 1, sq_ref.at[turn(y, by)], sq1.at[by - 1], ring_devices("y", by))

    lower, upper = pl.ds(0, 2), pl.ds(2, 2)
    low, high = pl.ds(0, rows // 2), pl.ds(rows // 2, rows // 2)

    def product(half, chunk, piece):
        block = x_ref[chunk, :, 0] if half == 0 else x_ref[:, chunk, 1]
        block = block.reshape(SIDE * rows, block.shape[-1])
        at = pl.multiple_of(piece * wide, 128)
        gate = jnp.dot(block, w_ref[:, pl.ds(at, wide)], preferred_element_type=F32)
        up = jnp.dot(block, w_ref[:, pl.ds(pl.multiple_of(units + at, 128), wide)], preferred_element_type=F32)
        return jnp.concatenate([gate, up], axis=1).reshape(SIDE, rows, width)

    def remote(src, dst, send, recv, axis, way):
        return pltpu.make_async_remote_copy(
            src_ref=src,
            dst_ref=dst,
            send_sem=send,
            recv_sem=recv,
            device_id=ring_devices(axis, 1 if way == 0 else 3),
            device_id_type=MESH,
        )

    def copy1(piece, half, kind, way, src):
        spot = (piece, half, kind, way)
        return remote(src, got1.at[spot], send1.at[spot], recv1.at[spot], names[half][0], way)

    def copy2(piece, half, kind, way, src):
        spot = (piece, half, kind, way)
        return remote(src, got2.at[spot], send2.at[spot], recv2.at[spot], names[half][1], way)

    def landed(ref, sem):
        pltpu.make_async_copy(ref, ref, sem).wait()

    def await1(piece, half, kind, way):
        landed(got1.at[piece, half, kind, way], recv1.at[piece, half, kind, way])
        return got1[piece, half, kind, way].astype(F32)

    def await2(piece, half, kind, way):
        landed(got2.at[piece, half, kind, way], recv2.at[piece, half, kind, way])
        return got2[piece, half, kind, way].astype(F32)

    def place(piece, half, first, second, part_rows):
        columns = pl.ds(pl.multiple_of(piece * wide, 128), wide)
        if half == 0:
            return out_ref.at[first, second, 0, part_rows, columns]
        return out_ref.at[second, first, 1, part_rows, columns]

    whole = pl.ds(0, rows)

    def copy3(piece, half, kind, way, src, dst):
        return remote(src, dst, send3.at[piece, half, kind, way], recv3.at[piece, half, kind, way], names[half][0], way)

    def copy4(piece, half, block, kind, way, src, dst):
        spot = (piece, half, block, kind, way)
        return remote(src, dst, send4.at[spot], recv4.at[spot], names[half][1], way)

    def send4_whole(piece, half, block, src):
        dst = place(piece, half, turn(spots[half][0], block), spots[half][1], whole)
        for way in range(2):
            copy4(piece, half, block, 0, way, src, dst).start()

    def relay4(piece, half, block):
        first = turn(spots[half][0], block)
        for way, by, part_rows in ((0, 3, low), (1, 1, high)):
            second = turn(spots[half][1], by)
            landed(place(piece, half, first, second, whole), recv4.at[piece, half, block, 0, way])
            came = place(piece, half, first, second, part_rows)
            copy4(piece, half, block, 1, way, came, came).start()

    def stage1(piece):
        for half in range(2):
            far = turn(spots[half][0], 2)
            part[piece, half, far] = product(half, far, piece).astype(BF)
            copy1(piece, half, 0, 0, part.at[piece, half, far, lower]).start()
            copy1(piece, half, 0, 1, part.at[piece, half, far, upper]).start()
        for half in range(2):
            right, left = turn(spots[half][0], 1), turn(spots[half][0], 3)
            part[piece, half, right] = product(half, right, piece).astype(BF)
            copy1(piece, half, 1, 0, part.at[piece, half, right, upper]).start()
            part[piece, half, left] = product(half, left, piece).astype(BF)
            copy1(piece, half, 1, 1, part.at[piece, half, left, lower]).start()

    def stage2(piece):
        for half in range(2):
            right, left = turn(spots[half][0], 1), turn(spots[half][0], 3)
            got = await1(piece, half, 0, 0)
            part[piece, half, right, lower] = (part[piece, half, right, lower].astype(F32) + got).astype(BF)
            copy1(piece, half, 2, 0, part.at[piece, half, right, lower]).start()
            got = await1(piece, half, 0, 1)
            part[piece, half, left, upper] = (part[piece, half, left, upper].astype(F32) + got).astype(BF)
            copy1(piece, half, 2, 1, part.at[piece, half, left, upper]).start()

    def stage3(piece):
        for half in range(2):
            own = product(half, spots[half][0], piece)
            mid[piece, half, lower] = (
                own[:2] + await1(piece, half, 1, 1) + await1(piece, half, 2, 0)
            ).astype(BF)
            mid[piece, half, upper] = (
                own[2:] + await1(piece, half, 1, 0) + await1(piece, half, 2, 1)
            ).astype(BF)
            far, right, left = (turn(spots[half][1], by) for by in (2, 1, 3))
            copy2(piece, half, 0, 0, mid.at[piece, half, far, low]).start()
            copy2(piece, half, 0, 1, mid.at[piece, half, far, high]).start()
            copy2(piece, half, 1, 0, mid.at[piece, half, right, high]).start()
            copy2(piece, half, 1, 1, mid.at[piece, half, left, low]).start()

    def stage4(piece):
        for half in range(2):
            right, left = turn(spots[half][1], 1), turn(spots[half][1], 3)
            got = await2(piece, half, 0, 0)
            mid[piece, half, right, low] = (mid[piece, half, right, low].astype(F32) + got).astype(BF)
            copy2(piece, half, 2, 0, mid.at[piece, half, right, low]).start()
            got = await2(piece, half, 0, 1)
            mid[piece, half, left, high] = (mid[piece, half, left, high].astype(F32) + got).astype(BF)
            copy2(piece, half, 2, 1, mid.at[piece, half, left, high]).start()

    def activate(sums, factor):
        sums = jnp.where(factor > 0, sums * factor, 0.0)
        gate, up = sums[:, :wide], sums[:, wide:]
        return (gate / (1.0 + jnp.exp(-gate)) * up).astype(BF)

    def stage5(piece):
        for half in range(2):
            own = spots[half][1]
            hid[piece, half, low] = activate(
                mid[piece, half, own, low].astype(F32) + await2(piece, half, 1, 1) + await2(piece, half, 2, 0),
                inv[half, low][:, :1],
            )
            hid[piece, half, high] = activate(
                mid[piece, half, own, high].astype(F32) + await2(piece, half, 1, 0) + await2(piece, half, 2, 1),
                inv[half, high][:, :1],
            )
            mine = hid.at[piece, half]
            dst = place(piece, half, *spots[half], whole)
            pltpu.make_async_copy(mine, dst, own_sem.at[piece, half]).start()
            for way in range(2):
                copy3(piece, half, 0, way, mine, dst).start()
            send4_whole(piece, half, 0, mine)

    def stage6(piece):
        for half in range(2):
            for way, by, part_rows in ((0, 3, low), (1, 1, high)):
                first = turn(spots[half][0], by)
                landed(place(piece, half, first, spots[half][1], whole), recv3.at[piece, half, 0, way])
                came = place(piece, half, first, spots[half][1], part_rows)
                copy3(piece, half, 1, way, came, came).start()
                send4_whole(piece, half, by, place(piece, half, first, spots[half][1], whole))
        for half in range(2):
            relay4(piece, half, 0)

    def stage7(piece):
        for half in range(2):
            far = turn(spots[half][0], 2)
            landed(place(piece, half, far, spots[half][1], low), recv3.at[piece, half, 1, 0])
            landed(place(piece, half, far, spots[half][1], high), recv3.at[piece, half, 1, 1])
            send4_whole(piece, half, 2, place(piece, half, far, spots[half][1], whole))
        for half in range(2):
            relay4(piece, half, 3)
            relay4(piece, half, 1)

    def stage8(piece):
        for half in range(2):
            relay4(piece, half, 2)

    def stage9(piece):
        for half in range(2):
            for block in range(4):
                first, second = turn(spots[half][0], block), turn(spots[half][1], 2)
                landed(place(piece, half, first, second, low), recv4.at[piece, half, block, 1, 0])
                landed(place(piece, half, first, second, high), recv4.at[piece, half, block, 1, 1])
            mine = place(piece, half, *spots[half], whole)
            landed(mine, own_sem.at[piece, half])
            for way in range(2):
                for kind in range(3):
                    copy1(piece, half, kind, way, part.at[piece, half, 0, lower]).wait_send()
                    copy2(piece, half, kind, way, mid.at[piece, half, 0, low]).wait_send()
                for kind, part_rows in ((0, whole), (1, low)):
                    ref = place(piece, half, *spots[half], part_rows)
                    copy3(piece, half, kind, way, ref, ref).wait_send()
                    for block in range(4):
                        copy4(piece, half, block, kind, way, ref, ref).wait_send()
        columns = pl.ds(pl.multiple_of(piece * wide, 128), wide)
        tokens = 2 * SIDE * rows
        for group in range(SIDE):
            values = out_ref[group, :, :, :, columns].reshape(tokens, wide)
            got = lax.dot_general(
                down_ref[:, columns], values, (((1,), (1,)), ((), ())), preferred_element_type=F32
            )
            spot = pl.ds(group * tokens, tokens)
            grown[:, spot] += got

    stages = (stage1, stage2, stage3, stage4, stage5, stage6, stage7, stage8, stage9)

    def step(t, carry):
        for lag, stage in enumerate(stages):
            piece = t - lag

            @pl.when((piece >= 0) & (piece < pieces))
            def _():
                stage(jnp.clip(piece, 0, pieces - 1))

        return carry

    grown[...] = jnp.zeros_like(grown)
    lax.fori_loop(0, 3, step, 0)

    for by in (1, 2, 3):
        squares.arrived(by - 1, sq1.at[by - 1])
    sqm[...] = sq_ref[y] + sq1[0] + sq1[1] + sq1[2]
    for by in (1, 2, 3):
        squares.start(2 + by, sqm.at[turn(z, by)], sq2.at[by - 1], ring_devices("z", by))
    lax.fori_loop(3, 4, step, 0)
    for by in (1, 2, 3):
        squares.arrived(2 + by, sq2.at[by - 1])
    everything = (sqm[z] + sq2[0] + sq2[1] + sq2[2])[:1]
    factor = lax.rsqrt(everything / D + epsilon)
    token = lax.broadcasted_iota(jnp.int32, (2 * rows, 128), 0)
    lane = lax.broadcasted_iota(jnp.int32, (2 * rows, 128), 1)
    column = jnp.sum(jnp.where(token == lane, factor, 0.0), axis=1, keepdims=True)
    inv[...] = jnp.broadcast_to(column, (2 * rows, 128)).reshape(2, rows, 128)
    lax.fori_loop(4, pieces + len(stages) - 1, step, 0)
    squares.sent()
    sums = Copies(sum_send, sum_recv)
    terms[...] = split_terms(grown[...])
    sum_narrow_body(terms, acc, mate, total, relay, direct, joined, sums)
    final_ref[...] = (res_ref[...].astype(F32) + acc[...]).astype(BF)
    sums.sent()


def token_blocks(sq, rows):
    blocks = jnp.pad(sq.reshape(SIDE, SIDE, 1, 2 * rows), ((0, 0), (0, 0), (0, 0), (0, 128 - 2 * rows)))
    return jnp.broadcast_to(blocks, (SIDE, SIDE, 8, 128))


def gate_up(x, w, sq, down, residual, pieces, collective_id):
    tokens, depth = x.shape
    units = w.shape[1] // 2
    width = 2 * units // pieces
    rows = tokens // (2 * SIDE * SIDE)
    dma = pltpu.SemaphoreType.DMA
    return pl.pallas_call(
        gate_up_kernel,
        out_shape=jax.ShapeDtypeStruct(residual.shape, BF),
        in_specs=[VM] * 5,
        out_specs=VM,
        scratch_shapes=[
            pltpu.VMEM((SIDE, SIDE, 2, rows, units), BF),
            pltpu.VMEM((pieces, 2, SIDE, SIDE, rows, width), BF),
            pltpu.VMEM((pieces, 2, SIDE, rows, width), BF),
            pltpu.VMEM((pieces, 2, rows, width // 2), BF),
            pltpu.VMEM((pieces, 2, 3, 2, 2, rows, width), BF),
            pltpu.VMEM((pieces, 2, 3, 2, rows // 2, width), BF),
            pltpu.VMEM((3, SIDE, 8, 128), F32),
            pltpu.VMEM((SIDE, 8, 128), F32),
            pltpu.VMEM((3, 8, 128), F32),
            pltpu.VMEM((2, rows, 128), F32),
            dma((pieces, 2, 3, 2)),
            dma((pieces, 2, 3, 2)),
            dma((pieces, 2, 3, 2)),
            dma((pieces, 2, 3, 2)),
            dma((pieces, 2, 2, 2)),
            dma((pieces, 2, 2, 2)),
            dma((pieces, 2, 4, 2, 2)),
            dma((pieces, 2, 4, 2, 2)),
            dma((pieces, 2)),
            dma((6,)),
            dma((6,)),
            pltpu.VMEM((down.shape[0], tokens), F32),
        ]
        + sum_scratch(*residual.shape),
        compiler_params=pltpu.CompilerParams(
            collective_id=collective_id, has_side_effects=True, vmem_limit_bytes=VMEM_LIMIT
        ),
        name="gate_up",
    )(x.reshape(SIDE, SIDE, 2, rows, depth), w, token_blocks(sq, rows), down, residual)


CHUNK = 2


def attend_kernel(
    lengths_ref, q_ref, cache_ref, own_ref, out_ref, sums_ref, span_ref, local_sem, send_sem, recv_sem
):
    scale = HDIM ** (-0.5)
    rows = q_ref.shape[1]
    per = own_ref.shape[1]
    block = cache_ref.shape[2] * CHUNK
    spot = lax.axis_index("wide")
    copies = Copies(send_sem, recv_sem)
    greet(wide_lines())
    gather = gather_direct_steps(own_ref, span_ref, local_sem, copies)
    next(gather)
    queries = [q_ref[request] for request in range(R)]

    def absorb(running, q, keys, values, allowed):
        peak, weight_sum, gathered = running
        scores = lax.dot_general(q, keys, (((1,), (1,)), ((), ())), preferred_element_type=F32) * scale
        scores = jnp.where(allowed(scores.shape), scores, floor_score)
        new_peak = jnp.maximum(peak, jnp.max(scores, axis=1, keepdims=True))
        weights = jnp.exp(scores - new_peak)
        factor = jnp.exp(peak - new_peak)
        weight_sum = weight_sum * factor + jnp.sum(weights, axis=1, keepdims=True)
        gathered = gathered * factor + jnp.dot(weights.astype(BF), values, preferred_element_type=F32)
        return new_peak, weight_sum, gathered

    def own_keys(shape):
        key = lax.broadcasted_iota(jnp.int32, shape, 1)
        row = lax.broadcasted_iota(jnp.int32, shape, 0)
        return key <= spot * per + lax.rem(row, per)

    running = [
        (
            jnp.full((rows, 1), floor_score, F32),
            jnp.zeros((rows, 1), F32),
            jnp.zeros((rows, HDIM), F32),
        )
        for _ in range(R)
    ]
    for index in range(cache_ref.shape[0] // CHUNK):
        for request in range(R):
            pair = cache_ref[pl.ds(index * CHUNK, CHUNK), request].reshape(block, 2 * HDIM)
            running[request] = absorb(
                running[request],
                queries[request],
                pair[:, :HDIM],
                pair[:, HDIM:],
                lambda shape: index * block + lax.broadcasted_iota(jnp.int32, shape, 1) < lengths_ref[request],
            )
        if index >= 2:
            next(gather, None)
    interleave(gather)
    for request in range(R):
        span = span_ref[:, :, request].reshape(SIDE * SIDE * per, 2 * HDIM)
        peak, weight_sum, gathered = absorb(
            running[request], queries[request], span[:, :HDIM], span[:, HDIM:], own_keys
        )
        out_ref[request] = (gathered / weight_sum).astype(BF)
        sums_ref[request] = jnp.broadcast_to(peak + jnp.log(weight_sum), (rows, HDIM))
    copies.sent()


def attend(lengths, queries, cache, own, collective_id):
    return pl.pallas_call(
        attend_kernel,
        out_shape=(
            jax.ShapeDtypeStruct(queries.shape, BF),
            jax.ShapeDtypeStruct(queries.shape, F32),
        ),
        in_specs=[SM, VM, VM, VM],
        out_specs=(VM, VM),
        scratch_shapes=[
            pltpu.VMEM((SIDE, SIDE) + own.shape, BF),
            pltpu.SemaphoreType.DMA,
            pltpu.SemaphoreType.DMA((DIRECT_COPIES,)),
            pltpu.SemaphoreType.DMA((DIRECT_COPIES,)),
        ],
        compiler_params=pltpu.CompilerParams(
            collective_id=collective_id, has_side_effects=True, vmem_limit_bytes=VMEM_LIMIT
        ),
        name="attend",
    )(lengths, queries, cache, own)


def token_angles(lengths, offsets, first_token, row_count, dim_size):
    token_ids = first_token + jnp.arange(row_count, dtype=jnp.int32)
    request_ids = token_ids % R
    start_pos = offsets + lengths
    matches = request_ids[:, None] == jnp.arange(start_pos.shape[0], dtype=jnp.int32)[None, :]
    chosen = jnp.sum(jnp.where(matches, start_pos[None, :], 0), axis=1)
    position = (chosen + token_ids // R).astype(jnp.float32)
    inverse = rope_base ** (-(jnp.arange(dim_size // 2, dtype=jnp.float32) * 2.0) / dim_size)
    return position[:, None] * inverse[None, :]


def rotate(values, angles):
    half_dim = values.shape[-1] // 2
    first_half = values[..., :half_dim]
    second_half = values[..., half_dim:]
    cosine = jnp.cos(angles)[:, None, :]
    sine_part = jnp.sin(angles)[:, None, :]
    return jnp.concatenate(
        [
            first_half * cosine - second_half * sine_part,
            second_half * cosine + first_half * sine_part,
        ],
        axis=-1,
    )


def to_send(flipped, gain):
    widened = flipped.astype(F32)
    squares = jnp.sum(widened * widened, axis=0, keepdims=True)
    high = lax.reduce_precision(squares, 8, 7)
    rest = squares - high
    middle = lax.reduce_precision(rest, 8, 7)
    low = rest - middle
    scaled = widened * gain.astype(F32)[:, None]
    pad = jnp.zeros((5, flipped.shape[1]), F32)
    return jnp.concatenate([scaled, high, middle, low, pad], axis=0).astype(BF)


def unpack(gathered, rows):
    scaled = gathered[:, :rows].reshape(8 * rows, -1).T
    squares = jnp.sum(gathered[:, rows : rows + 3].astype(F32), axis=(0, 1))
    return scaled, squares


def rescale(sums, squares):
    inv_scale = lax.rsqrt(squares / D + epsilon)[:, None]
    return jnp.where(inv_scale > 0, sums * inv_scale, 0.0)


def local(
    hidden_in, attn_gain, w_qkv, cache_kv, lengths, offsets, w_out, mlp_gain, w_gate_up, w_down
):
    all_tokens, features = hidden_in.shape
    per_device = all_tokens // lax.axis_size("wide")
    first_token = lax.axis_index("wide") * per_device
    flipped = hidden_in.T
    positions = cache_kv.shape[1]
    cache = cache_kv.reshape(R, positions, 2 * HDIM)
    gathered, cache_all = gather_both(to_send(flipped, attn_gain), cache, 1)
    scaled, squares = unpack(gathered, features)
    projected, squares = matmul_sum(scaled, w_qkv.reshape(w_qkv.shape[0], -1), squares, 3, 2)
    projected = rescale(projected, squares).reshape(per_device, GROUP + 2, HDIM)
    angles = token_angles(lengths, offsets, first_token, per_device, HDIM)
    rotated = rotate(projected[:, : GROUP + 1], angles).astype(BF)
    new_keys, new_values = rotated[:, GROUP], projected[:, GROUP + 1].astype(BF)
    new_cache = jnp.stack([new_keys, new_values], axis=1)[:, None]
    per_request = per_device // R
    span = jnp.concatenate([new_keys, new_values], axis=1).reshape(per_request, R, 2 * HDIM)
    queries = rotated[:, :GROUP].reshape(per_request, R, GROUP, HDIM).transpose(1, 2, 0, 3)
    attended, sums = attend(
        lengths,
        queries.reshape(R, GROUP * per_request, HDIM),
        cache_all.reshape(SIDE * SIDE, R, positions, 2 * HDIM),
        span.transpose(1, 0, 2),
        3,
    )
    attended = attended.reshape(R, GROUP, per_request, HDIM).transpose(2, 0, 1, 3).reshape(2, -1, GROUP * HDIM)
    softmax_sums = sums[:, :, 0].reshape(R, GROUP, per_request).transpose(2, 0, 1).reshape(per_device, GROUP)
    residual, gathered = out_proj(attended, w_out.T, flipped, mlp_gain, 5)
    scaled, squares = unpack(gathered, features)
    flat_gate_up = w_gate_up.reshape(w_gate_up.shape[0], -1)
    hidden_out = gate_up(scaled, flat_gate_up, squares, w_down.T, residual, 4, 7).T
    return (hidden_out, softmax_sums, new_cache)


def solution(mesh):
    return jax.shard_map(
        local,
        mesh=mesh,
        in_specs=(
            P(None, ("wide", "narrow")),
            P(("wide", "narrow")),
            P("wide", "narrow", None),
            P(None, "wide", "narrow", None, None),
            P(),
            P(),
            P("narrow", "wide"),
            P(("wide", "narrow")),
            P("wide", None, "narrow"),
            P("narrow", "wide"),
        ),
        out_specs=(
            P(None, ("wide", "narrow")),
            P("wide", "narrow"),
            P("wide", "narrow", None, None),
        ),
        check_vma=False,
    )
```

```python
import functools

import jax
import jax.numpy as jnp
from jax import lax
from jax.experimental import pallas as pl
from jax.experimental.pallas import tpu as pltpu
from jax.sharding import PartitionSpec as P

D = 7168
HDIM = 128
R = 2
GROUP = 7
SIDE = 4

epsilon = 1e-05
rope_base = 5000000.0
floor_score = -1e30

MESH = pl.DeviceIdType.MESH
BF = jnp.bfloat16
F32 = jnp.float32
ANY = pl.BlockSpec(memory_space=pl.ANY)
VM = pl.BlockSpec(memory_space=pltpu.VMEM)
SM = pl.BlockSpec(memory_space=pltpu.SMEM)
VMEM_LIMIT = 60 * 1024 * 1024


def wide_place():
    w = lax.axis_index("wide")
    return lax.div(w, SIDE), lax.rem(w, SIDE)


def turn(pos, by):
    return lax.rem(pos + by, SIDE)


def ring_devices(axis, by):
    if axis == "x":
        n = lax.axis_index("narrow")
        return {"narrow": turn(lax.div(n, 2), by) * 2 + lax.rem(n, 2)}
    y, z = wide_place()
    if axis == "y":
        return {"wide": turn(y, by) * SIDE + z}
    return {"wide": y * SIDE + turn(z, by)}


def partner_device():
    n = lax.axis_index("narrow")
    return {"narrow": lax.div(n, 2) * 2 + 1 - lax.rem(n, 2)}


def greet(devices):
    barrier = pltpu.get_barrier_semaphore()
    for device in devices:
        pl.semaphore_signal(barrier, inc=1, device_id=device, device_id_type=MESH)
    pl.semaphore_wait(barrier, len(devices))


class Copies:
    def __init__(self, send_sem, recv_sem):
        self.send_sem, self.recv_sem, self.used, self.made = send_sem, recv_sem, 0, []

    def slot(self):
        self.used += 1
        return self.used - 1

    def start(self, slot, src, dst, device):
        copy = pltpu.make_async_remote_copy(
            src_ref=src,
            dst_ref=dst,
            send_sem=self.send_sem.at[slot],
            recv_sem=self.recv_sem.at[slot],
            device_id=device,
            device_id_type=MESH,
        )
        copy.start()
        self.made.append(copy)

    def arrived(self, slot, dst):
        pltpu.make_async_copy(dst, dst, self.recv_sem.at[slot]).wait()

    def sent(self):
        for copy in self.made:
            copy.wait_send()


def interleave(*parts):
    live = list(parts)
    while live:
        for part in list(live):
            try:
                next(part)
            except StopIteration:
                live.remove(part)


def gather_wide_steps(x_ref, out_ref, local_sem, copies):
    y, z = wide_place()
    depth = x_ref.shape[1] // 2
    lower, upper = pl.ds(0, depth), pl.ds(depth, depth)

    def place(half, first, second):
        if half == 0:
            return out_ref.at[first, second, 0]
        return out_ref.at[second, first, 1]

    names = (("y", "z"), ("z", "y"))
    spots = ((y, z), (z, y))
    own = pltpu.make_async_copy(x_ref, out_ref.at[y, z], local_sem)
    own.start()
    hop1 = [[copies.slot() for _ in range(4)] for _ in range(2)]
    hop2 = [[[copies.slot() for _ in range(4)] for _ in range(4)] for _ in range(2)]

    def send2(half, block, src):
        first = turn(spots[half][0], block)
        target = place(half, first, spots[half][1])
        for way, by in ((0, 1), (1, 3)):
            copies.start(hop2[half][block][way], src, target, ring_devices(names[half][1], by))

    def relay2(half, block):
        first = turn(spots[half][0], block)
        for way, by, part in ((0, 1, lower), (1, 3, upper)):
            came = place(half, first, turn(spots[half][1], 4 - by))
            copies.arrived(hop2[half][block][way], came)
            copies.start(
                hop2[half][block][2 + way], came.at[part], came.at[part], ring_devices(names[half][1], by)
            )

    for half in range(2):
        target = place(half, *spots[half])
        for way, by in ((0, 1), (1, 3)):
            copies.start(hop1[half][way], x_ref.at[half], target, ring_devices(names[half][0], by))
        send2(half, 0, x_ref.at[half])
    yield
    for half in range(2):
        for way, by, part in ((0, 1, lower), (1, 3, upper)):
            came = place(half, turn(spots[half][0], 4 - by), spots[half][1])
            copies.arrived(hop1[half][way], came)
            copies.start(hop1[half][2 + way], came.at[part], came.at[part], ring_devices(names[half][0], by))
            send2(half, 4 - by, came)
        yield
    for half in range(2):
        relay2(half, 0)
        yield
    for half in range(2):
        far = place(half, turn(spots[half][0], 2), spots[half][1])
        copies.arrived(hop1[half][2], far.at[lower])
        copies.arrived(hop1[half][3], far.at[upper])
        send2(half, 2, far)
        yield
    for block in (3, 1, 2):
        for half in range(2):
            relay2(half, block)
            yield
    for half in range(2):
        for block in (0, 3, 1, 2):
            far = place(half, turn(spots[half][0], block), turn(spots[half][1], 2))
            copies.arrived(hop2[half][block][2], far.at[lower])
            copies.arrived(hop2[half][block][3], far.at[upper])
    own.wait()


WIDE_COPIES = 40


def gather_direct_steps(x_ref, out_ref, local_sem, copies):
    y, z = wide_place()
    names = (("y", "z"), ("z", "y"))
    spots = ((y, z), (z, y))

    def place(half, first, second):
        if half == 0:
            return out_ref.at[first, second, 0]
        return out_ref.at[second, first, 1]

    own = pltpu.make_async_copy(x_ref, out_ref.at[y, z], local_sem)
    own.start()
    hop1 = [[copies.slot() for _ in range(3)] for _ in range(2)]
    hop2 = [[[copies.slot() for _ in range(3)] for _ in range(4)] for _ in range(2)]

    def send2(half, block, src):
        target = place(half, turn(spots[half][0], block), spots[half][1])
        for by in (2, 1, 3):
            copies.start(hop2[half][block][by - 1], src, target, ring_devices(names[half][1], by))

    for half in range(2):
        target = place(half, *spots[half])
        for by in (2, 1, 3):
            copies.start(hop1[half][by - 1], x_ref.at[half], target, ring_devices(names[half][0], by))
    for half in range(2):
        send2(half, 0, x_ref.at[half])
    yield
    for by in (1, 3, 2):
        for half in range(2):
            came = place(half, turn(spots[half][0], 4 - by), spots[half][1])
            copies.arrived(hop1[half][by - 1], came)
            send2(half, 4 - by, came)
        yield
    for block in range(4):
        for half in range(2):
            for by in (1, 3, 2):
                came = place(half, turn(spots[half][0], block), turn(spots[half][1], 4 - by))
                copies.arrived(hop2[half][block][by - 1], came)
    own.wait()


DIRECT_COPIES = 30


def wide_lines():
    return [ring_devices(axis, by) for axis in ("y", "z") for by in (1, 2, 3)]


def wide_neighbours():
    return [ring_devices(axis, by) for axis in ("y", "z") for by in (1, 3)]


def gather_narrow_steps(x_ref, out_ref, local_sem, copies):
    n = lax.axis_index("narrow")
    x, core = lax.div(n, 2), lax.rem(n, 2)
    depth = x_ref.shape[0] // 2
    lower, upper = pl.ds(0, depth), pl.ds(depth, depth)
    own = pltpu.make_async_copy(x_ref, out_ref.at[n], local_sem)
    own.start()
    slots = [copies.slot() for _ in range(8)]
    for way, by in ((0, 1), (1, 3)):
        copies.start(slots[way], x_ref, out_ref.at[n], ring_devices("x", by))
    copies.start(slots[4], x_ref, out_ref.at[n], partner_device())
    yield
    for way, by, part in ((0, 1, lower), (1, 3, upper)):
        came = out_ref.at[turn(x, 4 - by) * 2 + core]
        copies.arrived(slots[way], came)
        copies.start(slots[2 + way], came.at[part], came.at[part], ring_devices("x", by))
        copies.start(slots[5 + way], came, came, partner_device())
    yield
    far = out_ref.at[turn(x, 2) * 2 + core]
    copies.arrived(slots[2], far.at[lower])
    copies.arrived(slots[3], far.at[upper])
    copies.start(slots[7], far, far, partner_device())
    yield
    for slot, by in ((4, 0), (5, 3), (6, 1), (7, 2)):
        copies.arrived(slots[slot], out_ref.at[turn(x, by) * 2 + 1 - core])
    own.wait()


NARROW_COPIES = 8


def narrow_neighbours():
    return [ring_devices("x", 1), ring_devices("x", 3), partner_device()]


def unpack_steps(got_ref, x_ref, sq_ref):
    rows = x_ref.shape[1] // 8
    tokens = x_ref.shape[0]
    width = tokens // SIDE
    sums = jnp.zeros((8, tokens), F32)
    for device in range(8):
        sums = sums + got_ref[device].astype(F32)[rows:]
    squares = jnp.broadcast_to(jnp.sum(sums, axis=0, keepdims=True), (8, tokens))
    for pair in range(tokens // 128):
        block = squares[:, pair * 128 : pair * 128 + 128]
        y, z = divmod(2 * pair, SIDE)
        sq_ref[y, z] = block
        sq_ref[y, z + 1] = pltpu.roll(block, 64, 1)
    yield
    for group in range(SIDE):
        spot = pl.ds(group * width, width)
        turned = jnp.concatenate([got_ref[device, :, spot].astype(F32)[:rows] for device in range(8)], axis=0)
        x_ref[spot, :] = turned.T.astype(BF)
        yield


def flatten_steps(w_ref, out_ref, paired, flat, sem):
    came = pltpu.make_async_copy(w_ref, paired, sem.at[0])
    came.start()
    yield
    yield
    came.wait()
    for start in range(0, w_ref.shape[0], 64):

        def some(index, carry):
            spot = pl.ds(pl.multiple_of(start + index * 16, 16), 16)
            flat[0, spot] = paired[spot, 0, :]
            flat[1, spot] = paired[spot, 1, :]
            return carry

        lax.fori_loop(0, 4, some, 0)
        yield
    went = pltpu.make_async_copy(flat, out_ref, sem.at[1])
    went.start()
    yield
    went.wait()


def gather_both_kernel(
    x_ref, cache_ref, w_ref, xo_ref, sqo_ref, cacheo_ref, wo_ref,
    got, own, paired, flat, local_sem, flat_sem, send_n, recv_n, send_w, recv_w,
):
    near, far = Copies(send_n, recv_n), Copies(send_w, recv_w)
    for half in range(2):
        own[half, :, :HDIM] = cache_ref[half, :, 0, :]
        own[half, :, HDIM:] = cache_ref[half, :, 1, :]
    greet(narrow_neighbours() + wide_neighbours())

    def features():
        yield from gather_narrow_steps(x_ref, got, local_sem.at[0], near)
        yield from unpack_steps(got, xo_ref, sqo_ref)

    interleave(
        features(),
        gather_wide_steps(own, cacheo_ref, local_sem.at[1], far),
        flatten_steps(w_ref, wo_ref, paired, flat, flat_sem),
    )
    near.sent()
    far.sent()


def gather_both(x, cache, w, collective_id):
    rows, tokens = x.shape
    rows -= 8
    dma = pltpu.SemaphoreType.DMA
    flat = (w.shape[1], w.shape[0], w.shape[2])
    block = cache.shape[:2] + (2 * HDIM,)
    return pl.pallas_call(
        gather_both_kernel,
        out_shape=(
            jax.ShapeDtypeStruct((tokens, 8 * rows), BF),
            jax.ShapeDtypeStruct((SIDE, SIDE, 8, 128), F32),
            jax.ShapeDtypeStruct((SIDE, SIDE) + block, BF),
            jax.ShapeDtypeStruct(flat, BF),
        ),
        in_specs=[VM, VM, ANY],
        out_specs=(VM, VM, VM, ANY),
        scratch_shapes=[
            pltpu.VMEM((8, rows + 8, tokens), BF),
            pltpu.VMEM(block, BF),
            pltpu.VMEM(w.shape, BF),
            pltpu.VMEM(flat, BF),
            dma((2,)),
            dma((2,)),
            dma((NARROW_COPIES,)),
            dma((NARROW_COPIES,)),
            dma((WIDE_COPIES,)),
            dma((WIDE_COPIES,)),
        ],
        compiler_params=pltpu.CompilerParams(
            collective_id=collective_id, has_side_effects=True, vmem_limit_bytes=VMEM_LIMIT
        ),
        name="gather_both",
    )(x, cache, w)


SUM_COPIES = 10


def sum_narrow_body(p_ref, acc, mate, total, relay, direct, joined, copies):
    n = lax.axis_index("narrow")
    x, core = lax.div(n, 2), lax.rem(n, 2)
    width = p_ref.shape[3] // 2
    lower, upper = pl.ds(0, width), pl.ds(width, width)
    right, left = ring_devices("x", 1), ring_devices("x", 3)
    order = (2, 1, 3, 0)
    mates = {by: copies.slot() for by in order}
    slots = [copies.slot() for _ in range(6)]
    for by in order:
        copies.start(mates[by], p_ref.at[turn(x, by), 1 - core], mate.at[by], partner_device())

    def pair(by):
        copies.arrived(mates[by], mate.at[by])
        return p_ref[turn(x, by), core].astype(F32) + mate[by].astype(F32)

    total[2] = pair(2).astype(BF)
    copies.start(slots[0], total.at[2, :, lower], relay.at[0], right)
    copies.start(slots[1], total.at[2, :, upper], relay.at[1], left)
    total[1] = pair(1).astype(BF)
    copies.start(slots[2], total.at[1, :, upper], direct.at[0], right)
    total[3] = pair(3).astype(BF)
    copies.start(slots[3], total.at[3, :, lower], direct.at[1], left)
    copies.arrived(slots[0], relay.at[0])
    total[1, :, lower] = (total[1, :, lower].astype(F32) + relay[0].astype(F32)).astype(BF)
    copies.start(slots[4], total.at[1, :, lower], joined.at[0], right)
    copies.arrived(slots[1], relay.at[1])
    total[3, :, upper] = (total[3, :, upper].astype(F32) + relay[1].astype(F32)).astype(BF)
    copies.start(slots[5], total.at[3, :, upper], joined.at[1], left)
    acc[...] = pair(0)
    copies.arrived(slots[2], direct.at[0])
    acc[:, upper] += direct[0].astype(F32)
    copies.arrived(slots[3], direct.at[1])
    acc[:, lower] += direct[1].astype(F32)
    copies.arrived(slots[4], joined.at[0])
    acc[:, lower] += joined[0].astype(F32)
    copies.arrived(slots[5], joined.at[1])
    acc[:, upper] += joined[1].astype(F32)


def sum_scratch(rows, cols):
    piece = pltpu.VMEM((2, rows, cols // 2), BF)
    dma = pltpu.SemaphoreType.DMA
    return [
        pltpu.VMEM((4, 2, rows, cols), BF),
        pltpu.VMEM((rows, cols), F32),
        pltpu.VMEM((4, rows, cols), BF),
        pltpu.VMEM((4, rows, cols), BF),
        piece,
        piece,
        piece,
        dma((SUM_COPIES,)),
        dma((SUM_COPIES,)),
    ]


def split_terms(terms):
    return terms.astype(BF).reshape(4, 2, terms.shape[0] // 8, terms.shape[1])


def out_proj_kernel(
    own_ref, w_ref, x_ref, gain_ref, res_ref, xo_ref, sqo_ref, got, all_ref, block, terms, acc, mate, total, relay, direct, joined,
    sum_send, sum_recv, local_sem, wide_send, wide_recv, near_send, near_recv,
):
    rows = x_ref.shape[0]
    wide, sums, near = Copies(wide_send, wide_recv), Copies(sum_send, sum_recv), Copies(near_send, near_recv)
    greet(wide_neighbours() + narrow_neighbours())
    interleave(gather_wide_steps(own_ref, all_ref, local_sem.at[0], wide))
    depth = w_ref.shape[1]
    tokens = x_ref.shape[1] // SIDE
    for group in range(SIDE):
        values = all_ref[group].reshape(tokens, depth)
        term = lax.dot_general(w_ref[...], values, (((1,), (1,)), ((), ())), preferred_element_type=F32)
        terms[:, :, :, pl.ds(group * tokens, tokens)] = split_terms(term)
    sum_narrow_body(terms, acc, mate, total, relay, direct, joined, sums)
    residual = (x_ref[...].astype(F32) + acc[...]).astype(BF)
    res_ref[...] = residual
    widened = residual.astype(F32)
    squares = jnp.sum(widened * widened, axis=0, keepdims=True)
    high = squares.astype(BF).astype(F32)
    rest = squares - high
    middle = rest.astype(BF).astype(F32)
    low = rest - middle
    line = lax.broadcasted_iota(jnp.int32, (8, widened.shape[1]), 0)
    tail = jnp.where(line == 0, high, jnp.where(line == 1, middle, jnp.where(line == 2, low, 0.0)))
    block[...] = jnp.concatenate([widened * gain_ref[:, :1], tail], axis=0).astype(BF)
    interleave(gather_narrow_steps(block, got, local_sem.at[1], near))
    interleave(unpack_steps(got, xo_ref, sqo_ref))
    wide.sent()
    sums.sent()
    near.sent()


def out_proj(own, w, x, gain, collective_id):
    rows, tokens = x.shape
    dma = pltpu.SemaphoreType.DMA
    return pl.pallas_call(
        out_proj_kernel,
        out_shape=(
            jax.ShapeDtypeStruct((rows, tokens), BF),
            jax.ShapeDtypeStruct((tokens, 8 * rows), BF),
            jax.ShapeDtypeStruct((SIDE, SIDE, 8, 128), F32),
        ),
        in_specs=[VM] * 4,
        out_specs=(VM, VM, VM),
        scratch_shapes=[
            pltpu.VMEM((8, rows + 8, tokens), BF),
            pltpu.VMEM((SIDE, SIDE) + own.shape, BF),
            pltpu.VMEM((rows + 8, tokens), BF),
        ]
        + sum_scratch(rows, tokens)
        + [
            dma((2,)),
            dma((WIDE_COPIES,)),
            dma((WIDE_COPIES,)),
            dma((NARROW_COPIES,)),
            dma((NARROW_COPIES,)),
        ],
        compiler_params=pltpu.CompilerParams(
            collective_id=collective_id, has_side_effects=True, vmem_limit_bytes=VMEM_LIMIT
        ),
        name="out_proj",
    )(own, w, x, jnp.broadcast_to(gain.astype(F32)[:, None], (rows, 128)))


def matmul_sum_kernel(
    x_ref, w_ref, sq_ref, out_ref, sqo_ref, part, mid, got1, got2, sq1, sqm, sq2,
    send1, recv1, send2, recv2, sq_send, sq_recv,
):
    pieces, width = part.shape[0], part.shape[-1]
    rows = x_ref.shape[3]
    y, z = wide_place()
    names = (("y", "z"), ("z", "y"))
    spots = ((y, z), (z, y))
    greet([ring_devices(axis, by) for axis in ("y", "z") for by in (1, 2, 3)])
    squares = Copies(sq_send, sq_recv)
    for by in (1, 2, 3):
        squares.start(by - 1, sq_ref.at[turn(y, by)], sq1.at[by - 1], ring_devices("y", by))

    def product(half, chunk, piece):
        block = x_ref[chunk, :, 0] if half == 0 else x_ref[:, chunk, 1]
        block = block.reshape(SIDE * rows, block.shape[-1])
        columns = pl.ds(pl.multiple_of(piece * width, 128), width)
        got = jnp.dot(block, w_ref[:, columns], preferred_element_type=F32)
        return got.reshape(SIDE, rows, width)

    def copy1(piece, half, kind, way, src):
        return pltpu.make_async_remote_copy(
            src_ref=src,
            dst_ref=got1.at[piece, half, kind, way],
            send_sem=send1.at[piece, half, kind, way],
            recv_sem=recv1.at[piece, half, kind, way],
            device_id=ring_devices(names[half][0], 1 if way == 0 else 3),
            device_id_type=MESH,
        )

    def copy2(piece, half, kind, way, src):
        return pltpu.make_async_remote_copy(
            src_ref=src,
            dst_ref=got2.at[piece, half, kind, way],
            send_sem=send2.at[piece, half, kind, way],
            recv_sem=recv2.at[piece, half, kind, way],
            device_id=ring_devices(names[half][1], 1 if way == 0 else 3),
            device_id_type=MESH,
        )

    def await1(piece, half, kind, way):
        ref = got1.at[piece, half, kind, way]
        pltpu.make_async_copy(ref, ref, recv1.at[piece, half, kind, way]).wait()
        return got1[piece, half, kind, way].astype(F32)

    def await2(piece, half, kind, way):
        ref = got2.at[piece, half, kind, way]
        pltpu.make_async_copy(ref, ref, recv2.at[piece, half, kind, way]).wait()
        return got2[piece, half, kind, way].astype(F32)

    lower, upper = pl.ds(0, 2), pl.ds(2, 2)
    low, high = pl.ds(0, rows // 2), pl.ds(rows // 2, rows // 2)

    def first(piece):
        for half in range(2):
            far = turn(spots[half][0], 2)
            part[piece, half, far] = product(half, far, piece).astype(BF)
            copy1(piece, half, 0, 0, part.at[piece, half, far, lower]).start()
            copy1(piece, half, 0, 1, part.at[piece, half, far, upper]).start()
        for half in range(2):
            right, left = turn(spots[half][0], 1), turn(spots[half][0], 3)
            part[piece, half, right] = product(half, right, piece).astype(BF)
            copy1(piece, half, 1, 0, part.at[piece, half, right, upper]).start()
            part[piece, half, left] = product(half, left, piece).astype(BF)
            copy1(piece, half, 1, 1, part.at[piece, half, left, lower]).start()

    def second(piece):
        for half in range(2):
            right, left = turn(spots[half][0], 1), turn(spots[half][0], 3)
            got = await1(piece, half, 0, 0)
            part[piece, half, right, lower] = (part[piece, half, right, lower].astype(F32) + got).astype(BF)
            copy1(piece, half, 2, 0, part.at[piece, half, right, lower]).start()
            got = await1(piece, half, 0, 1)
            part[piece, half, left, upper] = (part[piece, half, left, upper].astype(F32) + got).astype(BF)
            copy1(piece, half, 2, 1, part.at[piece, half, left, upper]).start()

    def third(piece):
        for half in range(2):
            own = product(half, spots[half][0], piece)
            mid[piece, half, lower] = (
                own[:2] + await1(piece, half, 1, 1) + await1(piece, half, 2, 0)
            ).astype(BF)
            mid[piece, half, upper] = (
                own[2:] + await1(piece, half, 1, 0) + await1(piece, half, 2, 1)
            ).astype(BF)
            far, right, left = (turn(spots[half][1], by) for by in (2, 1, 3))
            copy2(piece, half, 0, 0, mid.at[piece, half, far, low]).start()
            copy2(piece, half, 0, 1, mid.at[piece, half, far, high]).start()
            copy2(piece, half, 1, 0, mid.at[piece, half, right, high]).start()
            copy2(piece, half, 1, 1, mid.at[piece, half, left, low]).start()

    def fourth(piece):
        for half in range(2):
            right, left = turn(spots[half][1], 1), turn(spots[half][1], 3)
            got = await2(piece, half, 0, 0)
            mid[piece, half, right, low] = (mid[piece, half, right, low].astype(F32) + got).astype(BF)
            copy2(piece, half, 2, 0, mid.at[piece, half, right, low]).start()
            got = await2(piece, half, 0, 1)
            mid[piece, half, left, high] = (mid[piece, half, left, high].astype(F32) + got).astype(BF)
            copy2(piece, half, 2, 1, mid.at[piece, half, left, high]).start()

    def fifth(piece):
        columns = pl.ds(pl.multiple_of(piece * width, 128), width)
        for half in range(2):
            own = spots[half][1]
            out_ref[half, low, columns] = (
                mid[piece, half, own, low].astype(F32) + await2(piece, half, 1, 1) + await2(piece, half, 2, 0)
            )
            out_ref[half, high, columns] = (
                mid[piece, half, own, high].astype(F32) + await2(piece, half, 1, 0) + await2(piece, half, 2, 1)
            )

    stages = (first, second, third, fourth, fifth)

    def step(t, carry):
        for lag, stage in enumerate(stages):
            piece = t - lag

            @pl.when((piece >= 0) & (piece < pieces))
            def _():
                stage(jnp.clip(piece, 0, pieces - 1))

        return carry

    lax.fori_loop(0, pieces + len(stages) - 1, step, 0)

    for by in (1, 2, 3):
        squares.arrived(by - 1, sq1.at[by - 1])
    sqm[...] = sq_ref[y] + sq1[0] + sq1[1] + sq1[2]
    for by in (1, 2, 3):
        squares.start(2 + by, sqm.at[turn(z, by)], sq2.at[by - 1], ring_devices("z", by))
    for by in (1, 2, 3):
        squares.arrived(2 + by, sq2.at[by - 1])
    sqo_ref[...] = sqm[z] + sq2[0] + sq2[1] + sq2[2]
    squares.sent()

    def drain(piece, carry):
        for half in range(2):
            for kind in range(3):
                for way in range(2):
                    copy1(piece, half, kind, way, part.at[piece, half, 0, lower]).wait_send()
                    copy2(piece, half, kind, way, mid.at[piece, half, 0, low]).wait_send()
        return carry

    lax.fori_loop(0, pieces, drain, 0)


def matmul_sum(x, w, sq, pieces, collective_id):
    tokens, depth = x.shape
    cols = w.shape[1]
    width = cols // pieces
    rows = tokens // (2 * SIDE * SIDE)
    out, sq_out = pl.pallas_call(
        matmul_sum_kernel,
        out_shape=(
            jax.ShapeDtypeStruct((2, rows, cols), F32),
            jax.ShapeDtypeStruct((8, 128), F32),
        ),
        in_specs=[VM, VM, VM],
        out_specs=(VM, VM),
        scratch_shapes=[
            pltpu.VMEM((pieces, 2, SIDE, SIDE, rows, width), BF),
            pltpu.VMEM((pieces, 2, SIDE, rows, width), BF),
            pltpu.VMEM((pieces, 2, 3, 2, 2, rows, width), BF),
            pltpu.VMEM((pieces, 2, 3, 2, rows // 2, width), BF),
            pltpu.VMEM((3, SIDE, 8, 128), F32),
            pltpu.VMEM((SIDE, 8, 128), F32),
            pltpu.VMEM((3, 8, 128), F32),
            pltpu.SemaphoreType.DMA((pieces, 2, 3, 2)),
            pltpu.SemaphoreType.DMA((pieces, 2, 3, 2)),
            pltpu.SemaphoreType.DMA((pieces, 2, 3, 2)),
            pltpu.SemaphoreType.DMA((pieces, 2, 3, 2)),
            pltpu.SemaphoreType.DMA((6,)),
            pltpu.SemaphoreType.DMA((6,)),
        ],
        compiler_params=pltpu.CompilerParams(
            collective_id=collective_id, has_side_effects=True, vmem_limit_bytes=VMEM_LIMIT
        ),
        name=f"matmul_sum_{collective_id}",
    )(x.reshape(SIDE, SIDE, 2, rows, depth), w, sq)
    return out.reshape(2 * rows, cols), sq_out[0, : 2 * rows]


def gate_up_kernel(
    x_ref, w_ref, sq_ref, down_ref, res_ref, final_ref, out_ref, part, mid, hid, got1, got2, sq1, sqm, sq2, inv,
    send1, recv1, send2, recv2, send3, recv3, send4, recv4, own_sem, sq_send, sq_recv,
    grown, terms, acc, mate, total, relay, direct, joined, sum_send, sum_recv,
):
    pieces, width = part.shape[0], part.shape[-1]
    wide = width // 2
    rows = x_ref.shape[3]
    y, z = wide_place()
    names = (("y", "z"), ("z", "y"))
    spots = ((y, z), (z, y))
    greet(wide_lines() + narrow_neighbours())
    squares = Copies(sq_send, sq_recv)
    for by in (1, 2, 3):
        squares.start(by - 1, sq_ref.at[turn(y, by)], sq1.at[by - 1], ring_devices("y", by))

    lower, upper = pl.ds(0, 2), pl.ds(2, 2)
    low, high = pl.ds(0, rows // 2), pl.ds(rows // 2, rows // 2)

    def product(half, chunk, piece):
        block = x_ref[chunk, :, 0] if half == 0 else x_ref[:, chunk, 1]
        block = block.reshape(SIDE * rows, block.shape[-1])
        at = pl.multiple_of(piece * wide, 128)
        gate = jnp.dot(block, w_ref[0, :, pl.ds(at, wide)], preferred_element_type=F32)
        up = jnp.dot(block, w_ref[1, :, pl.ds(at, wide)], preferred_element_type=F32)
        return jnp.concatenate([gate, up], axis=1).reshape(SIDE, rows, width)

    def remote(src, dst, send, recv, axis, way):
        return pltpu.make_async_remote_copy(
            src_ref=src,
            dst_ref=dst,
            send_sem=send,
            recv_sem=recv,
            device_id=ring_devices(axis, 1 if way == 0 else 3),
            device_id_type=MESH,
        )

    def copy1(piece, half, kind, way, src):
        spot = (piece, half, kind, way)
        return remote(src, got1.at[spot], send1.at[spot], recv1.at[spot], names[half][0], way)

    def copy2(piece, half, kind, way, src):
        spot = (piece, half, kind, way)
        return remote(src, got2.at[spot], send2.at[spot], recv2.at[spot], names[half][1], way)

    def landed(ref, sem):
        pltpu.make_async_copy(ref, ref, sem).wait()

    def await1(piece, half, kind, way):
        landed(got1.at[piece, half, kind, way], recv1.at[piece, half, kind, way])
        return got1[piece, half, kind, way].astype(F32)

    def await2(piece, half, kind, way):
        landed(got2.at[piece, half, kind, way], recv2.at[piece, half, kind, way])
        return got2[piece, half, kind, way].astype(F32)

    def place(piece, half, first, second, part_rows):
        columns = pl.ds(pl.multiple_of(piece * wide, 128), wide)
        if half == 0:
            return out_ref.at[first, second, 0, part_rows, columns]
        return out_ref.at[second, first, 1, part_rows, columns]

    whole = pl.ds(0, rows)

    def copy3(piece, half, kind, way, src, dst):
        return remote(src, dst, send3.at[piece, half, kind, way], recv3.at[piece, half, kind, way], names[half][0], way)

    def copy4(piece, half, block, kind, way, src, dst):
        spot = (piece, half, block, kind, way)
        return remote(src, dst, send4.at[spot], recv4.at[spot], names[half][1], way)

    def send4_whole(piece, half, block, src):
        dst = place(piece, half, turn(spots[half][0], block), spots[half][1], whole)
        for way in range(2):
            copy4(piece, half, block, 0, way, src, dst).start()

    def relay4(piece, half, block):
        first = turn(spots[half][0], block)
        for way, by, part_rows in ((0, 3, low), (1, 1, high)):
            second = turn(spots[half][1], by)
            landed(place(piece, half, first, second, whole), recv4.at[piece, half, block, 0, way])
            came = place(piece, half, first, second, part_rows)
            copy4(piece, half, block, 1, way, came, came).start()

    def stage1(piece):
        for half in range(2):
            far = turn(spots[half][0], 2)
            part[piece, half, far] = product(half, far, piece).astype(BF)
            copy1(piece, half, 0, 0, part.at[piece, half, far, lower]).start()
            copy1(piece, half, 0, 1, part.at[piece, half, far, upper]).start()
        for half in range(2):
            right, left = turn(spots[half][0], 1), turn(spots[half][0], 3)
            part[piece, half, right] = product(half, right, piece).astype(BF)
            copy1(piece, half, 1, 0, part.at[piece, half, right, upper]).start()
            part[piece, half, left] = product(half, left, piece).astype(BF)
            copy1(piece, half, 1, 1, part.at[piece, half, left, lower]).start()

    def stage2(piece):
        for half in range(2):
            right, left = turn(spots[half][0], 1), turn(spots[half][0], 3)
            got = await1(piece, half, 0, 0)
            part[piece, half, right, lower] = (part[piece, half, right, lower].astype(F32) + got).astype(BF)
            copy1(piece, half, 2, 0, part.at[piece, half, right, lower]).start()
            got = await1(piece, half, 0, 1)
            part[piece, half, left, upper] = (part[piece, half, left, upper].astype(F32) + got).astype(BF)
            copy1(piece, half, 2, 1, part.at[piece, half, left, upper]).start()

    def stage3(piece):
        for half in range(2):
            own = product(half, spots[half][0], piece)
            mid[piece, half, lower] = (
                own[:2] + await1(piece, half, 1, 1) + await1(piece, half, 2, 0)
            ).astype(BF)
            mid[piece, half, upper] = (
                own[2:] + await1(piece, half, 1, 0) + await1(piece, half, 2, 1)
            ).astype(BF)
            far, right, left = (turn(spots[half][1], by) for by in (2, 1, 3))
            copy2(piece, half, 0, 0, mid.at[piece, half, far, low]).start()
            copy2(piece, half, 0, 1, mid.at[piece, half, far, high]).start()
            copy2(piece, half, 1, 0, mid.at[piece, half, right, high]).start()
            copy2(piece, half, 1, 1, mid.at[piece, half, left, low]).start()

    def stage4(piece):
        for half in range(2):
            right, left = turn(spots[half][1], 1), turn(spots[half][1], 3)
            got = await2(piece, half, 0, 0)
            mid[piece, half, right, low] = (mid[piece, half, right, low].astype(F32) + got).astype(BF)
            copy2(piece, half, 2, 0, mid.at[piece, half, right, low]).start()
            got = await2(piece, half, 0, 1)
            mid[piece, half, left, high] = (mid[piece, half, left, high].astype(F32) + got).astype(BF)
            copy2(piece, half, 2, 1, mid.at[piece, half, left, high]).start()

    def activate(sums, factor):
        sums = jnp.where(factor > 0, sums * factor, 0.0)
        gate, up = sums[:, :wide], sums[:, wide:]
        return (gate / (1.0 + jnp.exp(-gate)) * up).astype(BF)

    def stage5(piece):
        for half in range(2):
            own = spots[half][1]
            hid[piece, half, low] = activate(
                mid[piece, half, own, low].astype(F32) + await2(piece, half, 1, 1) + await2(piece, half, 2, 0),
                inv[half, low][:, :1],
            )
            hid[piece, half, high] = activate(
                mid[piece, half, own, high].astype(F32) + await2(piece, half, 1, 0) + await2(piece, half, 2, 1),
                inv[half, high][:, :1],
            )
            mine = hid.at[piece, half]
            dst = place(piece, half, *spots[half], whole)
            pltpu.make_async_copy(mine, dst, own_sem.at[piece, half]).start()
            for way in range(2):
                copy3(piece, half, 0, way, mine, dst).start()
            send4_whole(piece, half, 0, mine)

    def stage6(piece):
        for half in range(2):
            for way, by, part_rows in ((0, 3, low), (1, 1, high)):
                first = turn(spots[half][0], by)
                landed(place(piece, half, first, spots[half][1], whole), recv3.at[piece, half, 0, way])
                came = place(piece, half, first, spots[half][1], part_rows)
                copy3(piece, half, 1, way, came, came).start()
                send4_whole(piece, half, by, place(piece, half, first, spots[half][1], whole))
        for half in range(2):
            relay4(piece, half, 0)

    def stage7(piece):
        for half in range(2):
            far = turn(spots[half][0], 2)
            landed(place(piece, half, far, spots[half][1], low), recv3.at[piece, half, 1, 0])
            landed(place(piece, half, far, spots[half][1], high), recv3.at[piece, half, 1, 1])
            send4_whole(piece, half, 2, place(piece, half, far, spots[half][1], whole))
        for half in range(2):
            relay4(piece, half, 3)
            relay4(piece, half, 1)

    def stage8(piece):
        for half in range(2):
            relay4(piece, half, 2)

    def stage9(piece):
        for half in range(2):
            for block in range(4):
                first, second = turn(spots[half][0], block), turn(spots[half][1], 2)
                landed(place(piece, half, first, second, low), recv4.at[piece, half, block, 1, 0])
                landed(place(piece, half, first, second, high), recv4.at[piece, half, block, 1, 1])
            mine = place(piece, half, *spots[half], whole)
            landed(mine, own_sem.at[piece, half])
            for way in range(2):
                for kind in range(3):
                    copy1(piece, half, kind, way, part.at[piece, half, 0, lower]).wait_send()
                    copy2(piece, half, kind, way, mid.at[piece, half, 0, low]).wait_send()
                for kind, part_rows in ((0, whole), (1, low)):
                    ref = place(piece, half, *spots[half], part_rows)
                    copy3(piece, half, kind, way, ref, ref).wait_send()
                    for block in range(4):
                        copy4(piece, half, block, kind, way, ref, ref).wait_send()
        columns = pl.ds(pl.multiple_of(piece * wide, 128), wide)
        tokens = 2 * SIDE * rows
        for group in range(SIDE):
            values = out_ref[group, :, :, :, columns].reshape(tokens, wide)
            got = lax.dot_general(
                down_ref[:, columns], values, (((1,), (1,)), ((), ())), preferred_element_type=F32
            )
            spot = pl.ds(group * tokens, tokens)
            grown[:, spot] += got

    stages = (stage1, stage2, stage3, stage4, stage5, stage6, stage7, stage8, stage9)

    def step(t, carry):
        for lag, stage in enumerate(stages):
            piece = t - lag

            @pl.when((piece >= 0) & (piece < pieces))
            def _():
                stage(jnp.clip(piece, 0, pieces - 1))

        return carry

    grown[...] = jnp.zeros_like(grown)
    lax.fori_loop(0, 3, step, 0)

    for by in (1, 2, 3):
        squares.arrived(by - 1, sq1.at[by - 1])
    sqm[...] = sq_ref[y] + sq1[0] + sq1[1] + sq1[2]
    for by in (1, 2, 3):
        squares.start(2 + by, sqm.at[turn(z, by)], sq2.at[by - 1], ring_devices("z", by))
    lax.fori_loop(3, 4, step, 0)
    for by in (1, 2, 3):
        squares.arrived(2 + by, sq2.at[by - 1])
    everything = (sqm[z] + sq2[0] + sq2[1] + sq2[2])[:1]
    factor = lax.rsqrt(everything / D + epsilon)
    token = lax.broadcasted_iota(jnp.int32, (2 * rows, 128), 0)
    lane = lax.broadcasted_iota(jnp.int32, (2 * rows, 128), 1)
    column = jnp.sum(jnp.where(token == lane, factor, 0.0), axis=1, keepdims=True)
    inv[...] = jnp.broadcast_to(column, (2 * rows, 128)).reshape(2, rows, 128)
    lax.fori_loop(4, pieces + len(stages) - 1, step, 0)
    squares.sent()
    sums = Copies(sum_send, sum_recv)
    terms[...] = split_terms(grown[...])
    sum_narrow_body(terms, acc, mate, total, relay, direct, joined, sums)
    final_ref[...] = (res_ref[...].astype(F32) + acc[...]).astype(BF)
    sums.sent()


def gate_up(x, w, sq, down, residual, pieces, collective_id):
    tokens, depth = x.shape
    units = w.shape[2]
    width = 2 * units // pieces
    rows = tokens // (2 * SIDE * SIDE)
    dma = pltpu.SemaphoreType.DMA
    return pl.pallas_call(
        gate_up_kernel,
        out_shape=jax.ShapeDtypeStruct(residual.shape, BF),
        in_specs=[VM] * 5,
        out_specs=VM,
        scratch_shapes=[
            pltpu.VMEM((SIDE, SIDE, 2, rows, units), BF),
            pltpu.VMEM((pieces, 2, SIDE, SIDE, rows, width), BF),
            pltpu.VMEM((pieces, 2, SIDE, rows, width), BF),
            pltpu.VMEM((pieces, 2, rows, width // 2), BF),
            pltpu.VMEM((pieces, 2, 3, 2, 2, rows, width), BF),
            pltpu.VMEM((pieces, 2, 3, 2, rows // 2, width), BF),
            pltpu.VMEM((3, SIDE, 8, 128), F32),
            pltpu.VMEM((SIDE, 8, 128), F32),
            pltpu.VMEM((3, 8, 128), F32),
            pltpu.VMEM((2, rows, 128), F32),
            dma((pieces, 2, 3, 2)),
            dma((pieces, 2, 3, 2)),
            dma((pieces, 2, 3, 2)),
            dma((pieces, 2, 3, 2)),
            dma((pieces, 2, 2, 2)),
            dma((pieces, 2, 2, 2)),
            dma((pieces, 2, 4, 2, 2)),
            dma((pieces, 2, 4, 2, 2)),
            dma((pieces, 2)),
            dma((6,)),
            dma((6,)),
            pltpu.VMEM((down.shape[0], tokens), F32),
        ]
        + sum_scratch(*residual.shape),
        compiler_params=pltpu.CompilerParams(
            collective_id=collective_id, has_side_effects=True, vmem_limit_bytes=VMEM_LIMIT
        ),
        name="gate_up",
    )(x.reshape(SIDE, SIDE, 2, rows, depth), w, sq, down, residual)


CHUNK = 8


def attend_kernel(
    lengths_ref, q_ref, cache_ref, own_ref, out_ref, sums_ref, span_ref, local_sem, send_sem, recv_sem
):
    scale = HDIM ** (-0.5)
    rows = q_ref.shape[1]
    per = own_ref.shape[1]
    block = cache_ref.shape[2] * CHUNK
    spot = lax.axis_index("wide")
    copies = Copies(send_sem, recv_sem)
    greet(wide_lines())
    gather = gather_direct_steps(own_ref, span_ref, local_sem, copies)
    next(gather)
    queries = [q_ref[request] for request in range(R)]

    def absorb(running, q, keys, values, allowed):
        peak, weight_sum, gathered = running
        scores = lax.dot_general(q, keys, (((1,), (1,)), ((), ())), preferred_element_type=F32) * scale
        scores = jnp.where(allowed(scores.shape), scores, floor_score)
        new_peak = jnp.maximum(peak, jnp.max(scores, axis=1, keepdims=True))
        weights = jnp.exp(scores - new_peak)
        factor = jnp.exp(peak - new_peak)
        weight_sum = weight_sum * factor + jnp.sum(weights, axis=1, keepdims=True)
        gathered = gathered * factor + jnp.dot(weights.astype(BF), values, preferred_element_type=F32)
        return new_peak, weight_sum, gathered

    def own_keys(shape):
        key = lax.broadcasted_iota(jnp.int32, shape, 1)
        row = lax.broadcasted_iota(jnp.int32, shape, 0)
        return key <= spot * per + lax.rem(row, per)

    running = [
        (
            jnp.full((rows, 1), floor_score, F32),
            jnp.zeros((rows, 1), F32),
            jnp.zeros((rows, HDIM), F32),
        )
        for _ in range(R)
    ]
    for index in range(cache_ref.shape[0] // CHUNK):
        for request in range(R):
            pair = cache_ref[pl.ds(index * CHUNK, CHUNK), request].reshape(block, 2 * HDIM)
            running[request] = absorb(
                running[request],
                queries[request],
                pair[:, :HDIM],
                pair[:, HDIM:],
                lambda shape: index * block + lax.broadcasted_iota(jnp.int32, shape, 1) < lengths_ref[request],
            )
        if index >= 2:
            next(gather, None)
    interleave(gather)
    for request in range(R):
        span = span_ref[:, :, request].reshape(SIDE * SIDE * per, 2 * HDIM)
        peak, weight_sum, gathered = absorb(
            running[request], queries[request], span[:, :HDIM], span[:, HDIM:], own_keys
        )
        out_ref[request] = (gathered / weight_sum).astype(BF)
        sums_ref[request] = jnp.broadcast_to(peak + jnp.log(weight_sum), (rows, HDIM))
    copies.sent()


def attend(lengths, queries, cache, own, collective_id):
    return pl.pallas_call(
        attend_kernel,
        out_shape=(
            jax.ShapeDtypeStruct(queries.shape, BF),
            jax.ShapeDtypeStruct(queries.shape, F32),
        ),
        in_specs=[SM, VM, VM, VM],
        out_specs=(VM, VM),
        scratch_shapes=[
            pltpu.VMEM((SIDE, SIDE) + own.shape, BF),
            pltpu.SemaphoreType.DMA,
            pltpu.SemaphoreType.DMA((DIRECT_COPIES,)),
            pltpu.SemaphoreType.DMA((DIRECT_COPIES,)),
        ],
        compiler_params=pltpu.CompilerParams(
            collective_id=collective_id, has_side_effects=True, vmem_limit_bytes=VMEM_LIMIT
        ),
        name="attend",
    )(lengths, queries, cache, own)


def token_angles(lengths, offsets, first_token, row_count, dim_size):
    token_ids = first_token + jnp.arange(row_count, dtype=jnp.int32)
    request_ids = token_ids % R
    start_pos = offsets + lengths
    matches = request_ids[:, None] == jnp.arange(start_pos.shape[0], dtype=jnp.int32)[None, :]
    chosen = jnp.sum(jnp.where(matches, start_pos[None, :], 0), axis=1)
    position = (chosen + token_ids // R).astype(jnp.float32)
    inverse = rope_base ** (-(jnp.arange(dim_size // 2, dtype=jnp.float32) * 2.0) / dim_size)
    return position[:, None] * inverse[None, :]


def rotate(values, angles):
    half_dim = values.shape[-1] // 2
    first_half = values[..., :half_dim]
    second_half = values[..., half_dim:]
    cosine = jnp.cos(angles)[:, None, :]
    sine_part = jnp.sin(angles)[:, None, :]
    return jnp.concatenate(
        [
            first_half * cosine - second_half * sine_part,
            second_half * cosine + first_half * sine_part,
        ],
        axis=-1,
    )


def to_send(flipped, gain):
    widened = flipped.astype(F32)
    squares = jnp.sum(widened * widened, axis=0, keepdims=True)
    high = lax.reduce_precision(squares, 8, 7)
    rest = squares - high
    middle = lax.reduce_precision(rest, 8, 7)
    low = rest - middle
    scaled = widened * gain.astype(F32)[:, None]
    pad = jnp.zeros((5, flipped.shape[1]), F32)
    return jnp.concatenate([scaled, high, middle, low, pad], axis=0).astype(BF)


def rescale(sums, squares):
    inv_scale = lax.rsqrt(squares / D + epsilon)[:, None]
    return jnp.where(inv_scale > 0, sums * inv_scale, 0.0)


def local(
    hidden_in, attn_gain, w_qkv, cache_kv, lengths, offsets, w_out, mlp_gain, w_gate_up, w_down
):
    all_tokens, features = hidden_in.shape
    per_device = all_tokens // lax.axis_size("wide")
    first_token = lax.axis_index("wide") * per_device
    flipped = hidden_in.T
    positions = cache_kv.shape[1]
    cache = cache_kv.reshape(R, positions, 2, HDIM)
    scaled, squares, cache_all, flat_gate_up = gather_both(to_send(flipped, attn_gain), cache, w_gate_up, 1)
    projected, squares = matmul_sum(scaled, w_qkv.reshape(w_qkv.shape[0], -1), squares, 1, 2)
    projected = rescale(projected, squares).reshape(per_device, GROUP + 2, HDIM)
    angles = token_angles(lengths, offsets, first_token, per_device, HDIM)
    rotated = rotate(projected[:, : GROUP + 1], angles).astype(BF)
    new_keys, new_values = rotated[:, GROUP], projected[:, GROUP + 1].astype(BF)
    new_cache = jnp.stack([new_keys, new_values], axis=1)[:, None]
    per_request = per_device // R
    span = jnp.concatenate([new_keys, new_values], axis=1).reshape(per_request, R, 2 * HDIM)
    queries = rotated[:, :GROUP].reshape(per_request, R, GROUP, HDIM).transpose(1, 2, 0, 3)
    attended, sums = attend(
        lengths,
        queries.reshape(R, GROUP * per_request, HDIM),
        cache_all.reshape(SIDE * SIDE, R, positions, 2 * HDIM),
        span.transpose(1, 0, 2),
        3,
    )
    attended = attended.reshape(R, GROUP, per_request, HDIM).transpose(2, 0, 1, 3).reshape(2, -1, GROUP * HDIM)
    softmax_sums = sums[:, :, 0].reshape(R, GROUP, per_request).transpose(2, 0, 1).reshape(per_device, GROUP)
    residual, scaled, squares = out_proj(attended, w_out.T, flipped, mlp_gain, 5)
    hidden_out = gate_up(scaled, flat_gate_up, squares, w_down.T, residual, 2, 7).T
    return (hidden_out, softmax_sums, new_cache)


def solution(mesh):
    return jax.shard_map(
        local,
        mesh=mesh,
        in_specs=(
            P(None, ("wide", "narrow")),
            P(("wide", "narrow")),
            P("wide", "narrow", None),
            P(None, "wide", "narrow", None, None),
            P(),
            P(),
            P("narrow", "wide"),
            P(("wide", "narrow")),
            P("wide", None, "narrow"),
            P("narrow", "wide"),
        ),
        out_specs=(
            P(None, ("wide", "narrow")),
            P("wide", "narrow"),
            P("wide", "narrow", None, None),
        ),
        check_vma=False,
    )
```

```python
import functools

import jax
import jax.numpy as jnp
from jax import lax
from jax.experimental import pallas as pl
from jax.experimental.pallas import tpu as pltpu
from jax.sharding import PartitionSpec as P

D = 7168
HDIM = 128
R = 2
GROUP = 7
SIDE = 4

epsilon = 1e-05
rope_base = 5000000.0
floor_score = -1e30

MESH = pl.DeviceIdType.MESH
BF = jnp.bfloat16
F32 = jnp.float32
ANY = pl.BlockSpec(memory_space=pl.ANY)
VM = pl.BlockSpec(memory_space=pltpu.VMEM)
SM = pl.BlockSpec(memory_space=pltpu.SMEM)
VMEM_LIMIT = 60 * 1024 * 1024


def wide_place():
    w = lax.axis_index("wide")
    return lax.div(w, SIDE), lax.rem(w, SIDE)


def turn(pos, by):
    return lax.rem(pos + by, SIDE)


def ring_devices(axis, by):
    if axis == "x":
        n = lax.axis_index("narrow")
        return {"narrow": turn(lax.div(n, 2), by) * 2 + lax.rem(n, 2)}
    y, z = wide_place()
    if axis == "y":
        return {"wide": turn(y, by) * SIDE + z}
    return {"wide": y * SIDE + turn(z, by)}


def partner_device():
    n = lax.axis_index("narrow")
    return {"narrow": lax.div(n, 2) * 2 + 1 - lax.rem(n, 2)}


def greet(devices):
    barrier = pltpu.get_barrier_semaphore()
    for device in devices:
        pl.semaphore_signal(barrier, inc=1, device_id=device, device_id_type=MESH)
    pl.semaphore_wait(barrier, len(devices))


class Copies:
    def __init__(self, send_sem, recv_sem):
        self.send_sem, self.recv_sem, self.used, self.made = send_sem, recv_sem, 0, []

    def slot(self):
        self.used += 1
        return self.used - 1

    def start(self, slot, src, dst, device):
        copy = pltpu.make_async_remote_copy(
            src_ref=src,
            dst_ref=dst,
            send_sem=self.send_sem.at[slot],
            recv_sem=self.recv_sem.at[slot],
            device_id=device,
            device_id_type=MESH,
        )
        copy.start()
        self.made.append(copy)

    def arrived(self, slot, dst):
        pltpu.make_async_copy(dst, dst, self.recv_sem.at[slot]).wait()

    def sent(self):
        for copy in self.made:
            copy.wait_send()


def interleave(*parts):
    live = list(parts)
    while live:
        for part in list(live):
            try:
                next(part)
            except StopIteration:
                live.remove(part)


def gather_wide_steps(x_ref, out_ref, local_sem, copies):
    y, z = wide_place()
    depth = x_ref.shape[1] // 2
    lower, upper = pl.ds(0, depth), pl.ds(depth, depth)

    def place(half, first, second):
        if half == 0:
            return out_ref.at[first, second, 0]
        return out_ref.at[second, first, 1]

    names = (("y", "z"), ("z", "y"))
    spots = ((y, z), (z, y))
    own = pltpu.make_async_copy(x_ref, out_ref.at[y, z], local_sem)
    own.start()
    hop1 = [[copies.slot() for _ in range(4)] for _ in range(2)]
    hop2 = [[[copies.slot() for _ in range(4)] for _ in range(4)] for _ in range(2)]

    def send2(half, block, src):
        first = turn(spots[half][0], block)
        target = place(half, first, spots[half][1])
        for way, by in ((0, 1), (1, 3)):
            copies.start(hop2[half][block][way], src, target, ring_devices(names[half][1], by))

    def relay2(half, block):
        first = turn(spots[half][0], block)
        for way, by, part in ((0, 1, lower), (1, 3, upper)):
            came = place(half, first, turn(spots[half][1], 4 - by))
            copies.arrived(hop2[half][block][way], came)
            copies.start(
                hop2[half][block][2 + way], came.at[part], came.at[part], ring_devices(names[half][1], by)
            )

    for half in range(2):
        target = place(half, *spots[half])
        for way, by in ((0, 1), (1, 3)):
            copies.start(hop1[half][way], x_ref.at[half], target, ring_devices(names[half][0], by))
        send2(half, 0, x_ref.at[half])
    yield
    for half in range(2):
        for way, by, part in ((0, 1, lower), (1, 3, upper)):
            came = place(half, turn(spots[half][0], 4 - by), spots[half][1])
            copies.arrived(hop1[half][way], came)
            copies.start(hop1[half][2 + way], came.at[part], came.at[part], ring_devices(names[half][0], by))
            send2(half, 4 - by, came)
        yield
    for half in range(2):
        relay2(half, 0)
        yield
    for half in range(2):
        far = place(half, turn(spots[half][0], 2), spots[half][1])
        copies.arrived(hop1[half][2], far.at[lower])
        copies.arrived(hop1[half][3], far.at[upper])
        send2(half, 2, far)
        yield
    for block in (3, 1, 2):
        for half in range(2):
            relay2(half, block)
            yield
    for half in range(2):
        for block in (0, 3, 1, 2):
            far = place(half, turn(spots[half][0], block), turn(spots[half][1], 2))
            copies.arrived(hop2[half][block][2], far.at[lower])
            copies.arrived(hop2[half][block][3], far.at[upper])
    own.wait()


WIDE_COPIES = 40


def gather_direct_steps(x_ref, out_ref, local_sem, copies):
    y, z = wide_place()
    names = (("y", "z"), ("z", "y"))
    spots = ((y, z), (z, y))

    def place(half, first, second):
        if half == 0:
            return out_ref.at[first, second, 0]
        return out_ref.at[second, first, 1]

    own = pltpu.make_async_copy(x_ref, out_ref.at[y, z], local_sem)
    own.start()
    hop1 = [[copies.slot() for _ in range(3)] for _ in range(2)]
    hop2 = [[[copies.slot() for _ in range(3)] for _ in range(4)] for _ in range(2)]

    def send2(half, block, src):
        target = place(half, turn(spots[half][0], block), spots[half][1])
        for by in (2, 1, 3):
            copies.start(hop2[half][block][by - 1], src, target, ring_devices(names[half][1], by))

    for half in range(2):
        target = place(half, *spots[half])
        for by in (2, 1, 3):
            copies.start(hop1[half][by - 1], x_ref.at[half], target, ring_devices(names[half][0], by))
    for half in range(2):
        send2(half, 0, x_ref.at[half])
    yield
    for by in (1, 3, 2):
        for half in range(2):
            came = place(half, turn(spots[half][0], 4 - by), spots[half][1])
            copies.arrived(hop1[half][by - 1], came)
            send2(half, 4 - by, came)
        yield
    for block in range(4):
        for half in range(2):
            for by in (1, 3, 2):
                came = place(half, turn(spots[half][0], block), turn(spots[half][1], 4 - by))
                copies.arrived(hop2[half][block][by - 1], came)
    own.wait()


DIRECT_COPIES = 30


def wide_lines():
    return [ring_devices(axis, by) for axis in ("y", "z") for by in (1, 2, 3)]


def wide_neighbours():
    return [ring_devices(axis, by) for axis in ("y", "z") for by in (1, 3)]


def gather_narrow_steps(x_ref, out_ref, local_sem, copies):
    n = lax.axis_index("narrow")
    x, core = lax.div(n, 2), lax.rem(n, 2)
    depth = x_ref.shape[0] // 2
    lower, upper = pl.ds(0, depth), pl.ds(depth, depth)
    own = pltpu.make_async_copy(x_ref, out_ref.at[n], local_sem)
    own.start()
    slots = [copies.slot() for _ in range(8)]
    for way, by in ((0, 1), (1, 3)):
        copies.start(slots[way], x_ref, out_ref.at[n], ring_devices("x", by))
    copies.start(slots[4], x_ref, out_ref.at[n], partner_device())
    yield
    for way, by, part in ((0, 1, lower), (1, 3, upper)):
        came = out_ref.at[turn(x, 4 - by) * 2 + core]
        copies.arrived(slots[way], came)
        copies.start(slots[2 + way], came.at[part], came.at[part], ring_devices("x", by))
        copies.start(slots[5 + way], came, came, partner_device())
    yield
    far = out_ref.at[turn(x, 2) * 2 + core]
    copies.arrived(slots[2], far.at[lower])
    copies.arrived(slots[3], far.at[upper])
    copies.start(slots[7], far, far, partner_device())
    yield
    for slot, by in ((4, 0), (5, 3), (6, 1), (7, 2)):
        copies.arrived(slots[slot], out_ref.at[turn(x, by) * 2 + 1 - core])
    own.wait()


NARROW_COPIES = 8


def narrow_neighbours():
    return [ring_devices("x", 1), ring_devices("x", 3), partner_device()]


def unpack_steps(got_ref, x_ref, sq_ref):
    rows = x_ref.shape[1] // 8
    tokens = x_ref.shape[0]
    width = tokens // SIDE
    sums = jnp.zeros((8, tokens), F32)
    for device in range(8):
        sums = sums + got_ref[device].astype(F32)[rows:]
    squares = jnp.broadcast_to(jnp.sum(sums, axis=0, keepdims=True), (8, tokens))
    for pair in range(tokens // 128):
        block = squares[:, pair * 128 : pair * 128 + 128]
        y, z = divmod(2 * pair, SIDE)
        sq_ref[y, z] = block
        sq_ref[y, z + 1] = pltpu.roll(block, 64, 1)
    yield
    for group in range(SIDE):
        spot = pl.ds(group * width, width)
        turned = jnp.concatenate([got_ref[device, :, spot].astype(F32)[:rows] for device in range(8)], axis=0)
        x_ref[spot, :] = turned.T.astype(BF)
        yield


def flatten_steps(w_ref, out_ref, paired, flat, sem):
    came = pltpu.make_async_copy(w_ref, paired, sem.at[0])
    came.start()
    yield
    yield
    came.wait()
    for start in range(0, w_ref.shape[0], 64):

        def some(index, carry):
            spot = pl.ds(pl.multiple_of(start + index * 16, 16), 16)
            flat[0, spot] = paired[spot, 0, :]
            flat[1, spot] = paired[spot, 1, :]
            return carry

        lax.fori_loop(0, 4, some, 0)
        yield
    went = pltpu.make_async_copy(flat, out_ref, sem.at[1])
    went.start()
    yield
    went.wait()


def gather_both_kernel(
    x_ref, cache_ref, w_ref, xo_ref, sqo_ref, cacheo_ref, wo_ref,
    got, own, paired, flat, local_sem, flat_sem, send_n, recv_n, send_w, recv_w,
):
    near, far = Copies(send_n, recv_n), Copies(send_w, recv_w)
    for half in range(2):
        own[half, :, :HDIM] = cache_ref[half, :, 0, :]
        own[half, :, HDIM:] = cache_ref[half, :, 1, :]
    greet(narrow_neighbours() + wide_neighbours())

    def features():
        yield from gather_narrow_steps(x_ref, got, local_sem.at[0], near)
        yield from unpack_steps(got, xo_ref, sqo_ref)

    interleave(
        features(),
        gather_wide_steps(own, cacheo_ref, local_sem.at[1], far),
        flatten_steps(w_ref, wo_ref, paired, flat, flat_sem),
    )
    near.sent()
    far.sent()


def gather_both(x, cache, w, collective_id):
    rows, tokens = x.shape
    rows -= 8
    dma = pltpu.SemaphoreType.DMA
    flat = (w.shape[1], w.shape[0], w.shape[2])
    block = cache.shape[:2] + (2 * HDIM,)
    return pl.pallas_call(
        gather_both_kernel,
        out_shape=(
            jax.ShapeDtypeStruct((tokens, 8 * rows), BF),
            jax.ShapeDtypeStruct((SIDE, SIDE, 8, 128), F32),
            jax.ShapeDtypeStruct((SIDE, SIDE) + block, BF),
            jax.ShapeDtypeStruct(flat, BF),
        ),
        in_specs=[VM, VM, ANY],
        out_specs=(VM, VM, VM, ANY),
        scratch_shapes=[
            pltpu.VMEM((8, rows + 8, tokens), BF),
            pltpu.VMEM(block, BF),
            pltpu.VMEM(w.shape, BF),
            pltpu.VMEM(flat, BF),
            dma((2,)),
            dma((2,)),
            dma((NARROW_COPIES,)),
            dma((NARROW_COPIES,)),
            dma((WIDE_COPIES,)),
            dma((WIDE_COPIES,)),
        ],
        compiler_params=pltpu.CompilerParams(
            collective_id=collective_id, has_side_effects=True, vmem_limit_bytes=VMEM_LIMIT
        ),
        name="gather_both",
    )(x, cache, w)


SUM_COPIES = 10


def sum_narrow_body(p_ref, acc, mate, total, relay, direct, joined, copies):
    n = lax.axis_index("narrow")
    x, core = lax.div(n, 2), lax.rem(n, 2)
    width = p_ref.shape[3] // 2
    lower, upper = pl.ds(0, width), pl.ds(width, width)
    right, left = ring_devices("x", 1), ring_devices("x", 3)
    order = (2, 1, 3, 0)
    mates = {by: copies.slot() for by in order}
    slots = [copies.slot() for _ in range(6)]
    for by in order:
        copies.start(mates[by], p_ref.at[turn(x, by), 1 - core], mate.at[by], partner_device())

    def pair(by):
        copies.arrived(mates[by], mate.at[by])
        return p_ref[turn(x, by), core].astype(F32) + mate[by].astype(F32)

    total[2] = pair(2).astype(BF)
    copies.start(slots[0], total.at[2, :, lower], relay.at[0], right)
    copies.start(slots[1], total.at[2, :, upper], relay.at[1], left)
    total[1] = pair(1).astype(BF)
    copies.start(slots[2], total.at[1, :, upper], direct.at[0], right)
    total[3] = pair(3).astype(BF)
    copies.start(slots[3], total.at[3, :, lower], direct.at[1], left)
    copies.arrived(slots[0], relay.at[0])
    total[1, :, lower] = (total[1, :, lower].astype(F32) + relay[0].astype(F32)).astype(BF)
    copies.start(slots[4], total.at[1, :, lower], joined.at[0], right)
    copies.arrived(slots[1], relay.at[1])
    total[3, :, upper] = (total[3, :, upper].astype(F32) + relay[1].astype(F32)).astype(BF)
    copies.start(slots[5], total.at[3, :, upper], joined.at[1], left)
    acc[...] = pair(0)
    copies.arrived(slots[2], direct.at[0])
    acc[:, upper] += direct[0].astype(F32)
    copies.arrived(slots[3], direct.at[1])
    acc[:, lower] += direct[1].astype(F32)
    copies.arrived(slots[4], joined.at[0])
    acc[:, lower] += joined[0].astype(F32)
    copies.arrived(slots[5], joined.at[1])
    acc[:, upper] += joined[1].astype(F32)


def sum_scratch(rows, cols):
    piece = pltpu.VMEM((2, rows, cols // 2), BF)
    dma = pltpu.SemaphoreType.DMA
    return [
        pltpu.VMEM((4, 2, rows, cols), BF),
        pltpu.VMEM((rows, cols), F32),
        pltpu.VMEM((4, rows, cols), BF),
        pltpu.VMEM((4, rows, cols), BF),
        piece,
        piece,
        piece,
        dma((SUM_COPIES,)),
        dma((SUM_COPIES,)),
    ]


def split_terms(terms):
    return terms.astype(BF).reshape(4, 2, terms.shape[0] // 8, terms.shape[1])


def out_proj_kernel(
    own_ref, w_ref, x_ref, gain_ref, res_ref, xo_ref, sqo_ref, got, all_ref, block, terms, acc, mate, total, relay, direct, joined,
    sum_send, sum_recv, local_sem, wide_send, wide_recv, near_send, near_recv,
):
    rows = x_ref.shape[0]
    wide, sums, near = Copies(wide_send, wide_recv), Copies(sum_send, sum_recv), Copies(near_send, near_recv)
    greet(wide_neighbours() + narrow_neighbours())
    interleave(gather_wide_steps(own_ref, all_ref, local_sem.at[0], wide))
    depth = w_ref.shape[1]
    tokens = x_ref.shape[1] // SIDE
    for group in range(SIDE):
        values = all_ref[group].reshape(tokens, depth)
        term = lax.dot_general(w_ref[...], values, (((1,), (1,)), ((), ())), preferred_element_type=F32)
        terms[:, :, :, pl.ds(group * tokens, tokens)] = split_terms(term)
    sum_narrow_body(terms, acc, mate, total, relay, direct, joined, sums)
    residual = (x_ref[...].astype(F32) + acc[...]).astype(BF)
    res_ref[...] = residual
    widened = residual.astype(F32)
    squares = jnp.sum(widened * widened, axis=0, keepdims=True)
    high = squares.astype(BF).astype(F32)
    rest = squares - high
    middle = rest.astype(BF).astype(F32)
    low = rest - middle
    line = lax.broadcasted_iota(jnp.int32, (8, widened.shape[1]), 0)
    tail = jnp.where(line == 0, high, jnp.where(line == 1, middle, jnp.where(line == 2, low, 0.0)))
    block[...] = jnp.concatenate([widened * gain_ref[:, :1], tail], axis=0).astype(BF)
    interleave(gather_narrow_steps(block, got, local_sem.at[1], near))
    interleave(unpack_steps(got, xo_ref, sqo_ref))
    wide.sent()
    sums.sent()
    near.sent()


def out_proj(own, w, x, gain, collective_id):
    rows, tokens = x.shape
    dma = pltpu.SemaphoreType.DMA
    return pl.pallas_call(
        out_proj_kernel,
        out_shape=(
            jax.ShapeDtypeStruct((rows, tokens), BF),
            jax.ShapeDtypeStruct((tokens, 8 * rows), BF),
            jax.ShapeDtypeStruct((SIDE, SIDE, 8, 128), F32),
        ),
        in_specs=[VM] * 4,
        out_specs=(VM, VM, VM),
        scratch_shapes=[
            pltpu.VMEM((8, rows + 8, tokens), BF),
            pltpu.VMEM((SIDE, SIDE) + own.shape, BF),
            pltpu.VMEM((rows + 8, tokens), BF),
        ]
        + sum_scratch(rows, tokens)
        + [
            dma((2,)),
            dma((WIDE_COPIES,)),
            dma((WIDE_COPIES,)),
            dma((NARROW_COPIES,)),
            dma((NARROW_COPIES,)),
        ],
        compiler_params=pltpu.CompilerParams(
            collective_id=collective_id, has_side_effects=True, vmem_limit_bytes=VMEM_LIMIT
        ),
        name="out_proj",
    )(own, w, x, jnp.broadcast_to(gain.astype(F32)[:, None], (rows, 128)))


def matmul_sum_kernel(
    x_ref, w_ref, sq_ref, out_ref, sqo_ref, part, mid, got1, got2, sq1, sqm, sq2,
    send1, recv1, send2, recv2, sq_send, sq_recv,
):
    pieces, width = part.shape[0], part.shape[-1]
    rows = x_ref.shape[3]
    y, z = wide_place()
    names = (("y", "z"), ("z", "y"))
    spots = ((y, z), (z, y))
    greet([ring_devices(axis, by) for axis in ("y", "z") for by in (1, 2, 3)])
    squares = Copies(sq_send, sq_recv)
    for by in (1, 2, 3):
        squares.start(by - 1, sq_ref.at[turn(y, by)], sq1.at[by - 1], ring_devices("y", by))

    def product(half, chunk, piece):
        block = x_ref[chunk, :, 0] if half == 0 else x_ref[:, chunk, 1]
        block = block.reshape(SIDE * rows, block.shape[-1])
        columns = pl.ds(pl.multiple_of(piece * width, 128), width)
        got = jnp.dot(block, w_ref[:, columns], preferred_element_type=F32)
        return got.reshape(SIDE, rows, width)

    def copy1(piece, half, kind, way, src):
        return pltpu.make_async_remote_copy(
            src_ref=src,
            dst_ref=got1.at[piece, half, kind, way],
            send_sem=send1.at[piece, half, kind, way],
            recv_sem=recv1.at[piece, half, kind, way],
            device_id=ring_devices(names[half][0], 1 if way == 0 else 3),
            device_id_type=MESH,
        )

    def copy2(piece, half, kind, way, src):
        return pltpu.make_async_remote_copy(
            src_ref=src,
            dst_ref=got2.at[piece, half, kind, way],
            send_sem=send2.at[piece, half, kind, way],
            recv_sem=recv2.at[piece, half, kind, way],
            device_id=ring_devices(names[half][1], 1 if way == 0 else 3),
            device_id_type=MESH,
        )

    def await1(piece, half, kind, way):
        ref = got1.at[piece, half, kind, way]
        pltpu.make_async_copy(ref, ref, recv1.at[piece, half, kind, way]).wait()
        return got1[piece, half, kind, way].astype(F32)

    def await2(piece, half, kind, way):
        ref = got2.at[piece, half, kind, way]
        pltpu.make_async_copy(ref, ref, recv2.at[piece, half, kind, way]).wait()
        return got2[piece, half, kind, way].astype(F32)

    lower, upper = pl.ds(0, 2), pl.ds(2, 2)
    low, high = pl.ds(0, rows // 2), pl.ds(rows // 2, rows // 2)

    def first(piece):
        for half in range(2):
            far = turn(spots[half][0], 2)
            part[piece, half, far] = product(half, far, piece).astype(BF)
            copy1(piece, half, 0, 0, part.at[piece, half, far, lower]).start()
            copy1(piece, half, 0, 1, part.at[piece, half, far, upper]).start()
        for half in range(2):
            right, left = turn(spots[half][0], 1), turn(spots[half][0], 3)
            part[piece, half, right] = product(half, right, piece).astype(BF)
            copy1(piece, half, 1, 0, part.at[piece, half, right, upper]).start()
            part[piece, half, left] = product(half, left, piece).astype(BF)
            copy1(piece, half, 1, 1, part.at[piece, half, left, lower]).start()

    def second(piece):
        for half in range(2):
            right, left = turn(spots[half][0], 1), turn(spots[half][0], 3)
            got = await1(piece, half, 0, 0)
            part[piece, half, right, lower] = (part[piece, half, right, lower].astype(F32) + got).astype(BF)
            copy1(piece, half, 2, 0, part.at[piece, half, right, lower]).start()
            got = await1(piece, half, 0, 1)
            part[piece, half, left, upper] = (part[piece, half, left, upper].astype(F32) + got).astype(BF)
            copy1(piece, half, 2, 1, part.at[piece, half, left, upper]).start()

    def third(piece):
        for half in range(2):
            own = product(half, spots[half][0], piece)
            mid[piece, half, lower] = (
                own[:2] + await1(piece, half, 1, 1) + await1(piece, half, 2, 0)
            ).astype(BF)
            mid[piece, half, upper] = (
                own[2:] + await1(piece, half, 1, 0) + await1(piece, half, 2, 1)
            ).astype(BF)
            far, right, left = (turn(spots[half][1], by) for by in (2, 1, 3))
            copy2(piece, half, 0, 0, mid.at[piece, half, far, low]).start()
            copy2(piece, half, 0, 1, mid.at[piece, half, far, high]).start()
            copy2(piece, half, 1, 0, mid.at[piece, half, right, high]).start()
            copy2(piece, half, 1, 1, mid.at[piece, half, left, low]).start()

    def fourth(piece):
        for half in range(2):
            right, left = turn(spots[half][1], 1), turn(spots[half][1], 3)
            got = await2(piece, half, 0, 0)
            mid[piece, half, right, low] = (mid[piece, half, right, low].astype(F32) + got).astype(BF)
            copy2(piece, half, 2, 0, mid.at[piece, half, right, low]).start()
            got = await2(piece, half, 0, 1)
            mid[piece, half, left, high] = (mid[piece, half, left, high].astype(F32) + got).astype(BF)
            copy2(piece, half, 2, 1, mid.at[piece, half, left, high]).start()

    def fifth(piece):
        columns = pl.ds(pl.multiple_of(piece * width, 128), width)
        for half in range(2):
            own = spots[half][1]
            out_ref[half, low, columns] = (
                mid[piece, half, own, low].astype(F32) + await2(piece, half, 1, 1) + await2(piece, half, 2, 0)
            )
            out_ref[half, high, columns] = (
                mid[piece, half, own, high].astype(F32) + await2(piece, half, 1, 0) + await2(piece, half, 2, 1)
            )

    stages = (first, second, third, fourth, fifth)

    def step(t, carry):
        for lag, stage in enumerate(stages):
            piece = t - lag

            @pl.when((piece >= 0) & (piece < pieces))
            def _():
                stage(jnp.clip(piece, 0, pieces - 1))

        return carry

    lax.fori_loop(0, pieces + len(stages) - 1, step, 0)

    for by in (1, 2, 3):
        squares.arrived(by - 1, sq1.at[by - 1])
    sqm[...] = sq_ref[y] + sq1[0] + sq1[1] + sq1[2]
    for by in (1, 2, 3):
        squares.start(2 + by, sqm.at[turn(z, by)], sq2.at[by - 1], ring_devices("z", by))
    for by in (1, 2, 3):
        squares.arrived(2 + by, sq2.at[by - 1])
    sqo_ref[...] = sqm[z] + sq2[0] + sq2[1] + sq2[2]
    squares.sent()

    def drain(piece, carry):
        for half in range(2):
            for kind in range(3):
                for way in range(2):
                    copy1(piece, half, kind, way, part.at[piece, half, 0, lower]).wait_send()
                    copy2(piece, half, kind, way, mid.at[piece, half, 0, low]).wait_send()
        return carry

    lax.fori_loop(0, pieces, drain, 0)


def matmul_sum(x, w, sq, pieces, collective_id):
    tokens, depth = x.shape
    cols = w.shape[1]
    width = cols // pieces
    rows = tokens // (2 * SIDE * SIDE)
    out, sq_out = pl.pallas_call(
        matmul_sum_kernel,
        out_shape=(
            jax.ShapeDtypeStruct((2, rows, cols), F32),
            jax.ShapeDtypeStruct((8, 128), F32),
        ),
        in_specs=[VM, VM, VM],
        out_specs=(VM, VM),
        scratch_shapes=[
            pltpu.VMEM((pieces, 2, SIDE, SIDE, rows, width), BF),
            pltpu.VMEM((pieces, 2, SIDE, rows, width), BF),
            pltpu.VMEM((pieces, 2, 3, 2, 2, rows, width), BF),
            pltpu.VMEM((pieces, 2, 3, 2, rows // 2, width), BF),
            pltpu.VMEM((3, SIDE, 8, 128), F32),
            pltpu.VMEM((SIDE, 8, 128), F32),
            pltpu.VMEM((3, 8, 128), F32),
            pltpu.SemaphoreType.DMA((pieces, 2, 3, 2)),
            pltpu.SemaphoreType.DMA((pieces, 2, 3, 2)),
            pltpu.SemaphoreType.DMA((pieces, 2, 3, 2)),
            pltpu.SemaphoreType.DMA((pieces, 2, 3, 2)),
            pltpu.SemaphoreType.DMA((6,)),
            pltpu.SemaphoreType.DMA((6,)),
        ],
        compiler_params=pltpu.CompilerParams(
            collective_id=collective_id, has_side_effects=True, vmem_limit_bytes=VMEM_LIMIT
        ),
        name=f"matmul_sum_{collective_id}",
    )(x.reshape(SIDE, SIDE, 2, rows, depth), w, sq)
    return out, sq_out


def gate_up_kernel(
    x_ref, w_ref, sq_ref, down_ref, res_ref, final_ref, out_ref, part, mid, hid, got1, got2, sq1, sqm, sq2, inv,
    send1, recv1, send2, recv2, send3, recv3, send4, recv4, own_sem, sq_send, sq_recv,
    grown, terms, acc, mate, total, relay, direct, joined, sum_send, sum_recv,
):
    pieces, width = part.shape[0], part.shape[-1]
    wide = width // 2
    rows = x_ref.shape[3]
    y, z = wide_place()
    names = (("y", "z"), ("z", "y"))
    spots = ((y, z), (z, y))
    greet(wide_lines() + narrow_neighbours())
    squares = Copies(sq_send, sq_recv)
    for by in (1, 2, 3):
        squares.start(by - 1, sq_ref.at[turn(y, by)], sq1.at[by - 1], ring_devices("y", by))

    lower, upper = pl.ds(0, 2), pl.ds(2, 2)
    low, high = pl.ds(0, rows // 2), pl.ds(rows // 2, rows // 2)

    def product(half, chunk, piece):
        block = x_ref[chunk, :, 0] if half == 0 else x_ref[:, chunk, 1]
        block = block.reshape(SIDE * rows, block.shape[-1])
        at = pl.multiple_of(piece * wide, 128)
        gate = jnp.dot(block, w_ref[0, :, pl.ds(at, wide)], preferred_element_type=F32)
        up = jnp.dot(block, w_ref[1, :, pl.ds(at, wide)], preferred_element_type=F32)
        return jnp.concatenate([gate, up], axis=1).reshape(SIDE, rows, width)

    def remote(src, dst, send, recv, axis, way):
        return pltpu.make_async_remote_copy(
            src_ref=src,
            dst_ref=dst,
            send_sem=send,
            recv_sem=recv,
            device_id=ring_devices(axis, 1 if way == 0 else 3),
            device_id_type=MESH,
        )

    def copy1(piece, half, kind, way, src):
        spot = (piece, half, kind, way)
        return remote(src, got1.at[spot], send1.at[spot], recv1.at[spot], names[half][0], way)

    def copy2(piece, half, kind, way, src):
        spot = (piece, half, kind, way)
        return remote(src, got2.at[spot], send2.at[spot], recv2.at[spot], names[half][1], way)

    def landed(ref, sem):
        pltpu.make_async_copy(ref, ref, sem).wait()

    def await1(piece, half, kind, way):
        landed(got1.at[piece, half, kind, way], recv1.at[piece, half, kind, way])
        return got1[piece, half, kind, way].astype(F32)

    def await2(piece, half, kind, way):
        landed(got2.at[piece, half, kind, way], recv2.at[piece, half, kind, way])
        return got2[piece, half, kind, way].astype(F32)

    def place(piece, half, first, second, part_rows):
        columns = pl.ds(pl.multiple_of(piece * wide, 128), wide)
        if half == 0:
            return out_ref.at[first, second, 0, part_rows, columns]
        return out_ref.at[second, first, 1, part_rows, columns]

    whole = pl.ds(0, rows)

    def copy3(piece, half, kind, way, src, dst):
        return remote(src, dst, send3.at[piece, half, kind, way], recv3.at[piece, half, kind, way], names[half][0], way)

    def copy4(piece, half, block, kind, way, src, dst):
        spot = (piece, half, block, kind, way)
        return remote(src, dst, send4.at[spot], recv4.at[spot], names[half][1], way)

    def send4_whole(piece, half, block, src):
        dst = place(piece, half, turn(spots[half][0], block), spots[half][1], whole)
        for way in range(2):
            copy4(piece, half, block, 0, way, src, dst).start()

    def relay4(piece, half, block):
        first = turn(spots[half][0], block)
        for way, by, part_rows in ((0, 3, low), (1, 1, high)):
            second = turn(spots[half][1], by)
            landed(place(piece, half, first, second, whole), recv4.at[piece, half, block, 0, way])
            came = place(piece, half, first, second, part_rows)
            copy4(piece, half, block, 1, way, came, came).start()

    def stage1(piece):
        for half in range(2):
            far = turn(spots[half][0], 2)
            part[piece, half, far] = product(half, far, piece).astype(BF)
            copy1(piece, half, 0, 0, part.at[piece, half, far, lower]).start()
            copy1(piece, half, 0, 1, part.at[piece, half, far, upper]).start()
        for half in range(2):
            right, left = turn(spots[half][0], 1), turn(spots[half][0], 3)
            part[piece, half, right] = product(half, right, piece).astype(BF)
            copy1(piece, half, 1, 0, part.at[piece, half, right, upper]).start()
            part[piece, half, left] = product(half, left, piece).astype(BF)
            copy1(piece, half, 1, 1, part.at[piece, half, left, lower]).start()

    def stage2(piece):
        for half in range(2):
            right, left = turn(spots[half][0], 1), turn(spots[half][0], 3)
            got = await1(piece, half, 0, 0)
            part[piece, half, right, lower] = (part[piece, half, right, lower].astype(F32) + got).astype(BF)
            copy1(piece, half, 2, 0, part.at[piece, half, right, lower]).start()
            got = await1(piece, half, 0, 1)
            part[piece, half, left, upper] = (part[piece, half, left, upper].astype(F32) + got).astype(BF)
            copy1(piece, half, 2, 1, part.at[piece, half, left, upper]).start()

    def stage3(piece):
        for half in range(2):
            own = product(half, spots[half][0], piece)
            mid[piece, half, lower] = (
                own[:2] + await1(piece, half, 1, 1) + await1(piece, half, 2, 0)
            ).astype(BF)
            mid[piece, half, upper] = (
                own[2:] + await1(piece, half, 1, 0) + await1(piece, half, 2, 1)
            ).astype(BF)
            far, right, left = (turn(spots[half][1], by) for by in (2, 1, 3))
            copy2(piece, half, 0, 0, mid.at[piece, half, far, low]).start()
            copy2(piece, half, 0, 1, mid.at[piece, half, far, high]).start()
            copy2(piece, half, 1, 0, mid.at[piece, half, right, high]).start()
            copy2(piece, half, 1, 1, mid.at[piece, half, left, low]).start()

    def stage4(piece):
        for half in range(2):
            right, left = turn(spots[half][1], 1), turn(spots[half][1], 3)
            got = await2(piece, half, 0, 0)
            mid[piece, half, right, low] = (mid[piece, half, right, low].astype(F32) + got).astype(BF)
            copy2(piece, half, 2, 0, mid.at[piece, half, right, low]).start()
            got = await2(piece, half, 0, 1)
            mid[piece, half, left, high] = (mid[piece, half, left, high].astype(F32) + got).astype(BF)
            copy2(piece, half, 2, 1, mid.at[piece, half, left, high]).start()

    def activate(sums, factor):
        sums = jnp.where(factor > 0, sums * factor, 0.0)
        gate, up = sums[:, :wide], sums[:, wide:]
        return (gate / (1.0 + jnp.exp(-gate)) * up).astype(BF)

    def stage5(piece):
        for half in range(2):
            own = spots[half][1]
            hid[piece, half, low] = activate(
                mid[piece, half, own, low].astype(F32) + await2(piece, half, 1, 1) + await2(piece, half, 2, 0),
                inv[half, low][:, :1],
            )
            hid[piece, half, high] = activate(
                mid[piece, half, own, high].astype(F32) + await2(piece, half, 1, 0) + await2(piece, half, 2, 1),
                inv[half, high][:, :1],
            )
            mine = hid.at[piece, half]
            dst = place(piece, half, *spots[half], whole)
            pltpu.make_async_copy(mine, dst, own_sem.at[piece, half]).start()
            for way in range(2):
                copy3(piece, half, 0, way, mine, dst).start()
            send4_whole(piece, half, 0, mine)

    def stage6(piece):
        for half in range(2):
            for way, by, part_rows in ((0, 3, low), (1, 1, high)):
                first = turn(spots[half][0], by)
                landed(place(piece, half, first, spots[half][1], whole), recv3.at[piece, half, 0, way])
                came = place(piece, half, first, spots[half][1], part_rows)
                copy3(piece, half, 1, way, came, came).start()
                send4_whole(piece, half, by, place(piece, half, first, spots[half][1], whole))
        for half in range(2):
            relay4(piece, half, 0)

    def stage7(piece):
        for half in range(2):
            far = turn(spots[half][0], 2)
            landed(place(piece, half, far, spots[half][1], low), recv3.at[piece, half, 1, 0])
            landed(place(piece, half, far, spots[half][1], high), recv3.at[piece, half, 1, 1])
            send4_whole(piece, half, 2, place(piece, half, far, spots[half][1], whole))
        for half in range(2):
            relay4(piece, half, 3)
            relay4(piece, half, 1)

    def stage8(piece):
        for half in range(2):
            relay4(piece, half, 2)

    def stage9(piece):
        for half in range(2):
            for block in range(4):
                first, second = turn(spots[half][0], block), turn(spots[half][1], 2)
                landed(place(piece, half, first, second, low), recv4.at[piece, half, block, 1, 0])
                landed(place(piece, half, first, second, high), recv4.at[piece, half, block, 1, 1])
            mine = place(piece, half, *spots[half], whole)
            landed(mine, own_sem.at[piece, half])
            for way in range(2):
                for kind in range(3):
                    copy1(piece, half, kind, way, part.at[piece, half, 0, lower]).wait_send()
                    copy2(piece, half, kind, way, mid.at[piece, half, 0, low]).wait_send()
                for kind, part_rows in ((0, whole), (1, low)):
                    ref = place(piece, half, *spots[half], part_rows)
                    copy3(piece, half, kind, way, ref, ref).wait_send()
                    for block in range(4):
                        copy4(piece, half, block, kind, way, ref, ref).wait_send()
        columns = pl.ds(pl.multiple_of(piece * wide, 128), wide)
        tokens = 2 * SIDE * rows
        for group in range(SIDE):
            values = out_ref[group, :, :, :, columns].reshape(tokens, wide)
            got = lax.dot_general(
                down_ref[:, columns], values, (((1,), (1,)), ((), ())), preferred_element_type=F32
            )
            spot = pl.ds(group * tokens, tokens)
            grown[:, spot] += got

    stages = (stage1, stage2, stage3, stage4, stage5, stage6, stage7, stage8, stage9)

    def step(t, carry):
        for lag, stage in enumerate(stages):
            piece = t - lag

            @pl.when((piece >= 0) & (piece < pieces))
            def _():
                stage(jnp.clip(piece, 0, pieces - 1))

        return carry

    grown[...] = jnp.zeros_like(grown)
    lax.fori_loop(0, 3, step, 0)

    for by in (1, 2, 3):
        squares.arrived(by - 1, sq1.at[by - 1])
    sqm[...] = sq_ref[y] + sq1[0] + sq1[1] + sq1[2]
    for by in (1, 2, 3):
        squares.start(2 + by, sqm.at[turn(z, by)], sq2.at[by - 1], ring_devices("z", by))
    lax.fori_loop(3, 4, step, 0)
    for by in (1, 2, 3):
        squares.arrived(2 + by, sq2.at[by - 1])
    everything = (sqm[z] + sq2[0] + sq2[1] + sq2[2])[:1]
    factor = lax.rsqrt(everything / D + epsilon)
    token = lax.broadcasted_iota(jnp.int32, (2 * rows, 128), 0)
    lane = lax.broadcasted_iota(jnp.int32, (2 * rows, 128), 1)
    column = jnp.sum(jnp.where(token == lane, factor, 0.0), axis=1, keepdims=True)
    inv[...] = jnp.broadcast_to(column, (2 * rows, 128)).reshape(2, rows, 128)
    lax.fori_loop(4, pieces + len(stages) - 1, step, 0)
    squares.sent()
    sums = Copies(sum_send, sum_recv)
    terms[...] = split_terms(grown[...])
    sum_narrow_body(terms, acc, mate, total, relay, direct, joined, sums)
    final_ref[...] = (res_ref[...].astype(F32) + acc[...]).astype(BF)
    sums.sent()


def gate_up(x, w, sq, down, residual, pieces, collective_id):
    tokens, depth = x.shape
    units = w.shape[2]
    width = 2 * units // pieces
    rows = tokens // (2 * SIDE * SIDE)
    dma = pltpu.SemaphoreType.DMA
    return pl.pallas_call(
        gate_up_kernel,
        out_shape=jax.ShapeDtypeStruct(residual.shape, BF),
        in_specs=[VM] * 5,
        out_specs=VM,
        scratch_shapes=[
            pltpu.VMEM((SIDE, SIDE, 2, rows, units), BF),
            pltpu.VMEM((pieces, 2, SIDE, SIDE, rows, width), BF),
            pltpu.VMEM((pieces, 2, SIDE, rows, width), BF),
            pltpu.VMEM((pieces, 2, rows, width // 2), BF),
            pltpu.VMEM((pieces, 2, 3, 2, 2, rows, width), BF),
            pltpu.VMEM((pieces, 2, 3, 2, rows // 2, width), BF),
            pltpu.VMEM((3, SIDE, 8, 128), F32),
            pltpu.VMEM((SIDE, 8, 128), F32),
            pltpu.VMEM((3, 8, 128), F32),
            pltpu.VMEM((2, rows, 128), F32),
            dma((pieces, 2, 3, 2)),
            dma((pieces, 2, 3, 2)),
            dma((pieces, 2, 3, 2)),
            dma((pieces, 2, 3, 2)),
            dma((pieces, 2, 2, 2)),
            dma((pieces, 2, 2, 2)),
            dma((pieces, 2, 4, 2, 2)),
            dma((pieces, 2, 4, 2, 2)),
            dma((pieces, 2)),
            dma((6,)),
            dma((6,)),
            pltpu.VMEM((down.shape[0], tokens), F32),
        ]
        + sum_scratch(*residual.shape),
        compiler_params=pltpu.CompilerParams(
            collective_id=collective_id, has_side_effects=True, vmem_limit_bytes=VMEM_LIMIT
        ),
        name="gate_up",
    )(x.reshape(SIDE, SIDE, 2, rows, depth), w, sq, down, residual)


CHUNK = 8


def attend_kernel(
    lengths_ref, sums_in_ref, sq_ref, cos_ref, sin_ref, cache_ref, out_ref, sums_ref, fresh_ref,
    lines, q_ref, own_ref, rows_out, rows_sum, span_ref, local_sem, send_sem, recv_sem,
):
    scale = HDIM ** (-0.5)
    rows = q_ref.shape[1]
    per = own_ref.shape[1]
    tokens = R * per
    factor = lax.rsqrt(sq_ref[:1] / D + epsilon)
    token = lax.broadcasted_iota(jnp.int32, (tokens, 128), 0)
    lane = lax.broadcasted_iota(jnp.int32, (tokens, 128), 1)
    column = jnp.sum(jnp.where(token == lane, factor, 0.0), axis=1, keepdims=True)

    def slot_of(index, turned):
        got = sums_in_ref[:, :, index * HDIM : index * HDIM + HDIM].reshape(tokens, HDIM)
        got = jnp.where(column > 0, got * column, 0.0)
        if turned:
            got = got * cos_ref[...] + pltpu.roll(got, HDIM // 2, 1) * sin_ref[...]
        lines[index] = got
        return got.astype(BF)

    fresh_ref[:, :HDIM] = slot_of(GROUP, True)
    fresh_ref[:, HDIM:] = slot_of(GROUP + 1, False)
    for request in range(R):
        mine = pl.ds(request, per, stride=R)
        own_ref[request, :, :HDIM] = lines[GROUP, mine, :].astype(BF)
        own_ref[request, :, HDIM:] = lines[GROUP + 1, mine, :].astype(BF)
    block = cache_ref.shape[2] * CHUNK
    spot = lax.axis_index("wide")
    copies = Copies(send_sem, recv_sem)
    greet(wide_lines())
    gather = gather_direct_steps(own_ref, span_ref, local_sem, copies)
    next(gather)
    for index in range(GROUP):
        slot_of(index, True)
        for request in range(R):
            q_ref[request, index * per : index * per + per] = lines[index, pl.ds(request, per, stride=R), :].astype(BF)
    queries = [q_ref[request] for request in range(R)]

    def absorb(running, q, keys, values, allowed):
        peak, weight_sum, gathered = running
        scores = lax.dot_general(q, keys, (((1,), (1,)), ((), ())), preferred_element_type=F32) * scale
        scores = jnp.where(allowed(scores.shape), scores, floor_score)
        new_peak = jnp.maximum(peak, jnp.max(scores, axis=1, keepdims=True))
        weights = jnp.exp(scores - new_peak)
        factor = jnp.exp(peak - new_peak)
        weight_sum = weight_sum * factor + jnp.sum(weights, axis=1, keepdims=True)
        gathered = gathered * factor + jnp.dot(weights.astype(BF), values, preferred_element_type=F32)
        return new_peak, weight_sum, gathered

    def own_keys(shape):
        key = lax.broadcasted_iota(jnp.int32, shape, 1)
        row = lax.broadcasted_iota(jnp.int32, shape, 0)
        return key <= spot * per + lax.rem(row, per)

    running = [
        (
            jnp.full((rows, 1), floor_score, F32),
            jnp.zeros((rows, 1), F32),
            jnp.zeros((rows, HDIM), F32),
        )
        for _ in range(R)
    ]
    for index in range(cache_ref.shape[0] // CHUNK):
        for request in range(R):
            pair = cache_ref[pl.ds(index * CHUNK, CHUNK), request].reshape(block, 2 * HDIM)
            running[request] = absorb(
                running[request],
                queries[request],
                pair[:, :HDIM],
                pair[:, HDIM:],
                lambda shape: index * block + lax.broadcasted_iota(jnp.int32, shape, 1) < lengths_ref[request],
            )
        if index >= 2:
            next(gather, None)
    interleave(gather)
    for request in range(R):
        span = span_ref[:, :, request].reshape(SIDE * SIDE * per, 2 * HDIM)
        peak, weight_sum, gathered = absorb(
            running[request], queries[request], span[:, :HDIM], span[:, HDIM:], own_keys
        )
        gathered = gathered / weight_sum
        logs = peak + jnp.log(weight_sum)
        mine = pl.ds(request, per, stride=R)
        line = jnp.zeros((per, 128), F32)
        spot_of = lax.broadcasted_iota(jnp.int32, (per, 128), 1)
        for index in range(GROUP):
            rows_out[index, mine, :] = gathered[index * per : index * per + per]
            line = line + jnp.where(spot_of == index, logs[index * per : index * per + per], 0.0)
        rows_sum[mine, :] = line
    for index in range(GROUP):
        out_ref[:, :, index * HDIM : index * HDIM + HDIM] = rows_out[index].astype(BF).reshape(2, per, HDIM)
    sums_ref[...] = rows_sum[...]
    copies.sent()


def attend(lengths, sums, sq, cosine, sine, cache, collective_id):
    per = sums.shape[1]
    tokens = R * per
    dma = pltpu.SemaphoreType.DMA
    return pl.pallas_call(
        attend_kernel,
        out_shape=(
            jax.ShapeDtypeStruct((2, per, GROUP * HDIM), BF),
            jax.ShapeDtypeStruct((tokens, 128), F32),
            jax.ShapeDtypeStruct((tokens, 2 * HDIM), BF),
        ),
        in_specs=[SM] + [VM] * 5,
        out_specs=(VM, VM, VM),
        scratch_shapes=[
            pltpu.VMEM((GROUP + 2, tokens, HDIM), F32),
            pltpu.VMEM((R, GROUP * per, HDIM), BF),
            pltpu.VMEM((R, per, 2 * HDIM), BF),
            pltpu.VMEM((GROUP, tokens, HDIM), F32),
            pltpu.VMEM((tokens, 128), F32),
            pltpu.VMEM((SIDE, SIDE, R, per, 2 * HDIM), BF),
            dma,
            dma((DIRECT_COPIES,)),
            dma((DIRECT_COPIES,)),
        ],
        compiler_params=pltpu.CompilerParams(
            collective_id=collective_id, has_side_effects=True, vmem_limit_bytes=VMEM_LIMIT
        ),
        name="attend",
    )(lengths, sums, sq, cosine, sine, cache)


def token_angles(lengths, offsets, first_token, row_count, dim_size):
    token_ids = first_token + jnp.arange(row_count, dtype=jnp.int32)
    request_ids = token_ids % R
    start_pos = offsets + lengths
    matches = request_ids[:, None] == jnp.arange(start_pos.shape[0], dtype=jnp.int32)[None, :]
    chosen = jnp.sum(jnp.where(matches, start_pos[None, :], 0), axis=1)
    position = (chosen + token_ids // R).astype(jnp.float32)
    inverse = rope_base ** (-(jnp.arange(dim_size // 2, dtype=jnp.float32) * 2.0) / dim_size)
    return position[:, None] * inverse[None, :]


def to_send(flipped, gain):
    widened = flipped.astype(F32)
    squares = jnp.sum(widened * widened, axis=0, keepdims=True)
    high = lax.reduce_precision(squares, 8, 7)
    rest = squares - high
    middle = lax.reduce_precision(rest, 8, 7)
    low = rest - middle
    scaled = widened * gain.astype(F32)[:, None]
    pad = jnp.zeros((5, flipped.shape[1]), F32)
    return jnp.concatenate([scaled, high, middle, low, pad], axis=0).astype(BF)


def local(
    hidden_in, attn_gain, w_qkv, cache_kv, lengths, offsets, w_out, mlp_gain, w_gate_up, w_down
):
    all_tokens, features = hidden_in.shape
    per_device = all_tokens // lax.axis_size("wide")
    first_token = lax.axis_index("wide") * per_device
    flipped = hidden_in.T
    positions = cache_kv.shape[1]
    cache = cache_kv.reshape(R, positions, 2, HDIM)
    scaled, squares, cache_all, flat_gate_up = gather_both(to_send(flipped, attn_gain), cache, w_gate_up, 1)
    projected, squares = matmul_sum(scaled, w_qkv.reshape(w_qkv.shape[0], -1), squares, 1, 2)
    angles = token_angles(lengths, offsets, first_token, per_device, HDIM)
    cosine, sine = jnp.cos(angles), jnp.sin(angles)
    attended, sums, fresh = attend(
        lengths,
        projected,
        squares,
        jnp.concatenate([cosine, cosine], axis=1),
        jnp.concatenate([-sine, sine], axis=1),
        cache_all.reshape(SIDE * SIDE, R, positions, 2 * HDIM),
        3,
    )
    softmax_sums = sums[:, :GROUP]
    new_cache = fresh.reshape(per_device, 1, 2, HDIM)
    residual, scaled, squares = out_proj(attended, w_out.T, flipped, mlp_gain, 5)
    hidden_out = gate_up(scaled, flat_gate_up, squares, w_down.T, residual, 2, 7).T
    return (hidden_out, softmax_sums, new_cache)


def solution(mesh):
    return jax.shard_map(
        local,
        mesh=mesh,
        in_specs=(
            P(None, ("wide", "narrow")),
            P(("wide", "narrow")),
            P("wide", "narrow", None),
            P(None, "wide", "narrow", None, None),
            P(),
            P(),
            P("narrow", "wide"),
            P(("wide", "narrow")),
            P("wide", None, "narrow"),
            P("narrow", "wide"),
        ),
        out_specs=(
            P(None, ("wide", "narrow")),
            P("wide", "narrow"),
            P("wide", "narrow", None, None),
        ),
        check_vma=False,
    )
```

```python
import functools

import jax
import jax.numpy as jnp
from jax import lax
from jax.experimental import pallas as pl
from jax.experimental.pallas import tpu as pltpu
from jax.sharding import PartitionSpec as P

D = 7168
HDIM = 128
R = 2
GROUP = 7
SIDE = 4

epsilon = 1e-05
rope_base = 5000000.0
floor_score = -1e30

MESH = pl.DeviceIdType.MESH
BF = jnp.bfloat16
F32 = jnp.float32
ANY = pl.BlockSpec(memory_space=pl.ANY)
VM = pl.BlockSpec(memory_space=pltpu.VMEM)
SM = pl.BlockSpec(memory_space=pltpu.SMEM)
VMEM_LIMIT = 60 * 1024 * 1024


def wide_place():
    w = lax.axis_index("wide")
    return lax.div(w, SIDE), lax.rem(w, SIDE)


def turn(pos, by):
    return lax.rem(pos + by, SIDE)


def ring_devices(axis, by):
    if axis == "x":
        n = lax.axis_index("narrow")
        return {"narrow": turn(lax.div(n, 2), by) * 2 + lax.rem(n, 2)}
    y, z = wide_place()
    if axis == "y":
        return {"wide": turn(y, by) * SIDE + z}
    return {"wide": y * SIDE + turn(z, by)}


def partner_device():
    n = lax.axis_index("narrow")
    return {"narrow": lax.div(n, 2) * 2 + 1 - lax.rem(n, 2)}


def greet(devices):
    barrier = pltpu.get_barrier_semaphore()
    for device in devices:
        pl.semaphore_signal(barrier, inc=1, device_id=device, device_id_type=MESH)
    pl.semaphore_wait(barrier, len(devices))


class Copies:
    def __init__(self, send_sem, recv_sem):
        self.send_sem, self.recv_sem, self.used, self.made = send_sem, recv_sem, 0, []

    def slot(self):
        self.used += 1
        return self.used - 1

    def start(self, slot, src, dst, device):
        copy = pltpu.make_async_remote_copy(
            src_ref=src,
            dst_ref=dst,
            send_sem=self.send_sem.at[slot],
            recv_sem=self.recv_sem.at[slot],
            device_id=device,
            device_id_type=MESH,
        )
        copy.start()
        self.made.append(copy)

    def arrived(self, slot, dst):
        pltpu.make_async_copy(dst, dst, self.recv_sem.at[slot]).wait()

    def sent(self):
        for copy in self.made:
            copy.wait_send()


def interleave(*parts):
    live = list(parts)
    while live:
        for part in list(live):
            try:
                next(part)
            except StopIteration:
                live.remove(part)


def gather_wide_steps(x_ref, out_ref, local_sem, copies):
    y, z = wide_place()
    depth = x_ref.shape[1] // 2
    lower, upper = pl.ds(0, depth), pl.ds(depth, depth)

    def place(half, first, second):
        if half == 0:
            return out_ref.at[first, second, 0]
        return out_ref.at[second, first, 1]

    names = (("y", "z"), ("z", "y"))
    spots = ((y, z), (z, y))
    own = pltpu.make_async_copy(x_ref, out_ref.at[y, z], local_sem)
    own.start()
    hop1 = [[copies.slot() for _ in range(4)] for _ in range(2)]
    hop2 = [[[copies.slot() for _ in range(4)] for _ in range(4)] for _ in range(2)]

    def send2(half, block, src):
        first = turn(spots[half][0], block)
        target = place(half, first, spots[half][1])
        for way, by in ((0, 1), (1, 3)):
            copies.start(hop2[half][block][way], src, target, ring_devices(names[half][1], by))

    def relay2(half, block):
        first = turn(spots[half][0], block)
        for way, by, part in ((0, 1, lower), (1, 3, upper)):
            came = place(half, first, turn(spots[half][1], 4 - by))
            copies.arrived(hop2[half][block][way], came)
            copies.start(
                hop2[half][block][2 + way], came.at[part], came.at[part], ring_devices(names[half][1], by)
            )

    for half in range(2):
        target = place(half, *spots[half])
        for way, by in ((0, 1), (1, 3)):
            copies.start(hop1[half][way], x_ref.at[half], target, ring_devices(names[half][0], by))
        send2(half, 0, x_ref.at[half])
    yield
    for half in range(2):
        for way, by, part in ((0, 1, lower), (1, 3, upper)):
            came = place(half, turn(spots[half][0], 4 - by), spots[half][1])
            copies.arrived(hop1[half][way], came)
            copies.start(hop1[half][2 + way], came.at[part], came.at[part], ring_devices(names[half][0], by))
            send2(half, 4 - by, came)
        yield
    for half in range(2):
        relay2(half, 0)
        yield
    for half in range(2):
        far = place(half, turn(spots[half][0], 2), spots[half][1])
        copies.arrived(hop1[half][2], far.at[lower])
        copies.arrived(hop1[half][3], far.at[upper])
        send2(half, 2, far)
        yield
    for block in (3, 1, 2):
        for half in range(2):
            relay2(half, block)
            yield
    for half in range(2):
        for block in (0, 3, 1, 2):
            far = place(half, turn(spots[half][0], block), turn(spots[half][1], 2))
            copies.arrived(hop2[half][block][2], far.at[lower])
            copies.arrived(hop2[half][block][3], far.at[upper])
    own.wait()


WIDE_COPIES = 40


def gather_direct_steps(x_ref, out_ref, local_sem, copies):
    y, z = wide_place()
    names = (("y", "z"), ("z", "y"))
    spots = ((y, z), (z, y))

    def place(half, first, second):
        if half == 0:
            return out_ref.at[first, second, 0]
        return out_ref.at[second, first, 1]

    own = pltpu.make_async_copy(x_ref, out_ref.at[y, z], local_sem)
    own.start()
    hop1 = [[copies.slot() for _ in range(3)] for _ in range(2)]
    hop2 = [[[copies.slot() for _ in range(3)] for _ in range(4)] for _ in range(2)]

    def send2(half, block, src):
        target = place(half, turn(spots[half][0], block), spots[half][1])
        for by in (2, 1, 3):
            copies.start(hop2[half][block][by - 1], src, target, ring_devices(names[half][1], by))

    for half in range(2):
        target = place(half, *spots[half])
        for by in (2, 1, 3):
            copies.start(hop1[half][by - 1], x_ref.at[half], target, ring_devices(names[half][0], by))
    for half in range(2):
        send2(half, 0, x_ref.at[half])
    yield
    for by in (1, 3, 2):
        for half in range(2):
            came = place(half, turn(spots[half][0], 4 - by), spots[half][1])
            copies.arrived(hop1[half][by - 1], came)
            send2(half, 4 - by, came)
        yield
    for block in range(4):
        for half in range(2):
            for by in (1, 3, 2):
                came = place(half, turn(spots[half][0], block), turn(spots[half][1], 4 - by))
                copies.arrived(hop2[half][block][by - 1], came)
    own.wait()


DIRECT_COPIES = 30


def wide_lines():
    return [ring_devices(axis, by) for axis in ("y", "z") for by in (1, 2, 3)]


def wide_neighbours():
    return [ring_devices(axis, by) for axis in ("y", "z") for by in (1, 3)]


def gather_narrow_steps(x_ref, out_ref, local_sem, copies):
    n = lax.axis_index("narrow")
    x, core = lax.div(n, 2), lax.rem(n, 2)
    depth = x_ref.shape[0] // 2
    lower, upper = pl.ds(0, depth), pl.ds(depth, depth)
    own = pltpu.make_async_copy(x_ref, out_ref.at[n], local_sem)
    own.start()
    slots = [copies.slot() for _ in range(8)]
    for way, by in ((0, 1), (1, 3)):
        copies.start(slots[way], x_ref, out_ref.at[n], ring_devices("x", by))
    copies.start(slots[4], x_ref, out_ref.at[n], partner_device())
    yield
    for way, by, part in ((0, 1, lower), (1, 3, upper)):
        came = out_ref.at[turn(x, 4 - by) * 2 + core]
        copies.arrived(slots[way], came)
        copies.start(slots[2 + way], came.at[part], came.at[part], ring_devices("x", by))
        copies.start(slots[5 + way], came, came, partner_device())
    yield
    far = out_ref.at[turn(x, 2) * 2 + core]
    copies.arrived(slots[2], far.at[lower])
    copies.arrived(slots[3], far.at[upper])
    copies.start(slots[7], far, far, partner_device())
    yield
    for slot, by in ((4, 0), (5, 3), (6, 1), (7, 2)):
        copies.arrived(slots[slot], out_ref.at[turn(x, by) * 2 + 1 - core])
    own.wait()


NARROW_COPIES = 8


def narrow_neighbours():
    return [ring_devices("x", 1), ring_devices("x", 3), partner_device()]


def to_send(flipped, gain):
    widened = flipped.astype(F32)
    squares = jnp.sum(widened * widened, axis=0, keepdims=True)
    high = squares.astype(BF).astype(F32)
    rest = squares - high
    middle = rest.astype(BF).astype(F32)
    low = rest - middle
    line = lax.broadcasted_iota(jnp.int32, (8, widened.shape[1]), 0)
    tail = jnp.where(line == 0, high, jnp.where(line == 1, middle, jnp.where(line == 2, low, 0.0)))
    return jnp.concatenate([widened * gain, tail], axis=0).astype(BF)


def spread(gain):
    return jnp.broadcast_to(gain.astype(F32)[:, None], (gain.shape[0], 128))


def unpack_steps(got_ref, x_ref, sq_ref):
    rows = x_ref.shape[1] // 8
    tokens = x_ref.shape[0]
    width = tokens // SIDE
    sums = jnp.zeros((8, tokens), F32)
    for device in range(8):
        sums = sums + got_ref[device].astype(F32)[rows:]
    squares = jnp.broadcast_to(jnp.sum(sums, axis=0, keepdims=True), (8, tokens))
    for pair in range(tokens // 128):
        block = squares[:, pair * 128 : pair * 128 + 128]
        y, z = divmod(2 * pair, SIDE)
        sq_ref[y, z] = block
        sq_ref[y, z + 1] = pltpu.roll(block, 64, 1)
    yield
    for group in range(SIDE):
        spot = pl.ds(group * width, width)
        turned = jnp.concatenate([got_ref[device, :, spot].astype(F32)[:rows] for device in range(8)], axis=0)
        x_ref[spot, :] = turned.T.astype(BF)
        yield


def flatten_steps(w_ref, out_ref, paired, flat, sem):
    came = pltpu.make_async_copy(w_ref, paired, sem.at[0])
    came.start()
    yield
    yield
    came.wait()
    for start in range(0, w_ref.shape[0], 64):

        def some(index, carry):
            spot = pl.ds(pl.multiple_of(start + index * 16, 16), 16)
            flat[0, spot] = paired[spot, 0, :]
            flat[1, spot] = paired[spot, 1, :]
            return carry

        lax.fori_loop(0, 4, some, 0)
        yield
    went = pltpu.make_async_copy(flat, out_ref, sem.at[1])
    went.start()
    yield
    went.wait()


def gather_both_kernel(
    x_ref, gain_ref, cache_ref, w_ref, xo_ref, sqo_ref, cacheo_ref, wo_ref,
    block, got, own, paired, flat, local_sem, flat_sem, send_n, recv_n, send_w, recv_w,
):
    near, far = Copies(send_n, recv_n), Copies(send_w, recv_w)
    block[...] = to_send(x_ref[...], gain_ref[:, :1])
    for half in range(2):
        own[half, :, :HDIM] = cache_ref[half, :, 0, :]
        own[half, :, HDIM:] = cache_ref[half, :, 1, :]
    greet(narrow_neighbours() + wide_neighbours())

    def features():
        yield from gather_narrow_steps(block, got, local_sem.at[0], near)
        yield from unpack_steps(got, xo_ref, sqo_ref)

    interleave(
        features(),
        gather_wide_steps(own, cacheo_ref, local_sem.at[1], far),
        flatten_steps(w_ref, wo_ref, paired, flat, flat_sem),
    )
    near.sent()
    far.sent()


def gather_both(x, gain, cache, w, collective_id):
    rows, tokens = x.shape
    dma = pltpu.SemaphoreType.DMA
    flat = (w.shape[1], w.shape[0], w.shape[2])
    pair = cache.shape[:2] + (2 * HDIM,)
    return pl.pallas_call(
        gather_both_kernel,
        out_shape=(
            jax.ShapeDtypeStruct((tokens, 8 * rows), BF),
            jax.ShapeDtypeStruct((SIDE, SIDE, 8, 128), F32),
            jax.ShapeDtypeStruct((SIDE, SIDE) + pair, BF),
            jax.ShapeDtypeStruct(flat, BF),
        ),
        in_specs=[VM, VM, VM, ANY],
        out_specs=(VM, VM, VM, ANY),
        scratch_shapes=[
            pltpu.VMEM((rows + 8, tokens), BF),
            pltpu.VMEM((8, rows + 8, tokens), BF),
            pltpu.VMEM(pair, BF),
            pltpu.VMEM(w.shape, BF),
            pltpu.VMEM(flat, BF),
            dma((2,)),
            dma((2,)),
            dma((NARROW_COPIES,)),
            dma((NARROW_COPIES,)),
            dma((WIDE_COPIES,)),
            dma((WIDE_COPIES,)),
        ],
        compiler_params=pltpu.CompilerParams(
            collective_id=collective_id, has_side_effects=True, vmem_limit_bytes=VMEM_LIMIT
        ),
        name="gather_both",
    )(x, spread(gain), cache, w)


SUM_COPIES = 10


def sum_narrow_body(p_ref, acc, mate, total, relay, direct, joined, copies):
    n = lax.axis_index("narrow")
    x, core = lax.div(n, 2), lax.rem(n, 2)
    width = p_ref.shape[3] // 2
    lower, upper = pl.ds(0, width), pl.ds(width, width)
    right, left = ring_devices("x", 1), ring_devices("x", 3)
    order = (2, 1, 3, 0)
    mates = {by: copies.slot() for by in order}
    slots = [copies.slot() for _ in range(6)]
    for by in order:
        copies.start(mates[by], p_ref.at[turn(x, by), 1 - core], mate.at[by], partner_device())

    def pair(by):
        copies.arrived(mates[by], mate.at[by])
        return p_ref[turn(x, by), core].astype(F32) + mate[by].astype(F32)

    total[2] = pair(2).astype(BF)
    copies.start(slots[0], total.at[2, :, lower], relay.at[0], right)
    copies.start(slots[1], total.at[2, :, upper], relay.at[1], left)
    total[1] = pair(1).astype(BF)
    copies.start(slots[2], total.at[1, :, upper], direct.at[0], right)
    total[3] = pair(3).astype(BF)
    copies.start(slots[3], total.at[3, :, lower], direct.at[1], left)
    copies.arrived(slots[0], relay.at[0])
    total[1, :, lower] = (total[1, :, lower].astype(F32) + relay[0].astype(F32)).astype(BF)
    copies.start(slots[4], total.at[1, :, lower], joined.at[0], right)
    copies.arrived(slots[1], relay.at[1])
    total[3, :, upper] = (total[3, :, upper].astype(F32) + relay[1].astype(F32)).astype(BF)
    copies.start(slots[5], total.at[3, :, upper], joined.at[1], left)
    acc[...] = pair(0)
    copies.arrived(slots[2], direct.at[0])
    acc[:, upper] += direct[0].astype(F32)
    copies.arrived(slots[3], direct.at[1])
    acc[:, lower] += direct[1].astype(F32)
    copies.arrived(slots[4], joined.at[0])
    acc[:, lower] += joined[0].astype(F32)
    copies.arrived(slots[5], joined.at[1])
    acc[:, upper] += joined[1].astype(F32)


def sum_scratch(rows, cols):
    piece = pltpu.VMEM((2, rows, cols // 2), BF)
    dma = pltpu.SemaphoreType.DMA
    return [
        pltpu.VMEM((4, 2, rows, cols), BF),
        pltpu.VMEM((rows, cols), F32),
        pltpu.VMEM((4, rows, cols), BF),
        pltpu.VMEM((4, rows, cols), BF),
        piece,
        piece,
        piece,
        dma((SUM_COPIES,)),
        dma((SUM_COPIES,)),
    ]


def split_terms(terms):
    return terms.astype(BF).reshape(4, 2, terms.shape[0] // 8, terms.shape[1])


def out_proj_kernel(
    own_ref, w_ref, x_ref, gain_ref, res_ref, xo_ref, sqo_ref, got, all_ref, block, terms, acc, mate, total, relay, direct, joined,
    sum_send, sum_recv, local_sem, wide_send, wide_recv, near_send, near_recv,
):
    rows = x_ref.shape[0]
    wide, sums, near = Copies(wide_send, wide_recv), Copies(sum_send, sum_recv), Copies(near_send, near_recv)
    interleave(gather_wide_steps(own_ref, all_ref, local_sem.at[0], wide))
    depth = w_ref.shape[1]
    tokens = x_ref.shape[1] // SIDE
    for group in range(SIDE):
        values = all_ref[group].reshape(tokens, depth)
        term = lax.dot_general(w_ref[...], values, (((1,), (1,)), ((), ())), preferred_element_type=F32)
        terms[:, :, :, pl.ds(group * tokens, tokens)] = split_terms(term)
    sum_narrow_body(terms, acc, mate, total, relay, direct, joined, sums)
    residual = (x_ref[...].astype(F32) + acc[...]).astype(BF)
    res_ref[...] = residual
    block[...] = to_send(residual, gain_ref[:, :1])
    interleave(gather_narrow_steps(block, got, local_sem.at[1], near))
    interleave(unpack_steps(got, xo_ref, sqo_ref))
    wide.sent()
    sums.sent()
    near.sent()


def matmul_sum_kernel(
    x_ref, w_ref, sq_ref, out_ref, sqo_ref, part, mid, got1, got2, sq1, sqm, sq2,
    send1, recv1, send2, recv2, sq_send, sq_recv,
):
    pieces, width = part.shape[0], part.shape[-1]
    rows = x_ref.shape[3]
    y, z = wide_place()
    names = (("y", "z"), ("z", "y"))
    spots = ((y, z), (z, y))
    squares = Copies(sq_send, sq_recv)
    for by in (1, 2, 3):
        squares.start(by - 1, sq_ref.at[turn(y, by)], sq1.at[by - 1], ring_devices("y", by))

    def product(half, chunk, piece):
        block = x_ref[chunk, :, 0] if half == 0 else x_ref[:, chunk, 1]
        block = block.reshape(SIDE * rows, block.shape[-1])
        columns = pl.ds(pl.multiple_of(piece * width, 128), width)
        got = jnp.dot(block, w_ref[:, columns], preferred_element_type=F32)
        return got.reshape(SIDE, rows, width)

    def copy1(piece, half, kind, way, src):
        return pltpu.make_async_remote_copy(
            src_ref=src,
            dst_ref=got1.at[piece, half, kind, way],
            send_sem=send1.at[piece, half, kind, way],
            recv_sem=recv1.at[piece, half, kind, way],
            device_id=ring_devices(names[half][0], 1 if way == 0 else 3),
            device_id_type=MESH,
        )

    def copy2(piece, half, kind, way, src):
        return pltpu.make_async_remote_copy(
            src_ref=src,
            dst_ref=got2.at[piece, half, kind, way],
            send_sem=send2.at[piece, half, kind, way],
            recv_sem=recv2.at[piece, half, kind, way],
            device_id=ring_devices(names[half][1], 1 if way == 0 else 3),
            device_id_type=MESH,
        )

    def await1(piece, half, kind, way):
        ref = got1.at[piece, half, kind, way]
        pltpu.make_async_copy(ref, ref, recv1.at[piece, half, kind, way]).wait()
        return got1[piece, half, kind, way].astype(F32)

    def await2(piece, half, kind, way):
        ref = got2.at[piece, half, kind, way]
        pltpu.make_async_copy(ref, ref, recv2.at[piece, half, kind, way]).wait()
        return got2[piece, half, kind, way].astype(F32)

    lower, upper = pl.ds(0, 2), pl.ds(2, 2)
    low, high = pl.ds(0, rows // 2), pl.ds(rows // 2, rows // 2)

    def first(piece):
        for half in range(2):
            far = turn(spots[half][0], 2)
            part[piece, half, far] = product(half, far, piece).astype(BF)
            copy1(piece, half, 0, 0, part.at[piece, half, far, lower]).start()
            copy1(piece, half, 0, 1, part.at[piece, half, far, upper]).start()
        for half in range(2):
            right, left = turn(spots[half][0], 1), turn(spots[half][0], 3)
            part[piece, half, right] = product(half, right, piece).astype(BF)
            copy1(piece, half, 1, 0, part.at[piece, half, right, upper]).start()
            part[piece, half, left] = product(half, left, piece).astype(BF)
            copy1(piece, half, 1, 1, part.at[piece, half, left, lower]).start()

    def second(piece):
        for half in range(2):
            right, left = turn(spots[half][0], 1), turn(spots[half][0], 3)
            got = await1(piece, half, 0, 0)
            part[piece, half, right, lower] = (part[piece, half, right, lower].astype(F32) + got).astype(BF)
            copy1(piece, half, 2, 0, part.at[piece, half, right, lower]).start()
            got = await1(piece, half, 0, 1)
            part[piece, half, left, upper] = (part[piece, half, left, upper].astype(F32) + got).astype(BF)
            copy1(piece, half, 2, 1, part.at[piece, half, left, upper]).start()

    def third(piece):
        for half in range(2):
            own = product(half, spots[half][0], piece)
            mid[piece, half, lower] = (
                own[:2] + await1(piece, half, 1, 1) + await1(piece, half, 2, 0)
            ).astype(BF)
            mid[piece, half, upper] = (
                own[2:] + await1(piece, half, 1, 0) + await1(piece, half, 2, 1)
            ).astype(BF)
            far, right, left = (turn(spots[half][1], by) for by in (2, 1, 3))
            copy2(piece, half, 0, 0, mid.at[piece, half, far, low]).start()
            copy2(piece, half, 0, 1, mid.at[piece, half, far, high]).start()
            copy2(piece, half, 1, 0, mid.at[piece, half, right, high]).start()
            copy2(piece, half, 1, 1, mid.at[piece, half, left, low]).start()

    def fourth(piece):
        for half in range(2):
            right, left = turn(spots[half][1], 1), turn(spots[half][1], 3)
            got = await2(piece, half, 0, 0)
            mid[piece, half, right, low] = (mid[piece, half, right, low].astype(F32) + got).astype(BF)
            copy2(piece, half, 2, 0, mid.at[piece, half, right, low]).start()
            got = await2(piece, half, 0, 1)
            mid[piece, half, left, high] = (mid[piece, half, left, high].astype(F32) + got).astype(BF)
            copy2(piece, half, 2, 1, mid.at[piece, half, left, high]).start()

    def fifth(piece):
        columns = pl.ds(pl.multiple_of(piece * width, 128), width)
        for half in range(2):
            own = spots[half][1]
            out_ref[half, low, columns] = (
                mid[piece, half, own, low].astype(F32) + await2(piece, half, 1, 1) + await2(piece, half, 2, 0)
            )
            out_ref[half, high, columns] = (
                mid[piece, half, own, high].astype(F32) + await2(piece, half, 1, 0) + await2(piece, half, 2, 1)
            )

    stages = (first, second, third, fourth, fifth)

    def step(t, carry):
        for lag, stage in enumerate(stages):
            piece = t - lag

            @pl.when((piece >= 0) & (piece < pieces))
            def _():
                stage(jnp.clip(piece, 0, pieces - 1))

        return carry

    lax.fori_loop(0, pieces + len(stages) - 1, step, 0)

    for by in (1, 2, 3):
        squares.arrived(by - 1, sq1.at[by - 1])
    sqm[...] = sq_ref[y] + sq1[0] + sq1[1] + sq1[2]
    for by in (1, 2, 3):
        squares.start(2 + by, sqm.at[turn(z, by)], sq2.at[by - 1], ring_devices("z", by))
    for by in (1, 2, 3):
        squares.arrived(2 + by, sq2.at[by - 1])
    sqo_ref[...] = sqm[z] + sq2[0] + sq2[1] + sq2[2]
    squares.sent()

    def drain(piece, carry):
        for half in range(2):
            for kind in range(3):
                for way in range(2):
                    copy1(piece, half, kind, way, part.at[piece, half, 0, lower]).wait_send()
                    copy2(piece, half, kind, way, mid.at[piece, half, 0, low]).wait_send()
        return carry

    lax.fori_loop(0, pieces, drain, 0)


def gate_up_kernel(
    x_ref, w_ref, sq_ref, down_ref, res_ref, final_ref, out_ref, part, mid, hid, got1, got2, sq1, sqm, sq2, inv,
    send1, recv1, send2, recv2, send3, recv3, send4, recv4, own_sem, sq_send, sq_recv,
    grown, terms, acc, mate, total, relay, direct, joined, sum_send, sum_recv,
):
    pieces, width = part.shape[0], part.shape[-1]
    wide = width // 2
    rows = x_ref.shape[3]
    y, z = wide_place()
    names = (("y", "z"), ("z", "y"))
    spots = ((y, z), (z, y))
    greet(wide_lines() + narrow_neighbours())
    squares = Copies(sq_send, sq_recv)
    for by in (1, 2, 3):
        squares.start(by - 1, sq_ref.at[turn(y, by)], sq1.at[by - 1], ring_devices("y", by))

    lower, upper = pl.ds(0, 2), pl.ds(2, 2)
    low, high = pl.ds(0, rows // 2), pl.ds(rows // 2, rows // 2)

    def product(half, chunk, piece):
        block = x_ref[chunk, :, 0] if half == 0 else x_ref[:, chunk, 1]
        block = block.reshape(SIDE * rows, block.shape[-1])
        at = pl.multiple_of(piece * wide, 128)
        gate = jnp.dot(block, w_ref[0, :, pl.ds(at, wide)], preferred_element_type=F32)
        up = jnp.dot(block, w_ref[1, :, pl.ds(at, wide)], preferred_element_type=F32)
        return jnp.concatenate([gate, up], axis=1).reshape(SIDE, rows, width)

    def remote(src, dst, send, recv, axis, way):
        return pltpu.make_async_remote_copy(
            src_ref=src,
            dst_ref=dst,
            send_sem=send,
            recv_sem=recv,
            device_id=ring_devices(axis, 1 if way == 0 else 3),
            device_id_type=MESH,
        )

    def copy1(piece, half, kind, way, src):
        spot = (piece, half, kind, way)
        return remote(src, got1.at[spot], send1.at[spot], recv1.at[spot], names[half][0], way)

    def copy2(piece, half, kind, way, src):
        spot = (piece, half, kind, way)
        return remote(src, got2.at[spot], send2.at[spot], recv2.at[spot], names[half][1], way)

    def landed(ref, sem):
        pltpu.make_async_copy(ref, ref, sem).wait()

    def await1(piece, half, kind, way):
        landed(got1.at[piece, half, kind, way], recv1.at[piece, half, kind, way])
        return got1[piece, half, kind, way].astype(F32)

    def await2(piece, half, kind, way):
        landed(got2.at[piece, half, kind, way], recv2.at[piece, half, kind, way])
        return got2[piece, half, kind, way].astype(F32)

    def place(piece, half, first, second, part_rows):
        columns = pl.ds(pl.multiple_of(piece * wide, 128), wide)
        if half == 0:
            return out_ref.at[first, second, 0, part_rows, columns]
        return out_ref.at[second, first, 1, part_rows, columns]

    whole = pl.ds(0, rows)

    def copy3(piece, half, kind, way, src, dst):
        return remote(src, dst, send3.at[piece, half, kind, way], recv3.at[piece, half, kind, way], names[half][0], way)

    def copy4(piece, half, block, kind, way, src, dst):
        spot = (piece, half, block, kind, way)
        return remote(src, dst, send4.at[spot], recv4.at[spot], names[half][1], way)

    def send4_whole(piece, half, block, src):
        dst = place(piece, half, turn(spots[half][0], block), spots[half][1], whole)
        for way in range(2):
            copy4(piece, half, block, 0, way, src, dst).start()

    def relay4(piece, half, block):
        first = turn(spots[half][0], block)
        for way, by, part_rows in ((0, 3, low), (1, 1, high)):
            second = turn(spots[half][1], by)
            landed(place(piece, half, first, second, whole), recv4.at[piece, half, block, 0, way])
            came = place(piece, half, first, second, part_rows)
            copy4(piece, half, block, 1, way, came, came).start()

    def stage1(piece):
        for half in range(2):
            far = turn(spots[half][0], 2)
            part[piece, half, far] = product(half, far, piece).astype(BF)
            copy1(piece, half, 0, 0, part.at[piece, half, far, lower]).start()
            copy1(piece, half, 0, 1, part.at[piece, half, far, upper]).start()
        for half in range(2):
            right, left = turn(spots[half][0], 1), turn(spots[half][0], 3)
            part[piece, half, right] = product(half, right, piece).astype(BF)
            copy1(piece, half, 1, 0, part.at[piece, half, right, upper]).start()
            part[piece, half, left] = product(half, left, piece).astype(BF)
            copy1(piece, half, 1, 1, part.at[piece, half, left, lower]).start()

    def stage2(piece):
        for half in range(2):
            right, left = turn(spots[half][0], 1), turn(spots[half][0], 3)
            got = await1(piece, half, 0, 0)
            part[piece, half, right, lower] = (part[piece, half, right, lower].astype(F32) + got).astype(BF)
            copy1(piece, half, 2, 0, part.at[piece, half, right, lower]).start()
            got = await1(piece, half, 0, 1)
            part[piece, half, left, upper] = (part[piece, half, left, upper].astype(F32) + got).astype(BF)
            copy1(piece, half, 2, 1, part.at[piece, half, left, upper]).start()

    def stage3(piece):
        for half in range(2):
            own = product(half, spots[half][0], piece)
            mid[piece, half, lower] = (
                own[:2] + await1(piece, half, 1, 1) + await1(piece, half, 2, 0)
            ).astype(BF)
            mid[piece, half, upper] = (
                own[2:] + await1(piece, half, 1, 0) + await1(piece, half, 2, 1)
            ).astype(BF)
            far, right, left = (turn(spots[half][1], by) for by in (2, 1, 3))
            copy2(piece, half, 0, 0, mid.at[piece, half, far, low]).start()
            copy2(piece, half, 0, 1, mid.at[piece, half, far, high]).start()
            copy2(piece, half, 1, 0, mid.at[piece, half, right, high]).start()
            copy2(piece, half, 1, 1, mid.at[piece, half, left, low]).start()

    def stage4(piece):
        for half in range(2):
            right, left = turn(spots[half][1], 1), turn(spots[half][1], 3)
            got = await2(piece, half, 0, 0)
            mid[piece, half, right, low] = (mid[piece, half, right, low].astype(F32) + got).astype(BF)
            copy2(piece, half, 2, 0, mid.at[piece, half, right, low]).start()
            got = await2(piece, half, 0, 1)
            mid[piece, half, left, high] = (mid[piece, half, left, high].astype(F32) + got).astype(BF)
            copy2(piece, half, 2, 1, mid.at[piece, half, left, high]).start()

    def activate(sums, factor):
        sums = jnp.where(factor > 0, sums * factor, 0.0)
        gate, up = sums[:, :wide], sums[:, wide:]
        return (gate / (1.0 + jnp.exp(-gate)) * up).astype(BF)

    def stage5(piece):
        for half in range(2):
            own = spots[half][1]
            hid[piece, half, low] = activate(
                mid[piece, half, own, low].astype(F32) + await2(piece, half, 1, 1) + await2(piece, half, 2, 0),
                inv[half, low][:, :1],
            )
            hid[piece, half, high] = activate(
                mid[piece, half, own, high].astype(F32) + await2(piece, half, 1, 0) + await2(piece, half, 2, 1),
                inv[half, high][:, :1],
            )
            mine = hid.at[piece, half]
            dst = place(piece, half, *spots[half], whole)
            pltpu.make_async_copy(mine, dst, own_sem.at[piece, half]).start()
            for way in range(2):
                copy3(piece, half, 0, way, mine, dst).start()
            send4_whole(piece, half, 0, mine)

    def stage6(piece):
        for half in range(2):
            for way, by, part_rows in ((0, 3, low), (1, 1, high)):
                first = turn(spots[half][0], by)
                landed(place(piece, half, first, spots[half][1], whole), recv3.at[piece, half, 0, way])
                came = place(piece, half, first, spots[half][1], part_rows)
                copy3(piece, half, 1, way, came, came).start()
                send4_whole(piece, half, by, place(piece, half, first, spots[half][1], whole))
        for half in range(2):
            relay4(piece, half, 0)

    def stage7(piece):
        for half in range(2):
            far = turn(spots[half][0], 2)
            landed(place(piece, half, far, spots[half][1], low), recv3.at[piece, half, 1, 0])
            landed(place(piece, half, far, spots[half][1], high), recv3.at[piece, half, 1, 1])
            send4_whole(piece, half, 2, place(piece, half, far, spots[half][1], whole))
        for half in range(2):
            relay4(piece, half, 3)
            relay4(piece, half, 1)

    def stage8(piece):
        for half in range(2):
            relay4(piece, half, 2)

    def stage9(piece):
        for half in range(2):
            for block in range(4):
                first, second = turn(spots[half][0], block), turn(spots[half][1], 2)
                landed(place(piece, half, first, second, low), recv4.at[piece, half, block, 1, 0])
                landed(place(piece, half, first, second, high), recv4.at[piece, half, block, 1, 1])
            mine = place(piece, half, *spots[half], whole)
            landed(mine, own_sem.at[piece, half])
            for way in range(2):
                for kind in range(3):
                    copy1(piece, half, kind, way, part.at[piece, half, 0, lower]).wait_send()
                    copy2(piece, half, kind, way, mid.at[piece, half, 0, low]).wait_send()
                for kind, part_rows in ((0, whole), (1, low)):
                    ref = place(piece, half, *spots[half], part_rows)
                    copy3(piece, half, kind, way, ref, ref).wait_send()
                    for block in range(4):
                        copy4(piece, half, block, kind, way, ref, ref).wait_send()
        columns = pl.ds(pl.multiple_of(piece * wide, 128), wide)
        tokens = 2 * SIDE * rows
        for group in range(SIDE):
            values = out_ref[group, :, :, :, columns].reshape(tokens, wide)
            got = lax.dot_general(
                down_ref[:, columns], values, (((1,), (1,)), ((), ())), preferred_element_type=F32
            )
            spot = pl.ds(group * tokens, tokens)
            grown[:, spot] += got

    stages = (stage1, stage2, stage3, stage4, stage5, stage6, stage7, stage8, stage9)

    def step(t, carry):
        for lag, stage in enumerate(stages):
            piece = t - lag

            @pl.when((piece >= 0) & (piece < pieces))
            def _():
                stage(jnp.clip(piece, 0, pieces - 1))

        return carry

    grown[...] = jnp.zeros_like(grown)
    lax.fori_loop(0, 3, step, 0)

    for by in (1, 2, 3):
        squares.arrived(by - 1, sq1.at[by - 1])
    sqm[...] = sq_ref[y] + sq1[0] + sq1[1] + sq1[2]
    for by in (1, 2, 3):
        squares.start(2 + by, sqm.at[turn(z, by)], sq2.at[by - 1], ring_devices("z", by))
    lax.fori_loop(3, 4, step, 0)
    for by in (1, 2, 3):
        squares.arrived(2 + by, sq2.at[by - 1])
    everything = (sqm[z] + sq2[0] + sq2[1] + sq2[2])[:1]
    factor = lax.rsqrt(everything / D + epsilon)
    token = lax.broadcasted_iota(jnp.int32, (2 * rows, 128), 0)
    lane = lax.broadcasted_iota(jnp.int32, (2 * rows, 128), 1)
    column = jnp.sum(jnp.where(token == lane, factor, 0.0), axis=1, keepdims=True)
    inv[...] = jnp.broadcast_to(column, (2 * rows, 128)).reshape(2, rows, 128)
    lax.fori_loop(4, pieces + len(stages) - 1, step, 0)
    squares.sent()
    sums = Copies(sum_send, sum_recv)
    terms[...] = split_terms(grown[...])
    sum_narrow_body(terms, acc, mate, total, relay, direct, joined, sums)
    final_ref[...] = (res_ref[...].astype(F32) + acc[...]).astype(BF)
    sums.sent()


def gate_up(x, w, sq, down, residual, pieces, collective_id):
    tokens, depth = x.shape
    units = w.shape[2]
    width = 2 * units // pieces
    rows = tokens // (2 * SIDE * SIDE)
    dma = pltpu.SemaphoreType.DMA
    return pl.pallas_call(
        gate_up_kernel,
        out_shape=jax.ShapeDtypeStruct(residual.shape, BF),
        in_specs=[VM] * 5,
        out_specs=VM,
        scratch_shapes=[
            pltpu.VMEM((SIDE, SIDE, 2, rows, units), BF),
            pltpu.VMEM((pieces, 2, SIDE, SIDE, rows, width), BF),
            pltpu.VMEM((pieces, 2, SIDE, rows, width), BF),
            pltpu.VMEM((pieces, 2, rows, width // 2), BF),
            pltpu.VMEM((pieces, 2, 3, 2, 2, rows, width), BF),
            pltpu.VMEM((pieces, 2, 3, 2, rows // 2, width), BF),
            pltpu.VMEM((3, SIDE, 8, 128), F32),
            pltpu.VMEM((SIDE, 8, 128), F32),
            pltpu.VMEM((3, 8, 128), F32),
            pltpu.VMEM((2, rows, 128), F32),
            dma((pieces, 2, 3, 2)),
            dma((pieces, 2, 3, 2)),
            dma((pieces, 2, 3, 2)),
            dma((pieces, 2, 3, 2)),
            dma((pieces, 2, 2, 2)),
            dma((pieces, 2, 2, 2)),
            dma((pieces, 2, 4, 2, 2)),
            dma((pieces, 2, 4, 2, 2)),
            dma((pieces, 2)),
            dma((6,)),
            dma((6,)),
            pltpu.VMEM((down.shape[0], tokens), F32),
        ]
        + sum_scratch(*residual.shape),
        compiler_params=pltpu.CompilerParams(
            collective_id=collective_id, has_side_effects=True, vmem_limit_bytes=VMEM_LIMIT
        ),
        name="gate_up",
    )(x.reshape(SIDE, SIDE, 2, rows, depth), w, sq, down, residual)


CHUNK = 8


def attend_kernel(
    lengths_ref, sums_in_ref, sq_ref, cos_ref, sin_ref, cache_ref, out_ref, sums_ref, fresh_ref,
    lines, q_ref, own_ref, rows_out, rows_sum, span_ref, local_sem, send_sem, recv_sem,
):
    scale = HDIM ** (-0.5)
    rows = q_ref.shape[1]
    per = own_ref.shape[1]
    tokens = R * per
    factor = lax.rsqrt(sq_ref[:1] / D + epsilon)
    token = lax.broadcasted_iota(jnp.int32, (tokens, 128), 0)
    lane = lax.broadcasted_iota(jnp.int32, (tokens, 128), 1)
    column = jnp.sum(jnp.where(token == lane, factor, 0.0), axis=1, keepdims=True)

    def slot_of(index, turned):
        got = sums_in_ref[:, :, index * HDIM : index * HDIM + HDIM].reshape(tokens, HDIM)
        got = jnp.where(column > 0, got * column, 0.0)
        if turned:
            got = got * cos_ref[...] + pltpu.roll(got, HDIM // 2, 1) * sin_ref[...]
        lines[index] = got
        return got.astype(BF)

    fresh_ref[:, :HDIM] = slot_of(GROUP, True)
    fresh_ref[:, HDIM:] = slot_of(GROUP + 1, False)
    for request in range(R):
        mine = pl.ds(request, per, stride=R)
        own_ref[request, :, :HDIM] = lines[GROUP, mine, :].astype(BF)
        own_ref[request, :, HDIM:] = lines[GROUP + 1, mine, :].astype(BF)
    block = cache_ref.shape[2] * CHUNK
    spot = lax.axis_index("wide")
    copies = Copies(send_sem, recv_sem)
    gather = gather_direct_steps(own_ref, span_ref, local_sem, copies)
    next(gather)
    for index in range(GROUP):
        slot_of(index, True)
        for request in range(R):
            q_ref[request, index * per : index * per + per] = lines[index, pl.ds(request, per, stride=R), :].astype(BF)
    queries = [q_ref[request] for request in range(R)]

    def absorb(running, q, keys, values, allowed):
        peak, weight_sum, gathered = running
        scores = lax.dot_general(q, keys, (((1,), (1,)), ((), ())), preferred_element_type=F32) * scale
        scores = jnp.where(allowed(scores.shape), scores, floor_score)
        new_peak = jnp.maximum(peak, jnp.max(scores, axis=1, keepdims=True))
        weights = jnp.exp(scores - new_peak)
        factor = jnp.exp(peak - new_peak)
        weight_sum = weight_sum * factor + jnp.sum(weights, axis=1, keepdims=True)
        gathered = gathered * factor + jnp.dot(weights.astype(BF), values, preferred_element_type=F32)
        return new_peak, weight_sum, gathered

    def own_keys(shape):
        key = lax.broadcasted_iota(jnp.int32, shape, 1)
        row = lax.broadcasted_iota(jnp.int32, shape, 0)
        return key <= spot * per + lax.rem(row, per)

    running = [
        (
            jnp.full((rows, 1), floor_score, F32),
            jnp.zeros((rows, 1), F32),
            jnp.zeros((rows, HDIM), F32),
        )
        for _ in range(R)
    ]
    for index in range(cache_ref.shape[0] // CHUNK):
        for request in range(R):
            pair = cache_ref[pl.ds(index * CHUNK, CHUNK), request].reshape(block, 2 * HDIM)
            running[request] = absorb(
                running[request],
                queries[request],
                pair[:, :HDIM],
                pair[:, HDIM:],
                lambda shape: index * block + lax.broadcasted_iota(jnp.int32, shape, 1) < lengths_ref[request],
            )
        if index >= 2:
            next(gather, None)
    interleave(gather)
    for request in range(R):
        span = span_ref[:, :, request].reshape(SIDE * SIDE * per, 2 * HDIM)
        peak, weight_sum, gathered = absorb(
            running[request], queries[request], span[:, :HDIM], span[:, HDIM:], own_keys
        )
        gathered = gathered / weight_sum
        logs = peak + jnp.log(weight_sum)
        mine = pl.ds(request, per, stride=R)
        line = jnp.zeros((per, 128), F32)
        spot_of = lax.broadcasted_iota(jnp.int32, (per, 128), 1)
        for index in range(GROUP):
            rows_out[index, mine, :] = gathered[index * per : index * per + per]
            line = line + jnp.where(spot_of == index, logs[index * per : index * per + per], 0.0)
        rows_sum[mine, :] = line
    for index in range(GROUP):
        out_ref[:, :, index * HDIM : index * HDIM + HDIM] = rows_out[index].astype(BF).reshape(2, per, HDIM)
    sums_ref[...] = rows_sum[...]
    copies.sent()


def matmul_scratch(pieces, rows, width):
    dma = pltpu.SemaphoreType.DMA
    return [
        pltpu.VMEM((pieces, 2, SIDE, SIDE, rows, width), BF),
        pltpu.VMEM((pieces, 2, SIDE, rows, width), BF),
        pltpu.VMEM((pieces, 2, 3, 2, 2, rows, width), BF),
        pltpu.VMEM((pieces, 2, 3, 2, rows // 2, width), BF),
        pltpu.VMEM((3, SIDE, 8, 128), F32),
        pltpu.VMEM((SIDE, 8, 128), F32),
        pltpu.VMEM((3, 8, 128), F32),
        dma((pieces, 2, 3, 2)),
        dma((pieces, 2, 3, 2)),
        dma((pieces, 2, 3, 2)),
        dma((pieces, 2, 3, 2)),
        dma((6,)),
        dma((6,)),
    ]


def attend_scratch(per):
    tokens = R * per
    dma = pltpu.SemaphoreType.DMA
    return [
        pltpu.VMEM((GROUP + 2, tokens, HDIM), F32),
        pltpu.VMEM((R, GROUP * per, HDIM), BF),
        pltpu.VMEM((R, per, 2 * HDIM), BF),
        pltpu.VMEM((GROUP, tokens, HDIM), F32),
        pltpu.VMEM((tokens, 128), F32),
        pltpu.VMEM((SIDE, SIDE, R, per, 2 * HDIM), BF),
        dma,
        dma((DIRECT_COPIES,)),
        dma((DIRECT_COPIES,)),
    ]


def proj_scratch(per, rows, tokens):
    dma = pltpu.SemaphoreType.DMA
    return [
        pltpu.VMEM((8, rows + 8, tokens), BF),
        pltpu.VMEM((SIDE, SIDE, 2, per, GROUP * HDIM), BF),
        pltpu.VMEM((rows + 8, tokens), BF),
        *sum_scratch(rows, tokens),
        dma((2,)),
        dma((WIDE_COPIES,)),
        dma((WIDE_COPIES,)),
        dma((NARROW_COPIES,)),
        dma((NARROW_COPIES,)),
    ]


def attention_kernel(
    count_matmul, count_attend, lengths_ref, x_ref, wq_ref, sq_ref, cos_ref, sin_ref, cache_ref, wo_ref, flip_ref, gain_ref,
    sums_ref, fresh_ref, res_ref, xo_ref, sqo_ref, proj, total_sq, attended, *scratch,
):
    greet(wide_lines() + narrow_neighbours())
    for_attend = count_matmul + count_attend
    matmul_sum_kernel(x_ref, wq_ref, sq_ref, proj, total_sq, *scratch[:count_matmul])
    attend_kernel(
        lengths_ref, proj, total_sq, cos_ref, sin_ref, cache_ref, attended, sums_ref, fresh_ref,
        *scratch[count_matmul:for_attend],
    )
    out_proj_kernel(attended, wo_ref, flip_ref, gain_ref, res_ref, xo_ref, sqo_ref, *scratch[for_attend:])


def attention(lengths, x, wq, sq, cosine, sine, cache, wo, flipped, gain, collective_id):
    rows, tokens = flipped.shape
    cols = wq.shape[1]
    per = tokens // (2 * SIDE * SIDE)
    for_matmul, for_attend = matmul_scratch(1, per, cols), attend_scratch(per)
    return pl.pallas_call(
        functools.partial(attention_kernel, len(for_matmul), len(for_attend)),
        out_shape=(
            jax.ShapeDtypeStruct((2 * per, 128), F32),
            jax.ShapeDtypeStruct((2 * per, 2 * HDIM), BF),
            jax.ShapeDtypeStruct((rows, tokens), BF),
            jax.ShapeDtypeStruct((tokens, 8 * rows), BF),
            jax.ShapeDtypeStruct((SIDE, SIDE, 8, 128), F32),
        ),
        in_specs=[SM] + [VM] * 9,
        out_specs=(VM,) * 5,
        scratch_shapes=[
            pltpu.VMEM((2, per, cols), F32),
            pltpu.VMEM((8, 128), F32),
            pltpu.VMEM((2, per, GROUP * HDIM), BF),
            *for_matmul,
            *for_attend,
            *proj_scratch(per, rows, tokens),
        ],
        compiler_params=pltpu.CompilerParams(
            collective_id=collective_id, has_side_effects=True, vmem_limit_bytes=VMEM_LIMIT
        ),
        name="attention",
    )(lengths, x.reshape(SIDE, SIDE, 2, per, x.shape[1]), wq, sq, cosine, sine, cache, wo, flipped, spread(gain))


def token_angles(lengths, offsets, first_token, row_count, dim_size):
    token_ids = first_token + jnp.arange(row_count, dtype=jnp.int32)
    request_ids = token_ids % R
    start_pos = offsets + lengths
    matches = request_ids[:, None] == jnp.arange(start_pos.shape[0], dtype=jnp.int32)[None, :]
    chosen = jnp.sum(jnp.where(matches, start_pos[None, :], 0), axis=1)
    position = (chosen + token_ids // R).astype(jnp.float32)
    inverse = rope_base ** (-(jnp.arange(dim_size // 2, dtype=jnp.float32) * 2.0) / dim_size)
    return position[:, None] * inverse[None, :]


def local(
    hidden_in, attn_gain, w_qkv, cache_kv, lengths, offsets, w_out, mlp_gain, w_gate_up, w_down
):
    all_tokens, features = hidden_in.shape
    per_device = all_tokens // lax.axis_size("wide")
    first_token = lax.axis_index("wide") * per_device
    flipped = hidden_in.T
    positions = cache_kv.shape[1]
    cache = cache_kv.reshape(R, positions, 2, HDIM)
    scaled, squares, cache_all, flat_gate_up = gather_both(flipped, attn_gain, cache, w_gate_up, 1)
    angles = token_angles(lengths, offsets, first_token, per_device, HDIM)
    cosine, sine = jnp.cos(angles), jnp.sin(angles)
    sums, fresh, residual, scaled, squares = attention(
        lengths,
        scaled,
        w_qkv.reshape(w_qkv.shape[0], -1),
        squares,
        jnp.concatenate([cosine, cosine], axis=1),
        jnp.concatenate([-sine, sine], axis=1),
        cache_all.reshape(SIDE * SIDE, R, positions, 2 * HDIM),
        w_out.T,
        flipped,
        mlp_gain,
        2,
    )
    softmax_sums = sums[:, :GROUP]
    new_cache = fresh.reshape(per_device, 1, 2, HDIM)
    hidden_out = gate_up(scaled, flat_gate_up, squares, w_down.T, residual, 2, 7).T
    return (hidden_out, softmax_sums, new_cache)


def solution(mesh):
    return jax.shard_map(
        local,
        mesh=mesh,
        in_specs=(
            P(None, ("wide", "narrow")),
            P(("wide", "narrow")),
            P("wide", "narrow", None),
            P(None, "wide", "narrow", None, None),
            P(),
            P(),
            P("narrow", "wide"),
            P(("wide", "narrow")),
            P("wide", None, "narrow"),
            P("narrow", "wide"),
        ),
        out_specs=(
            P(None, ("wide", "narrow")),
            P("wide", "narrow"),
            P("wide", "narrow", None, None),
        ),
        check_vma=False,
    )
```
